32 devices in a mesh: groups: 2 (over y), chan: 4 (over z), blk: 2 (over x), dir: 2 (over core).
Axes of the slice: x: 2, y: 2, z: 4, core: 2. Of those that a mesh axis runs over, the one named last changes fastest.
Arguments:
- visibilities: float32 [16, 8, 2, 512], P('groups', 'chan', 'blk'), parts along dimension 0, may hold values from -6 to 6
- antenna_pairs: int32 [2, 2, 512], P(None, 'blk'), may hold values from 0 to 511, as said below
- valid_mask: int32 [2, 1024], P('blk', 'groups'), parts along dimension 1, may hold values 0 or 1
- station_positions: float32 [2, 512], replicated, may hold values from -20 to 20
- source_offsets: float32 [2, 256], replicated, may hold values from -0.3 to 0.3
- brightness: float32 [4, 256], replicated, may hold values from -0.375 to 0.375
- source_cluster: int32 [256], replicated, may hold values from 0 to 15
- jones_gains: float32 [16, 16, 512], P('dir', 'groups'), parts along dimension 1, may hold values from -3 to 3
Outputs:
- residuals: float32 [16, 8, 2, 512], P('groups', None, 'blk', 'chan'), parts along dimension 0
- solved_gains: float32 [16, 16, 512], P('dir', 'groups'), parts along dimension 1
The draws below stay inside these ranges and needn't reach their ends.
There are 2 independent parts, one for each index of `groups`. The reference program is written for one: setup_inputs(seed, part) draws one part's arguments, and reference() takes and returns one part's arrays. A program takes and returns all parts, laid end to end along the dimension named above; an argument that names none is the same for every part. Nothing has to cross between parts.
Inputs may be any that keep to these rules, and one draw needn't show every extreme that they name: `antenna_pairs`: the two stations of a baseline differ. The t-th aligned run of 128 baselines (numbered as in the reference program) joins a station of block i with one of block j, where (i, j) is pair number t mod 36 in the row-order list of pairs i <= j of the 8 blocks of 64 consecutive stations.
All inputs are finite; a program needn't handle non-finite values. No bound on the sum of `valid_mask` on one device may be relied on, other than what follows from the above.
Results may differ from the reference program's by a relative error of at most 0.0003.
Values sent between devices are 32-bit elements; how exact they have to be, the bound alone decides.
No kernel may reach another device: no remote copies, remote signals or barrier semaphores. Data moves between devices by JAX's collectives and lax.ppermute only.
A program may use at most 64 MiB of HBM per device.

```python
import math
import jax
import jax.numpy as jnp
import numpy as np
from jax import lax

S = 512
DIRS = 16
K = 256
ITERS = 2
BASE_DEV = 128
CH = 8
NBLK = 2
SLICE = 512


UPPER_FIRST = np.triu_indices(8)[0].astype(np.int32)


UPPER_SECOND = np.triu_indices(8)[1].astype(np.int32)


def draw_antenna_pairs(key, part):
    baseline_total = NBLK * SLICE
    owners = jnp.arange(baseline_total) // BASE_DEV
    pair_slot = owners % 36
    block_first = jnp.asarray(UPPER_FIRST)[pair_slot]
    block_second = jnp.asarray(UPPER_SECOND)[pair_slot]
    block_size = S // 8
    key_first, key_second, key_bump = jax.random.split(key, 3)
    offset_first = jax.random.randint(key_first, (baseline_total,), 0, block_size)
    offset_second = jax.random.randint(key_second, (baseline_total,), 0, block_size)
    bump_value = jax.random.randint(key_bump, (baseline_total,), 1, block_size)
    offset_second = jnp.where(block_first == block_second, (offset_first + bump_value) % block_size, offset_second)
    stations = jnp.stack([block_first * block_size + offset_first, block_second * block_size + offset_second])
    return stations.reshape(2, NBLK, SLICE).astype(jnp.int32)


def set_ends(drawn, key, low, top_value):
    longest = drawn.shape.index(max(drawn.shape))
    spots = []
    for shift in (0, 1):
        where = [jax.random.randint(jax.random.fold_in(key, axis), (), 0, length) for axis, length in enumerate(drawn.shape)]
        where[longest] = (where[longest] + shift) % drawn.shape[longest]
        spots.append(tuple(where))
    return drawn.at[spots[0]].set(low).at[spots[1]].set(top_value)


def steps_of(rng, extent, cuts, low, high):
    level, own = 1.0, jax.random.fold_in(rng, 6)
    for position, parts in cuts:
        heights = jnp.exp(jax.random.uniform(jax.random.fold_in(own, position), (parts,), jnp.float32, low / len(cuts), high / len(cuts)))
        level = level * jnp.repeat(heights, extent[position] // parts).reshape([-1 if axis == position else 1 for axis in range(len(extent))])
    return level


def centred(own_key, dims, width, bound, shards=(), held_as=jnp.bfloat16):
    result = jax.random.normal(own_key, dims, jnp.float32) * width
    if len(shards) > 0:
        result = steps_of(own_key, dims, shards, -0.22, 0.18) * result
    return jnp.clip(result, min=-bound, max=bound).astype(held_as)


def setup_inputs(seed: int = 0, part: int = 0) -> dict:
    seeds = jax.random.split(jax.random.key(seed), 9)
    part_keys = jax.random.split(jax.random.fold_in(seeds[8], part), 9)
    return {
        "visibilities": centred(part_keys[0], (8, CH, NBLK, SLICE), 1.0, 6.0, ((1, 4), (2, 2)), jnp.float32),
        "antenna_pairs": draw_antenna_pairs(jax.random.fold_in(seeds[8], 71), part),
        "valid_mask": set_ends((jax.random.randint(part_keys[2], (NBLK, SLICE), 0, 8) < 7).astype(jnp.int32), jax.random.fold_in(part_keys[2], 1), 0, 1),
        "station_positions": jnp.clip(jax.random.uniform(seeds[3], (2, S), jnp.float32, -20.0, 20.0), -20.0, 20.0),
        "source_offsets": jnp.clip(jax.random.uniform(seeds[4], (2, K), jnp.float32, -0.3, 0.3), -0.3, 0.3),
        "brightness": centred(seeds[5], (4, K), K ** -0.5, 0.375, (), jnp.float32),
        "source_cluster": set_ends(jax.random.randint(seeds[6], (K,), 0, DIRS), jax.random.fold_in(seeds[6], 1), 0, DIRS - 1).astype(jnp.int32),
        "jones_gains": centred(part_keys[7], (DIRS, 8, S), 0.5, 3.0, ((0, 2),), jnp.float32),
    }


TWO_PI = 2.0 * math.pi
STEP_SIZE = 0.3
EPSILON = 1e-6
HIGHEST = lax.Precision.HIGHEST


def jones_product(former, latter):
    real_list = []
    imag_list = []
    for row_number in (0, 1):
        for column in (0, 1):
            real_list.append(former[2 * row_number] * latter[column] - former[4 + 2 * row_number] * latter[4 + column] + former[2 * row_number + 1] * latter[2 + column] - former[5 + 2 * row_number] * latter[6 + column])
            imag_list.append(former[2 * row_number] * latter[4 + column] + former[4 + 2 * row_number] * latter[column] + former[2 * row_number + 1] * latter[6 + column] + former[5 + 2 * row_number] * latter[2 + column])
    return jnp.stack(real_list + imag_list)


def adjoint(matrix):
    return jnp.stack([matrix[0], matrix[2], matrix[1], matrix[3], -matrix[4], -matrix[6], -matrix[5], -matrix[7]])


def source_table(brightness, source_cluster, direction_ids):
    member = (source_cluster[None, :] == direction_ids[:, None]).astype(jnp.float32)
    return (brightness[:, None, :] * member[None, :, :]).reshape(4 * direction_ids.shape[0], brightness.shape[1])


def coherency(bright_table, geometry, scales):
    phase_grid = (TWO_PI * scales)[None, :, None] * geometry[:, None, :]
    phases_flat = phase_grid.reshape(geometry.shape[0], -1)
    real_block = jnp.dot(bright_table, jnp.cos(phases_flat), precision=HIGHEST)
    imag_block = -jnp.dot(bright_table, jnp.sin(phases_flat), precision=HIGHEST)
    dir_count = bright_table.shape[0] // 4
    return jnp.concatenate([real_block, imag_block], axis=0).reshape(8, dir_count, scales.shape[0], geometry.shape[1])


def reference(visibilities, antenna_pairs, valid_mask, station_positions, source_offsets, brightness, source_cluster, jones_gains):
    first_station = antenna_pairs[0].reshape(-1).astype(jnp.int32)
    second_station = antenna_pairs[1].reshape(-1).astype(jnp.int32)
    vis_flat = visibilities.reshape(8, CH, NBLK * SLICE)
    weight_row = valid_mask.reshape(-1).astype(jnp.float32)
    u_coord = station_positions[0][first_station] - station_positions[0][second_station]
    v_coord = station_positions[1][first_station] - station_positions[1][second_station]
    geometry = source_offsets[0][:, None] * u_coord[None, :] + source_offsets[1][:, None] * v_coord[None, :]
    scales = 1.0 + 0.5 * jnp.arange(CH).astype(jnp.float32) / CH
    bright_table = source_table(brightness, source_cluster, jnp.arange(DIRS).astype(jnp.int32))
    by_channel = jnp.moveaxis(vis_flat, 1, 0)

    def channel_state(gains_now, channel_vis, scale_one):
        coherent = coherency(bright_table, geometry, scale_one[None])[:, :, 0, :]
        gain_first = jnp.take(gains_now, first_station, axis=2).transpose(1, 0, 2)
        gain_second = jnp.take(gains_now, second_station, axis=2).transpose(1, 0, 2)
        model_vis = jnp.sum(jones_product(jones_product(gain_first, coherent), adjoint(gain_second)), axis=1)
        residual_now = weight_row * (channel_vis - model_vis)
        return coherent, gain_first, gain_second, residual_now

    def gradient(gains_now):
        def channel_step(running, inputs):
            channel_vis, scale_one = inputs
            coherent, gain_first, gain_second, residual_now = channel_state(gains_now, channel_vis, scale_one)
            toward_second = jones_product(gain_second, adjoint(coherent))
            toward_first = jones_product(gain_first, coherent)
            grad_first = jones_product(residual_now[:, None], toward_second)
            grad_second = jones_product(adjoint(residual_now)[:, None], toward_first)
            curv_first = weight_row * jnp.sum(toward_second * toward_second, axis=0)
            curv_second = weight_row * jnp.sum(toward_first * toward_first, axis=0)
            return (running[0] + grad_first, running[1] + grad_second, running[2] + curv_first, running[3] + curv_second), None

        base_total = NBLK * SLICE
        zero_sums = (jnp.zeros((8, DIRS, base_total), jnp.float32), jnp.zeros((8, DIRS, base_total), jnp.float32), jnp.zeros((DIRS, base_total), jnp.float32), jnp.zeros((DIRS, base_total), jnp.float32))
        totals, ignored = lax.scan(channel_step, zero_sums, (by_channel, scales))
        grad_station = jax.ops.segment_sum(jnp.moveaxis(totals[0], 2, 0), first_station, num_segments=S) + jax.ops.segment_sum(jnp.moveaxis(totals[1], 2, 0), second_station, num_segments=S)
        curv_station = jax.ops.segment_sum(totals[2].T, first_station, num_segments=S) + jax.ops.segment_sum(totals[3].T, second_station, num_segments=S)
        return grad_station.transpose(2, 1, 0), curv_station.T

    gains_now = jones_gains
    for iteration in range(ITERS):
        grad_station, curv_station = gradient(gains_now)
        gains_now = gains_now + STEP_SIZE * grad_station / (curv_station[:, None, :] + EPSILON)

    def final_channel(inputs):
        return channel_state(gains_now, inputs[0], inputs[1])[3]

    resid_all = lax.map(final_channel, (by_channel, scales))
    residuals = jnp.moveaxis(resid_all, 0, 1).reshape(8, CH, NBLK, SLICE)
    return residuals, gains_now
```

```python
import functools
import math

import jax
import jax.numpy as jnp
from jax import lax
from jax.experimental import pallas as pl
from jax.experimental.pallas import tpu as pltpu
from jax.sharding import PartitionSpec as P

ITERS = 2


TWO_PI = 2.0 * math.pi
STEP_SIZE = 0.3
EPSILON = 1e-06
HIGHEST = lax.Precision.HIGHEST


def jones_product(former, latter):
    real_list = []
    imag_list = []
    for row_number in (0, 1):
        for column in (0, 1):
            real_list.append(
                former[2 * row_number] * latter[column]
                - former[4 + 2 * row_number] * latter[4 + column]
                + former[2 * row_number + 1] * latter[2 + column]
                - former[5 + 2 * row_number] * latter[6 + column]
            )
            imag_list.append(
                former[2 * row_number] * latter[4 + column]
                + former[4 + 2 * row_number] * latter[column]
                + former[2 * row_number + 1] * latter[6 + column]
                + former[5 + 2 * row_number] * latter[2 + column]
            )
    return jnp.stack(real_list + imag_list)


def adjoint(matrix):
    return jnp.stack(
        [matrix[0], matrix[2], matrix[1], matrix[3], -matrix[4], -matrix[6], -matrix[5], -matrix[7]]
    )


def source_table(brightness, source_cluster, direction_ids):
    member = (source_cluster[None, :] == direction_ids[:, None]).astype(jnp.float32)
    return (brightness[:, None, :] * member[None, :, :]).reshape(
        4 * direction_ids.shape[0], brightness.shape[1]
    )


def coherency(bright_table, geometry, scales):
    phase_grid = (TWO_PI * scales)[None, :, None] * geometry[:, None, :]
    phases_flat = phase_grid.reshape(geometry.shape[0], -1)
    real_block = jnp.dot(bright_table, jnp.cos(phases_flat), precision=HIGHEST)
    imag_block = -jnp.dot(bright_table, jnp.sin(phases_flat), precision=HIGHEST)
    dir_count = bright_table.shape[0] // 4
    return jnp.concatenate([real_block, imag_block], axis=0).reshape(
        8, dir_count, scales.shape[0], geometry.shape[1]
    )


def per_device(
    visibilities,
    antenna_pairs,
    valid_mask,
    station_positions,
    source_offsets,
    brightness,
    source_cluster,
    jones_gains,
):
    relay_count = lax.axis_size("chan")
    base_count = antenna_pairs.shape[2] // relay_count
    station_count = station_positions.shape[1]
    offset = lax.axis_index("chan") * base_count
    own_pairs = lax.dynamic_slice_in_dim(antenna_pairs[:, 0], offset, base_count, 1)
    first_station = own_pairs[0]
    second_station = own_pairs[1]
    weight_row = lax.dynamic_slice_in_dim(valid_mask[0], offset, base_count, 0).astype(jnp.float32)
    regrouped = lax.all_to_all(visibilities, "chan", split_axis=3, concat_axis=1, tiled=True)[
        :, :, 0, :
    ]
    total_channels = regrouped.shape[1]
    own_directions = jones_gains.shape[0]
    channel_ids = jnp.arange(total_channels)
    gains_now = jones_gains
    direction_ids = lax.axis_index("dir") * own_directions + jnp.arange(own_directions)
    local_channels = regrouped.shape[1]
    scales = 1.0 + 0.5 * channel_ids.astype(jnp.float32) / total_channels
    u_coord = station_positions[0][first_station] - station_positions[0][second_station]
    v_coord = station_positions[1][first_station] - station_positions[1][second_station]
    geometry = (
        source_offsets[0][:, None] * u_coord[None, :]
        + source_offsets[1][:, None] * v_coord[None, :]
    )
    bright_table = source_table(brightness, source_cluster, direction_ids)
    group_size = math.gcd(local_channels, max(1, 2048 // base_count))
    group_count = local_channels // group_size
    scale_groups = scales.reshape(group_count, group_size)
    onehot_first = (first_station[:, None] == jnp.arange(station_count)[None, :]).astype(
        jnp.float32
    )
    onehot_second = (second_station[:, None] == jnp.arange(station_count)[None, :]).astype(
        jnp.float32
    )

    def station_gains(gains_current):
        gain_first = jnp.take(gains_current, first_station, axis=2).transpose(1, 0, 2)[
            :, :, None, :
        ]
        gain_second = jnp.take(gains_current, second_station, axis=2).transpose(1, 0, 2)[
            :, :, None, :
        ]
        return (gain_first, gain_second)

    def residual_of(gains_current):
        gain_first, gain_second = station_gains(gains_current)

        def residual_one_group(scale_group):
            coherent = coherency(bright_table, geometry, scale_group)
            return jnp.sum(
                jones_product(jones_product(gain_first, coherent), adjoint(gain_second)), axis=1
            )

        partial_model = jnp.moveaxis(lax.map(residual_one_group, scale_groups), 0, 1).reshape(
            8, local_channels, base_count
        )
        model_vis = lax.psum(partial_model, "dir")
        return weight_row * (regrouped - model_vis)

    for iteration in range(ITERS):
        residual_now = residual_of(gains_now)
        updated_gain_first, updated_gain_second = station_gains(gains_now)
        resid_groups = jnp.moveaxis(
            residual_now.reshape(8, group_count, group_size, base_count), 1, 0
        )
        dir_count = gains_now.shape[0]

        def updated_one_group(running, inputs):
            scale_group, resid_group = inputs
            coherent = coherency(bright_table, geometry, scale_group)
            toward_second = jones_product(updated_gain_second, adjoint(coherent))
            toward_first = jones_product(updated_gain_first, coherent)
            grad_first = jnp.sum(jones_product(resid_group[:, None], toward_second), axis=2)
            grad_second = jnp.sum(
                jones_product(adjoint(resid_group)[:, None], toward_first), axis=2
            )
            curv_first = jnp.sum(toward_second * toward_second, axis=(0, 2))
            curv_second = jnp.sum(toward_first * toward_first, axis=(0, 2))
            return (
                (
                    running[0] + grad_first,
                    running[1] + grad_second,
                    running[2] + curv_first,
                    running[3] + curv_second,
                ),
                None,
            )

        zero_sums = (
            jnp.zeros((8, dir_count, base_count), jnp.float32),
            jnp.zeros((8, dir_count, base_count), jnp.float32),
            jnp.zeros((dir_count, base_count), jnp.float32),
            jnp.zeros((dir_count, base_count), jnp.float32),
        )
        totals, ignored = lax.scan(updated_one_group, zero_sums, (scale_groups, resid_groups))
        grad_station = jnp.einsum(
            "cdb,bs->dcs", totals[0], onehot_first, precision=HIGHEST
        ) + jnp.einsum("cdb,bs->dcs", totals[1], onehot_second, precision=HIGHEST)
        curv_station = jnp.dot(weight_row * totals[2], onehot_first, precision=HIGHEST) + jnp.dot(
            weight_row * totals[3], onehot_second, precision=HIGHEST
        )
        grad_station, curv_station = lax.psum((grad_station, curv_station), ("chan", "blk"))
        gains_now = gains_now + STEP_SIZE * grad_station / (curv_station[:, None, :] + EPSILON)
    residual_now = residual_of(gains_now)
    return (residual_now[:, :, None, :], gains_now)


COS_TERMS = (
    0.9999999890590228,
    -19.739204499454,
    64.93911745989914,
    -85.45013953093448,
    60.16763095128989,
    -25.96759924954187,
    6.528658162606979,
)
SIN_TERMS = (
    6.283185302511502,
    -41.34170040531754,
    81.6051313857969,
    -76.70301535383193,
    42.02592698564183,
    -14.899846667160109,
    3.2381375090822355,
)
RUN = 128
BLOCK = 64
BLOCKS = 8


def pieces(value, count):
    result = []
    for index in range(count):
        piece = value.astype(jnp.bfloat16)
        result.append(piece)
        if index < count - 1:
            value = value - piece.astype(jnp.float32)
    return result


def dot_f32(left, right, contract_right=0):
    return lax.dot_general(
        left,
        right,
        (((1,), (contract_right,)), ((), ())),
        preferred_element_type=jnp.float32,
    )


def horner(terms, x):
    total = jnp.full_like(x, terms[-1])
    for term in terms[-2::-1]:
        total = total * x + term
    return total


def turn_pair(turns):
    rest = turns - jnp.round(turns)
    square = rest * rest
    return horner(COS_TERMS, square), horner([-term for term in SIN_TERMS], square) * rest


def product(a, b):
    real = []
    imag = []
    for row in (0, 1):
        for col in (0, 1):
            ar, br, cr, dr = a[2 * row], b[col], a[2 * row + 1], b[2 + col]
            ai, bi, ci, di = a[4 + 2 * row], b[4 + col], a[5 + 2 * row], b[6 + col]
            real.append(ar * br - ai * bi + cr * dr - ci * di)
            imag.append(ar * bi + ai * br + cr * di + ci * dr)
    return real + imag


def dagger(a):
    return [a[0], a[2], a[1], a[3], -a[4], -a[6], -a[5], -a[7]]


class Place:
    def __init__(self, runs):
        self.chan = lax.axis_index("chan")
        self.core = lax.axis_index("dir")
        self.window = lax.axis_index("blk") * lax.axis_size("dir") + self.core
        self.runs = runs
        self.lanes = runs * RUN
        self.first_lane = pl.multiple_of(self.core * self.lanes, self.lanes)
        self.width = runs * BLOCK
        self.first_station = pl.multiple_of(self.window * self.width, self.width)

    def onehot(self, pairs_ref, side):
        station = pairs_ref[side, :, pl.ds(self.first_lane, self.lanes)]
        local = jnp.where(station < BLOCK, station, station - self.first_station + RUN)
        rows = lax.broadcasted_iota(jnp.int32, (RUN + self.width, self.lanes), 0)
        return jnp.where(rows == local, 1.0, 0.0).astype(jnp.bfloat16)

    def slot(self, channel, per_shard):
        return jnp.bitwise_xor(channel // per_shard, self.chan) * per_shard + channel % per_shard


def coherency_kernel(
    runs, channels, per_shard, pairs, positions, offsets, brightness, cluster, out, base, spin, parts
):
    place = Place(runs)
    table = jnp.concatenate(
        [positions[:, 0:RUN], positions[:, pl.ds(place.first_station, place.width)]], axis=1
    )
    table = jnp.concatenate([p.astype(jnp.float32) for p in pieces(table, 3)] + [jnp.zeros((2, table.shape[1]))])
    table = table.astype(jnp.bfloat16)
    there = []
    for side in (0, 1):
        found = dot_f32(table, place.onehot(pairs, side))
        there.append(found[0:2] + found[2:4] + found[4:6])
    span = there[0] - there[1]
    sources = offsets.shape[1]
    columns = jnp.transpose(jnp.concatenate([offsets[...], jnp.zeros((6, sources))]))
    step = 16
    for start in range(0, sources, step):
        rows = slice(start, start + step)
        geometry = columns[rows, 0:1] * span[0:1] + columns[rows, 1:2] * span[1:2]
        base[0, rows], base[1, rows] = turn_pair(geometry)
        spin[0, rows], spin[1, rows] = turn_pair(geometry * (0.5 / channels))

    directions = out.shape[1] // 8
    member = lax.broadcasted_iota(jnp.int32, (directions, sources), 0) == cluster[...]
    bright = jnp.concatenate([jnp.where(member, brightness[n : n + 1], 0.0) for n in range(4)])
    high, low = pieces(bright, 2)
    both = jnp.concatenate([high, low])
    half = 4 * directions
    for channel in range(channels):
        for start in range(0, sources, step):
            rows = slice(start, start + step)
            c, s = base[0, rows], base[1, rows]
            for index, value in enumerate((c, s)):
                first, second = pieces(value, 2)
                parts[channel % 2, index, 0, rows] = first
                parts[channel % 2, index, 1, rows] = second
            if channel < channels - 1:
                dc, ds = spin[0, rows], spin[1, rows]
                base[0, rows] = c * dc - s * ds
                base[1, rows] = s * dc + c * ds
        slot = place.slot(channel, per_shard)
        for index in (0, 1):
            wide = dot_f32(both, parts[channel % 2, index, 0])
            narrow = dot_f32(high, parts[channel % 2, index, 1])
            out[slot, half * index : half * (index + 1)] = wide[:half] + wide[half:] + narrow


def iterate(place, coherent, shards, mask, pairs, jones, near, far, error, gather, sums):
    first_hot = place.onehot(pairs, 0)
    second_hot = place.onehot(pairs, 1)
    rows = jones.shape[0]
    directions = rows // 8
    split = jnp.concatenate([p for p in pieces(jones[...], 3)])
    for side, hot in enumerate((first_hot, second_hot)):
        found = dot_f32(split, hot)
        found = found[:rows] + found[rows : 2 * rows] + found[2 * rows :]
        for run in range(place.runs):
            gather[side, run] = found[:, run * RUN : (run + 1) * RUN]
    weight = mask[:, pl.ds(place.first_lane, place.lanes)].astype(jnp.float32)
    channels = coherent.shape[0]
    per_shard = shards[0].shape[1]
    halves = directions // 8

    for run in range(place.runs):
        lanes = slice(run * RUN, (run + 1) * RUN)
        w = weight[:, lanes]

        def gains(side, h):
            return [gather[side, run, pl.ds(64 * h + n, 8, stride=8), :] for n in range(8)]

        for channel in range(channels):
            shard = shards[channel // per_shard]
            models = [None] * 8
            for h in range(halves):
                coh = [
                    coherent[channel, n * directions + 8 * h : n * directions + 8 * h + 8, lanes]
                    for n in range(8)
                ]
                toward_first = product(gains(0, h), coh)
                toward_second = product(gains(1, h), dagger(coh))
                for n in range(8):
                    near[h, channel, n] = toward_first[n]
                    far[h, channel, n] = toward_second[n]
                part = product(toward_first, dagger(gains(1, h)))
                models = part if h == 0 else [a + b for a, b in zip(models, part)]
            at = pl.multiple_of(place.first_lane + run * RUN, RUN)
            for n in range(8):
                model = jnp.sum(models[n], axis=0, keepdims=True)
                seen = shard[n, channel % per_shard, :, pl.ds(at, RUN)]
                error[channel, n : n + 1] = w * (seen - model)

        for h in range(halves):
            zero = jnp.zeros((8, RUN), jnp.float32)
            first, second, curve_first, curve_second = [zero] * 8, [zero] * 8, zero, zero
            for channel in range(channels):
                err = [jnp.broadcast_to(error[channel, n : n + 1], (8, RUN)) for n in range(8)]
                z = [near[h, channel, n] for n in range(8)]
                y = [far[h, channel, n] for n in range(8)]
                first = [a + b for a, b in zip(first, product(err, y))]
                second = [a + b for a, b in zip(second, product(dagger(err), z))]
                for n in range(8):
                    curve_first = curve_first + y[n] * y[n]
                    curve_second = curve_second + z[n] * z[n]
            for n in range(8):
                sums[0, run, pl.ds(64 * h + n, 8, stride=8), :] = first[n]
                sums[1, run, pl.ds(64 * h + n, 8, stride=8), :] = second[n]
            sums[0, run, rows + 8 * h : rows + 8 * h + 8] = w * curve_first
            sums[1, run, rows + 8 * h : rows + 8 * h + 8] = w * curve_second

    total = None
    height = sums.shape[2]
    for side, hot in enumerate((first_hot, second_hot)):
        whole = jnp.concatenate([sums[side, run] for run in range(place.runs)], axis=1)
        found = dot_f32(jnp.concatenate(pieces(whole, 2)), hot, 1)
        found = found[:height] + found[height:]
        total = found if total is None else total + found
    return total


def pack(total, rows):
    half = rows // 2
    low = jnp.concatenate([total[:half], total[rows : rows + half // 8]])
    high = jnp.concatenate([total[half:rows], total[rows + half // 8 :]])
    lane = lax.broadcasted_iota(jnp.int32, low.shape, 1)
    return jnp.where(lane < BLOCK, low, pltpu.roll(high, BLOCK, 1))


def unpack(packed):
    half = packed.shape[0] * 8 // 9
    turned = pltpu.roll(packed, BLOCK, 1)
    return jnp.concatenate([packed[:half], turned[:half], packed[half:], turned[half:]])


def update(jones, lanes, sums, keep=None):
    rows = jones.shape[0]
    for d in range(rows // 8):
        now = jones[8 * d : 8 * d + 8, lanes]
        curve = sums[rows + d : rows + d + 1] + EPSILON
        new = now + STEP_SIZE * sums[8 * d : 8 * d + 8] / curve
        if keep is not None:
            new = jnp.where(keep, new, now)
        jones[8 * d : 8 * d + 8, lanes] = new


def block_zero():
    return lax.broadcasted_iota(jnp.int32, (8, RUN), 1) < BLOCK


def first_kernel(
    runs, pairs, mask, coherent, own, other, s0, s1, s2, s3, packed, mine, jones, near, far, error, gather, sums
):
    place = Place(runs)
    count = own.shape[0] * own.shape[1]
    for ref, core in ((own, place.core), (other, 1 - place.core)):
        at = pl.ds(pl.multiple_of(core * count, count), count)
        value = ref[:, :, 0:RUN]
        jones[at, 0:RUN] = value.reshape(count, RUN)
        value = ref[:, :, pl.ds(place.first_station, place.width)]
        jones[at, RUN:] = value.reshape(count, place.width)
    total = iterate(place, coherent, (s0, s1, s2, s3), mask, pairs, jones, near, far, error, gather, sums)
    packed[...] = pack(total[:, :RUN], jones.shape[0])
    mine[...] = total[:, RUN:]


def second_kernel(
    runs, pairs, mask, coherent, before, mine, sum_here, sum_there, s0, s1, s2, s3,
    packed, jones, near, far, error, gather, sums,
):
    place = Place(runs)
    jones[...] = before[...]
    update(jones, slice(0, RUN), unpack(sum_here[...] + sum_there[...]), block_zero())
    update(jones, slice(RUN, None), mine[...])
    total = iterate(place, coherent, (s0, s1, s2, s3), mask, pairs, jones, near, far, error, gather, sums)
    rows = jones.shape[0]
    held = packed.shape[0] - rows // 2
    packed[:held] = pack(total[:, :RUN], rows)
    update(jones, slice(RUN, None), total[:, RUN:])
    packed[held:] = jones[pl.ds(pl.multiple_of((1 - place.core) * (rows // 2), rows // 2), rows // 2), RUN:]


def join_kernel(here, there, jones, out):
    held = out.shape[0] - 2 * (jones.shape[0] // 2)
    half = jones.shape[0] // 2
    core = lax.axis_index("dir")
    out[:held] = here[:held] + there[:held]
    out[held : held + half] = jones[pl.ds(pl.multiple_of(core * half, half), half), RUN:]
    out[held + half :] = there[held:]


def last_kernel(
    runs, pairs, mask, coherent, before, here, there, s0, s1, s2, s3, residual, solved, jones, gather
):
    place = Place(runs)
    jones[...] = before[...]
    rows = jones.shape[0]
    half = rows // 2
    held = here.shape[0] - rows
    update(jones, slice(0, RUN), unpack(here[:held] + there[:held]), block_zero())

    blk = lax.axis_index("blk")
    for ref, b in ((here, blk), (there, 1 - blk)):
        for at, core in ((held, place.core), (held + half, 1 - place.core)):
            lanes = pl.ds(pl.multiple_of((2 * b + core) * place.width, place.width), place.width)
            solved[:, :, lanes] = ref[at : at + half].reshape(half // 8, 8, place.width)
    zero = jones[pl.ds(pl.multiple_of(place.core * half, half), half), 0:RUN].reshape(half // 8, 8, RUN)
    lane = lax.broadcasted_iota(jnp.int32, zero.shape, 2)
    solved[:, :, 0:RUN] = jnp.where(lane < BLOCK, zero, solved[:, :, 0:RUN])

    directions = rows // 8
    run = lax.rem(place.chan, runs)
    shift = pl.multiple_of(run * RUN, RUN)
    split = jnp.concatenate([p for p in pieces(jones[...], 3)])
    for side in (0, 1):
        found = dot_f32(split, place.onehot(pairs, side))
        found = found[:rows] + found[rows : 2 * rows] + found[2 * rows :]
        for index in range(runs):
            gather[side, index] = found[:, index * RUN : (index + 1) * RUN]
    at = pl.multiple_of(place.first_lane + shift, RUN)
    w = mask[:, pl.ds(at, RUN)].astype(jnp.float32)
    shards = (s0, s1, s2, s3)
    channels = coherent.shape[0]
    per_shard = s0.shape[1]
    here_lanes = pl.ds(shift, RUN)

    def gains(side, h):
        return [gather[side, run, pl.ds(64 * h + n, 8, stride=8), :] for n in range(8)]

    for channel in range(channels):
        models = None
        for h in range(directions // 8):
            coh = [
                coherent[channel, n * directions + 8 * h : n * directions + 8 * h + 8, here_lanes]
                for n in range(8)
            ]
            part = product(product(gains(0, h), coh), dagger(gains(1, h)))
            models = part if models is None else [a + b for a, b in zip(models, part)]
        shard = shards[channel // per_shard]
        true_channel = place.slot(channel, per_shard)
        for n in range(8):
            model = jnp.sum(models[n], axis=0, keepdims=True)
            seen = shard[n, channel % per_shard, :, pl.ds(at, RUN)]
            residual[n, true_channel] = w * (seen - model)


def call(kernel, out_shape, scratch, *operands):
    return pl.pallas_call(
        kernel,
        out_shape=out_shape,
        in_specs=[pl.BlockSpec(memory_space=pltpu.VMEM)] * len(operands),
        out_specs=jax.tree.map(lambda _: pl.BlockSpec(memory_space=pltpu.VMEM), out_shape),
        scratch_shapes=scratch,
        compiler_params=pltpu.CompilerParams(vmem_limit_bytes=40 << 20),
    )(*operands)


def f32(*shape):
    return jax.ShapeDtypeStruct(shape, jnp.float32)


def swap(x, axis, bit=1):
    return lax.ppermute(x, axis, [(i, i ^ bit) for i in range(lax.axis_size(axis))])


def per_device_owned(
    visibilities,
    antenna_pairs,
    valid_mask,
    station_positions,
    source_offsets,
    brightness,
    source_cluster,
    jones_gains,
):
    relay_count = lax.axis_size("chan")
    runs = relay_count // lax.axis_size("dir")
    per_shard = visibilities.shape[1]
    channels = per_shard * relay_count
    half_directions = jones_gains.shape[0]
    directions = 2 * half_directions
    rows = 8 * directions
    lanes = runs * RUN
    width = runs * BLOCK
    sources = source_offsets.shape[1]

    other = swap(jones_gains, "dir")
    shards = [visibilities] + [swap(visibilities, "chan", bit) for bit in range(1, relay_count)]
    coherent = call(
        functools.partial(coherency_kernel, runs, channels, per_shard),
        f32(channels, rows, lanes),
        [
            pltpu.VMEM((2, sources, lanes), jnp.float32),
            pltpu.VMEM((2, sources, lanes), jnp.float32),
            pltpu.VMEM((2, 2, 2, sources, lanes), jnp.bfloat16),
        ],
        antenna_pairs,
        station_positions,
        source_offsets,
        brightness,
        source_cluster[None, :],
    )
    scratch = [
        pltpu.VMEM((directions // 8, channels, 8, 8, RUN), jnp.float32),
        pltpu.VMEM((directions // 8, channels, 8, 8, RUN), jnp.float32),
        pltpu.VMEM((channels, 8, RUN), jnp.float32),
        pltpu.VMEM((2, runs, rows, RUN), jnp.float32),
        pltpu.VMEM((2, runs, rows + directions, RUN), jnp.float32),
    ]
    table = f32(rows, RUN + width)
    held = (rows + directions) // 2
    packed, mine, jones = call(
        functools.partial(first_kernel, runs),
        (f32(held, RUN), f32(rows + directions, width), table),
        scratch,
        antenna_pairs,
        valid_mask,
        coherent,
        jones_gains,
        other,
        *shards,
    )
    packed = packed + swap(packed, "dir")
    there = swap(packed, "blk")
    packed, jones = call(
        functools.partial(second_kernel, runs),
        (f32(held + rows // 2, RUN), table),
        scratch,
        antenna_pairs,
        valid_mask,
        coherent,
        jones,
        mine,
        packed,
        there,
        *shards,
    )
    joined = call(
        join_kernel,
        f32(held + rows, RUN),
        [],
        packed,
        swap(packed, "dir"),
        jones,
    )
    residual, solved = call(
        functools.partial(last_kernel, runs),
        (f32(8, channels, 1, RUN), f32(half_directions, 8, station_positions.shape[1])),
        [pltpu.VMEM((rows, RUN + width), jnp.float32), pltpu.VMEM((2, runs, rows, RUN), jnp.float32)],
        antenna_pairs,
        valid_mask,
        coherent,
        jones,
        joined,
        swap(joined, "blk"),
        *shards,
    )
    held_here = lax.axis_index("chan") // runs == lax.axis_index("dir")
    residual = jnp.where(held_here, residual, swap(residual, "dir"))
    return residual, solved


def owned_layout(mesh, shapes):
    sizes = mesh.shape
    owners = sizes["chan"] * sizes["blk"]
    visibilities, pairs, jones = shapes
    return (
        owners == BLOCKS
        and sizes["blk"] == 2
        and sizes["dir"] == 2
        and sizes["chan"] == 4
        and pairs[1] * pairs[2] == owners * RUN
        and jones[0] == 16
        and jones[2] == BLOCKS * BLOCK
        and visibilities[1] % sizes["chan"] == 0
    )


def solution(mesh):
    in_specs = (
        P("groups", "chan", "blk", None),
        P(None, "blk", None),
        P("blk", "groups"),
        P(),
        P(),
        P(),
        P(),
        P("dir", "groups", None),
    )
    out_specs = (P("groups", None, "blk", "chan"), P("dir", "groups", None))

    def run(*arrays):
        owned = owned_layout(mesh, (arrays[0].shape, arrays[1].shape, arrays[7].shape))
        body = per_device_owned if owned else per_device
        return jax.shard_map(
            body, mesh=mesh, in_specs=in_specs, out_specs=out_specs, check_vma=False
        )(*arrays)

    return run
```

```python
import functools
import math

import jax
import jax.numpy as jnp
from jax import lax
from jax.experimental import pallas as pl
from jax.experimental.pallas import tpu as pltpu
from jax.sharding import PartitionSpec as P

ITERS = 2


TWO_PI = 2.0 * math.pi
STEP_SIZE = 0.3
EPSILON = 1e-06
HIGHEST = lax.Precision.HIGHEST


def jones_product(former, latter):
    real_list = []
    imag_list = []
    for row_number in (0, 1):
        for column in (0, 1):
            real_list.append(
                former[2 * row_number] * latter[column]
                - former[4 + 2 * row_number] * latter[4 + column]
                + former[2 * row_number + 1] * latter[2 + column]
                - former[5 + 2 * row_number] * latter[6 + column]
            )
            imag_list.append(
                former[2 * row_number] * latter[4 + column]
                + former[4 + 2 * row_number] * latter[column]
                + former[2 * row_number + 1] * latter[6 + column]
                + former[5 + 2 * row_number] * latter[2 + column]
            )
    return jnp.stack(real_list + imag_list)


def adjoint(matrix):
    return jnp.stack(
        [matrix[0], matrix[2], matrix[1], matrix[3], -matrix[4], -matrix[6], -matrix[5], -matrix[7]]
    )


def source_table(brightness, source_cluster, direction_ids):
    member = (source_cluster[None, :] == direction_ids[:, None]).astype(jnp.float32)
    return (brightness[:, None, :] * member[None, :, :]).reshape(
        4 * direction_ids.shape[0], brightness.shape[1]
    )


def coherency(bright_table, geometry, scales):
    phase_grid = (TWO_PI * scales)[None, :, None] * geometry[:, None, :]
    phases_flat = phase_grid.reshape(geometry.shape[0], -1)
    real_block = jnp.dot(bright_table, jnp.cos(phases_flat), precision=HIGHEST)
    imag_block = -jnp.dot(bright_table, jnp.sin(phases_flat), precision=HIGHEST)
    dir_count = bright_table.shape[0] // 4
    return jnp.concatenate([real_block, imag_block], axis=0).reshape(
        8, dir_count, scales.shape[0], geometry.shape[1]
    )


def per_device(
    visibilities,
    antenna_pairs,
    valid_mask,
    station_positions,
    source_offsets,
    brightness,
    source_cluster,
    jones_gains,
):
    relay_count = lax.axis_size("chan")
    base_count = antenna_pairs.shape[2] // relay_count
    station_count = station_positions.shape[1]
    offset = lax.axis_index("chan") * base_count
    own_pairs = lax.dynamic_slice_in_dim(antenna_pairs[:, 0], offset, base_count, 1)
    first_station = own_pairs[0]
    second_station = own_pairs[1]
    weight_row = lax.dynamic_slice_in_dim(valid_mask[0], offset, base_count, 0).astype(jnp.float32)
    regrouped = lax.all_to_all(visibilities, "chan", split_axis=3, concat_axis=1, tiled=True)[
        :, :, 0, :
    ]
    total_channels = regrouped.shape[1]
    own_directions = jones_gains.shape[0]
    channel_ids = jnp.arange(total_channels)
    gains_now = jones_gains
    direction_ids = lax.axis_index("dir") * own_directions + jnp.arange(own_directions)
    local_channels = regrouped.shape[1]
    scales = 1.0 + 0.5 * channel_ids.astype(jnp.float32) / total_channels
    u_coord = station_positions[0][first_station] - station_positions[0][second_station]
    v_coord = station_positions[1][first_station] - station_positions[1][second_station]
    geometry = (
        source_offsets[0][:, None] * u_coord[None, :]
        + source_offsets[1][:, None] * v_coord[None, :]
    )
    bright_table = source_table(brightness, source_cluster, direction_ids)
    group_size = math.gcd(local_channels, max(1, 2048 // base_count))
    group_count = local_channels // group_size
    scale_groups = scales.reshape(group_count, group_size)
    onehot_first = (first_station[:, None] == jnp.arange(station_count)[None, :]).astype(
        jnp.float32
    )
    onehot_second = (second_station[:, None] == jnp.arange(station_count)[None, :]).astype(
        jnp.float32
    )

    def station_gains(gains_current):
        gain_first = jnp.take(gains_current, first_station, axis=2).transpose(1, 0, 2)[
            :, :, None, :
        ]
        gain_second = jnp.take(gains_current, second_station, axis=2).transpose(1, 0, 2)[
            :, :, None, :
        ]
        return (gain_first, gain_second)

    def residual_of(gains_current):
        gain_first, gain_second = station_gains(gains_current)

        def residual_one_group(scale_group):
            coherent = coherency(bright_table, geometry, scale_group)
            return jnp.sum(
                jones_product(jones_product(gain_first, coherent), adjoint(gain_second)), axis=1
            )

        partial_model = jnp.moveaxis(lax.map(residual_one_group, scale_groups), 0, 1).reshape(
            8, local_channels, base_count
        )
        model_vis = lax.psum(partial_model, "dir")
        return weight_row * (regrouped - model_vis)

    for iteration in range(ITERS):
        residual_now = residual_of(gains_now)
        updated_gain_first, updated_gain_second = station_gains(gains_now)
        resid_groups = jnp.moveaxis(
            residual_now.reshape(8, group_count, group_size, base_count), 1, 0
        )
        dir_count = gains_now.shape[0]

        def updated_one_group(running, inputs):
            scale_group, resid_group = inputs
            coherent = coherency(bright_table, geometry, scale_group)
            toward_second = jones_product(updated_gain_second, adjoint(coherent))
            toward_first = jones_product(updated_gain_first, coherent)
            grad_first = jnp.sum(jones_product(resid_group[:, None], toward_second), axis=2)
            grad_second = jnp.sum(
                jones_product(adjoint(resid_group)[:, None], toward_first), axis=2
            )
            curv_first = jnp.sum(toward_second * toward_second, axis=(0, 2))
            curv_second = jnp.sum(toward_first * toward_first, axis=(0, 2))
            return (
                (
                    running[0] + grad_first,
                    running[1] + grad_second,
                    running[2] + curv_first,
                    running[3] + curv_second,
                ),
                None,
            )

        zero_sums = (
            jnp.zeros((8, dir_count, base_count), jnp.float32),
            jnp.zeros((8, dir_count, base_count), jnp.float32),
            jnp.zeros((dir_count, base_count), jnp.float32),
            jnp.zeros((dir_count, base_count), jnp.float32),
        )
        totals, ignored = lax.scan(updated_one_group, zero_sums, (scale_groups, resid_groups))
        grad_station = jnp.einsum(
            "cdb,bs->dcs", totals[0], onehot_first, precision=HIGHEST
        ) + jnp.einsum("cdb,bs->dcs", totals[1], onehot_second, precision=HIGHEST)
        curv_station = jnp.dot(weight_row * totals[2], onehot_first, precision=HIGHEST) + jnp.dot(
            weight_row * totals[3], onehot_second, precision=HIGHEST
        )
        grad_station, curv_station = lax.psum((grad_station, curv_station), ("chan", "blk"))
        gains_now = gains_now + STEP_SIZE * grad_station / (curv_station[:, None, :] + EPSILON)
    residual_now = residual_of(gains_now)
    return (residual_now[:, :, None, :], gains_now)


COS_TERMS = (
    0.9999999890590228,
    -19.739204499454,
    64.93911745989914,
    -85.45013953093448,
    60.16763095128989,
    -25.96759924954187,
    6.528658162606979,
)
SIN_TERMS = (
    6.283185302511502,
    -41.34170040531754,
    81.6051313857969,
    -76.70301535383193,
    42.02592698564183,
    -14.899846667160109,
    3.2381375090822355,
)
RUN = 128
BLOCK = 64
BLOCKS = 8
PAIR = 2 * RUN


def pieces(value, count):
    result = []
    for index in range(count):
        piece = value.astype(jnp.bfloat16)
        result.append(piece)
        if index < count - 1:
            value = value - piece.astype(jnp.float32)
    return result


def dot_f32(left, right, contract_right=0):
    return lax.dot_general(
        left,
        right,
        (((1,), (contract_right,)), ((), ())),
        preferred_element_type=jnp.float32,
    )


def horner(terms, x):
    total = jnp.full_like(x, terms[-1])
    for term in terms[-2::-1]:
        total = total * x + term
    return total


def turn_pair(turns):
    rest = turns - jnp.round(turns)
    square = rest * rest
    return horner(COS_TERMS, square), horner([-term for term in SIN_TERMS], square) * rest


def product(a, b, dagger_a=False, dagger_b=False, total=None):
    result = [None] * 8 if total is None else list(total)

    def add(n, x, y, positive):
        term = x * y
        if result[n] is None:
            result[n] = term if positive else -term
        else:
            result[n] = result[n] + term if positive else result[n] - term

    for row in (0, 1):
        for col in (0, 1):
            n = 2 * row + col
            for inner in (0, 1):
                i = 2 * inner + row if dagger_a else 2 * row + inner
                j = 2 * col + inner if dagger_b else 2 * inner + col
                add(n, a[i], b[j], True)
                add(n, a[4 + i], b[4 + j], dagger_a != dagger_b)
                if dagger_a:
                    add(4 + n, a[i], b[4 + j], not dagger_b)
                    add(4 + n, a[4 + i], b[j], False)
                else:
                    add(4 + n, a[4 + i], b[j], True)
                    add(4 + n, a[i], b[4 + j], not dagger_b)
    return result


def sum_rows(parts):
    row = lax.broadcasted_iota(jnp.int32, parts[0].shape, 0)
    low = row < 4
    parts = [
        jnp.where(low, a, b) + pltpu.roll(jnp.where(low, b, a), 4, 0)
        for a, b in zip(parts[:4], parts[4:])
    ]
    for step in (2, 1):
        low = jnp.bitwise_and(row, step) == 0
        parts = [
            jnp.where(low, a + pltpu.roll(a, 8 - step, 0), b + pltpu.roll(b, step, 0))
            for a, b in zip(parts[:step], parts[step:])
        ]
    return parts[0]


class Place:
    def __init__(self):
        self.chan = lax.axis_index("chan")
        self.core = lax.axis_index("dir")
        self.blk = lax.axis_index("blk")
        self.first_lane = pl.multiple_of(self.core * PAIR, PAIR)
        self.last_core = self.chan // 2
        self.last_lane = pl.multiple_of(self.chan * RUN, RUN)

    def first_station(self, core):
        return pl.multiple_of((2 * self.blk + core) * RUN, RUN)

    def slot(self, channel, per_shard):
        return jnp.bitwise_xor(channel // per_shard, self.chan) * per_shard + channel % per_shard


def onehot(station, first_station):
    local = jnp.where(station < BLOCK, station, station - first_station + RUN)
    rows = lax.broadcasted_iota(jnp.int32, (2 * RUN, station.shape[1]), 0)
    return jnp.where(rows == local, 1.0, 0.0).astype(jnp.bfloat16)


def split_rows(value, count):
    split = [p.astype(jnp.float32) for p in pieces(value, count)]
    missing = -count * value.shape[0] % 16
    if missing:
        split.append(jnp.zeros((missing, value.shape[1]), jnp.float32))
    return jnp.concatenate(split).astype(jnp.bfloat16)


def grams(coh):
    re, im = coh[:4], coh[4:]
    size = [a * a + b * b for a, b in zip(re, im)]

    def cross(i, j, k, l):
        real = re[i] * re[j] + im[i] * im[j] + re[k] * re[l] + im[k] * im[l]
        imag = re[i] * im[j] - im[i] * re[j] + re[k] * im[l] - im[k] * re[l]
        return [real + real, imag + imag]

    inner = [size[0] + size[2], size[1] + size[3]] + cross(0, 1, 2, 3)
    outer = [size[0] + size[1], size[2] + size[3]] + cross(2, 0, 3, 1)
    return inner + outer


def curvature_of(gain, gram):
    re, im = gain[:4], gain[4:]
    size = [a * a + b * b for a, b in zip(re, im)]
    real = re[0] * re[1] + im[0] * im[1] + re[2] * re[3] + im[2] * im[3]
    imag = im[0] * re[1] - re[0] * im[1] + im[2] * re[3] - re[2] * im[3]
    total = (size[0] + size[2]) * gram[0] + (size[1] + size[3]) * gram[1] + real * gram[2] - imag * gram[3]
    return jnp.maximum(total, 0.0)


def coherency_kernel(
    channels, per_shard, pairs_at, positions_at, offsets_at, brightness_at, cluster_at, mask_at, seen_at, jones_at,
    out, last_out, gram, hots, last_hots, mask, seen, jones,
    pairs, positions, offsets, brightness, cluster, base, spin, parts, last_parts, sems,
):
    copies = [
        pltpu.make_async_copy(source, target, sems.at[index])
        for index, (source, target) in enumerate(
            (
                (pairs_at, pairs),
                (positions_at, positions),
                (offsets_at, offsets),
                (brightness_at, brightness),
                (cluster_at, cluster),
                (mask_at, mask),
                (seen_at, seen),
                (jones_at, jones),
            )
        )
    ]
    for copy in copies:
        copy.start()
    for copy in copies[:5]:
        copy.wait()
    place = Place()
    spans = []
    for hot_ref, lanes, core in (
        (hots, pl.ds(place.first_lane, PAIR), place.core),
        (last_hots, pl.ds(place.last_lane, RUN), place.last_core),
    ):
        first_station = place.first_station(core)
        table = jnp.concatenate([positions[:, 0:RUN], positions[:, pl.ds(first_station, RUN)]], axis=1)
        table = split_rows(table, 3)
        there = []
        for side in (0, 1):
            hot_ref[side] = onehot(pairs[side, :, lanes], first_station)
            found = dot_f32(table, hot_ref[side])
            there.append(found[0:2] + found[2:4] + found[4:6])
        spans.append(there[0] - there[1])
    span = jnp.concatenate(spans, axis=1)
    sources = offsets.shape[1]
    columns = jnp.transpose(jnp.concatenate([offsets[...], jnp.zeros((6, sources))]))
    step = 16
    for start in range(0, sources, step):
        rows = slice(start, start + step)
        geometry = columns[rows, 0:1] * span[0:1] + columns[rows, 1:2] * span[1:2]
        base[0, rows], base[1, rows] = turn_pair(geometry)
        spin[0, rows], spin[1, rows] = turn_pair(geometry * (0.5 / channels))

    directions = out.shape[1] // 12
    member = lax.broadcasted_iota(jnp.int32, (directions, sources), 0) == cluster[...]
    bright = jnp.concatenate([jnp.where(member, brightness[n : n + 1], 0.0) for n in range(4)])
    high, low = pieces(bright, 2)
    both = jnp.concatenate([high, low])
    half = 4 * directions

    def table_times(refs):
        wide = dot_f32(both, refs[0])
        return wide[:half] + wide[half:] + dot_f32(high, refs[1])

    for channel in range(channels):
        odd = channel % 2
        for start in range(0, sources, step):
            rows = slice(start, start + step)
            c, s = base[0, rows], base[1, rows]
            for index, value in enumerate((c, s)):
                for size, piece in enumerate(pieces(value, 2)):
                    parts[odd, index, size, rows] = piece[:, :PAIR]
                    last_parts[index, size, rows, odd * RUN : (odd + 1) * RUN] = piece[:, PAIR:]
            if channel < channels - 1:
                dc, ds = spin[0, rows], spin[1, rows]
                base[0, rows] = c * dc - s * ds
                base[1, rows] = s * dc + c * ds
        slot = place.slot(channel, per_shard)
        found = [table_times((parts[odd, index, 0], parts[odd, index, 1])) for index in (0, 1)]
        out[slot, :half] = found[0]
        out[slot, half : 2 * half] = found[1]
        out[slot, 2 * half :] = found[0] - found[1]
        entries = [found[n // 4][n % 4 * directions : (n % 4 + 1) * directions] for n in range(8)]
        for n, value in enumerate(grams(entries)):
            rows = slice(n * directions, (n + 1) * directions)
            gram[rows] = value if channel == 0 else gram[rows] + value
        if odd:
            for index in (0, 1):
                found = table_times((last_parts[index, 0], last_parts[index, 1]))
                for before in (0, 1):
                    slot = place.slot(channel - 1 + before, per_shard)
                    last_out[slot, half * index : half * (index + 1)] = found[:, before * RUN : (before + 1) * RUN]
    for copy in copies[5:]:
        copy.wait()


def gather_gains(table, hots, gather):
    rows = table.shape[0]
    split = jnp.concatenate(pieces(table, 2))
    for side in (0, 1):
        found = dot_f32(split, hots[side])
        found = found[:rows] + found[rows:]
        for run in range(found.shape[1] // RUN):
            gather[side, run] = found[:, run * RUN : (run + 1) * RUN]


def gains_of(gather, side, run, h):
    return [gather[side, run, pl.ds(64 * h + n, 8, stride=8), :] for n in range(8)]


def coherent_of(coherent, channel, h, lanes, directions, count):
    return [
        coherent[channel, n * directions + 8 * h : n * directions + 8 * h + 8, lanes] for n in range(count)
    ]


def small_product(a, b, turned=False):
    order = ((0, 1), (2, 3)) if turned else ((0, 2), (1, 3))
    return [
        a[2 * row] * b[order[col][0]] + a[2 * row + 1] * b[order[col][1]] for row in (0, 1) for col in (0, 1)
    ]


def less(a, b):
    return [x - y for x, y in zip(a, b)]


def plus(a, b):
    return [x + y for x, y in zip(a, b)]


def model_parts(first, second, coh):
    re, im, mixed = coh[:4], coh[4:8], coh[8:]
    p1 = small_product(first[:4], re)
    p2 = small_product(first[4:8], im)
    p3 = small_product(first[8:], mixed)
    zr = less(p1, p2)
    zi = less(plus(p1, p2), p3)
    return (
        small_product(zr, second[:4], True)
        + small_product(zi, second[4:8], True)
        + small_product(plus(zr, zi), second[8:], True)
    )


def model_of(parts):
    a, b, d = parts[:4], parts[4:8], parts[8:]
    return plus(a, b) + plus(less(d, a), b)


def with_difference(matrix):
    return matrix + less(matrix[:4], matrix[4:])


def multiply_into(total, a, b, conj_b=False):
    real = a[0] * b[0]
    imag = a[1] * b[0]
    if total is not None:
        real, imag = total[0] + real, total[1] + imag
    if conj_b:
        return real + a[1] * b[1], imag - a[0] * b[1]
    return real - a[1] * b[1], imag + a[0] * b[1]


def iterate(place, coherent, gram, hots, shards, mask, jones, model, error, gather, sums):
    rows = jones.shape[0]
    directions = rows // 8
    halves = rows // 64
    gather_gains(jones[...], hots, gather)
    weight = mask[:, pl.ds(place.first_lane, PAIR)].astype(jnp.float32)
    channels = coherent.shape[0]
    per_shard = shards[0].shape[1]
    for run in range(2):
        lanes = slice(run * RUN, (run + 1) * RUN)
        w = weight[:, lanes]
        at = pl.multiple_of(place.first_lane + run * RUN, RUN)
        for h in range(halves):
            first_gain = with_difference(gains_of(gather, 0, run, h))
            second_gain = with_difference(gains_of(gather, 1, run, h))
            for channel in range(channels):
                coh = coherent_of(coherent, channel, h, lanes, directions, 12)
                part = model_parts(first_gain, second_gain, coh)
                if h > 0:
                    part = [a + model[channel, n] for n, a in enumerate(part)]
                if h < halves - 1:
                    for n in range(12):
                        model[channel, n] = part[n]
                else:
                    seen = shards[channel // per_shard][:, channel % per_shard, 0, pl.ds(at, RUN)]
                    err = w * (seen - sum_rows(model_of(part)))
                    error[channel, 0] = err
                    error[channel, 1] = err + pltpu.roll(err, 4, 0)

        for h in range(halves):
            first_gain, second_gain = gains_of(gather, 0, run, h), gains_of(gather, 1, run, h)
            second = [None] * 4
            for i in (0, 1):
                zero = jnp.zeros((8, RUN), jnp.float32)
                p1, p2, p3 = [zero] * 8, [zero] * 8, [zero] * 8
                for channel in range(channels):
                    coh = coherent_of(coherent, channel, h, lanes, directions, 12)

                    def err(tile, n):
                        return jnp.broadcast_to(error[channel, tile, n : n + 1], (8, RUN))

                    for j in (0, 1):
                        er, ei, es = err(0, 2 * i + j), err(0, 4 + 2 * i + j), err(1, 2 * i + j)
                        for kl in range(4):
                            n = 4 * j + kl
                            p1[n] = p1[n] + er * coh[kl]
                            p2[n] = p2[n] + ei * coh[4 + kl]
                            p3[n] = p3[n] + es * coh[8 + kl]
                outer = list(zip(plus(p1, p2), plus(less(p3, p1), p2)))
                for l in (0, 1):
                    total = None
                    for j in (0, 1):
                        for k in (0, 1):
                            g = (second_gain[2 * j + k], second_gain[4 + 2 * j + k])
                            total = multiply_into(total, outer[4 * j + 2 * l + k], g)
                    for imag in (0, 1):
                        n = 4 * imag + 2 * i + l
                        sums[0, run, pl.ds(64 * h + n, 8, stride=8), :] = total[imag]
                for a in (0, 1):
                    for l in (0, 1):
                        for k in (0, 1):
                            g = (first_gain[2 * i + k], first_gain[4 + 2 * i + k])
                            second[2 * a + l] = multiply_into(
                                second[2 * a + l], g, outer[4 * a + 2 * k + l], conj_b=True
                            )
            for n in range(8):
                sums[1, run, pl.ds(64 * h + n, 8, stride=8), :] = second[n % 4][n // 4]
            form = [gram[n * directions + 8 * h : n * directions + 8 * h + 8, lanes] for n in range(8)]
            sums[0, run, rows + 8 * h : rows + 8 * h + 8] = w * curvature_of(second_gain, form[:4])
            sums[1, run, rows + 8 * h : rows + 8 * h + 8] = w * curvature_of(first_gain, form[4:])

    total = None
    height = sums.shape[2]
    for side in (0, 1):
        whole = jnp.concatenate([sums[side, run] for run in range(2)], axis=1)
        found = dot_f32(jnp.concatenate(pieces(whole, 2)), hots[side], 1)
        found = found[:height] + found[height:]
        total = found if total is None else total + found
    return total


def pack(total, rows):
    half = rows // 2
    low = jnp.concatenate([total[:half], total[rows : rows + half // 8]])
    high = jnp.concatenate([total[half:rows], total[rows + half // 8 :]])
    lane = lax.broadcasted_iota(jnp.int32, low.shape, 1)
    return jnp.where(lane < BLOCK, low, pltpu.roll(high, BLOCK, 1))


def unpack(packed):
    half = packed.shape[0] * 8 // 9
    turned = pltpu.roll(packed, BLOCK, 1)
    return jnp.concatenate([packed[:half], turned[:half], packed[half:], turned[half:]])


def update(jones, lanes, sums, keep=None):
    rows = jones.shape[0]
    for d in range(rows // 8):
        now = jones[8 * d : 8 * d + 8, lanes]
        ratio = STEP_SIZE / (sums[rows + d : rows + d + 1] + EPSILON)
        new = now + ratio * sums[8 * d : 8 * d + 8]
        if keep is not None:
            new = jnp.where(keep, new, now)
        jones[8 * d : 8 * d + 8, lanes] = new


def block_zero():
    return lax.broadcasted_iota(jnp.int32, (8, RUN), 1) < BLOCK


def first_kernel(
    mask, coherent, gram, hots, own, other, s0, s1, s2, s3, packed, mine, jones, model, error, gather, sums
):
    place = Place()
    count = own.shape[0] * own.shape[1]
    for ref, core in ((own, place.core), (other, 1 - place.core)):
        at = pl.ds(pl.multiple_of(core * count, count), count)
        jones[at, 0:RUN] = ref[:, :, 0:RUN].reshape(count, RUN)
        window = ref[:, :, pl.ds(place.first_station(place.core), RUN)]
        jones[at, RUN:] = window.reshape(count, RUN)
    total = iterate(
        place, coherent, gram, hots, (s0, s1, s2, s3), mask, jones, model, error, gather, sums
    )
    packed[...] = pack(total[:, :RUN], jones.shape[0])
    mine[...] = total[:, RUN:]


def second_kernel(
    mask, coherent, gram, hots, before, mine, sum_here, sum_there, s0, s1, s2, s3,
    packed, jones, model, error, gather, sums,
):
    place = Place()
    jones[...] = before[...]
    update(jones, slice(0, RUN), unpack(sum_here[...] + sum_there[...]), block_zero())
    update(jones, slice(RUN, None), mine[...])
    total = iterate(
        place, coherent, gram, hots, (s0, s1, s2, s3), mask, jones, model, error, gather, sums
    )
    rows = jones.shape[0]
    held = packed.shape[0] - rows
    packed[:held] = pack(total[:, :RUN], rows)
    update(jones, slice(RUN, None), total[:, RUN:])
    packed[held:] = jones[:, RUN:]


def join_kernel(here, there, out):
    half = here.shape[0] * 8 // 25
    held = here.shape[0] - 2 * half
    at = pl.ds(pl.multiple_of(held + lax.axis_index("dir") * half, 8), half)
    out[:held] = here[:held] + there[:held]
    out[held : held + half] = here[at]
    out[held + half :] = there[at]


def last_kernel(
    mask, coherent, hots, before, mine, other, here, there, s0, s1, s2, s3, residual, solved, jones, gather
):
    place = Place()
    rows = before.shape[0]
    half = rows // 2
    held = here.shape[0] - rows
    own_core_last = place.last_core == place.core
    jones[:, 0:RUN] = before[:, 0:RUN]
    jones[:, RUN:] = jnp.where(own_core_last, mine[held:], other[held:])
    update(jones, slice(0, RUN), unpack(here[:held] + there[:held]), block_zero())

    for ref, blk in ((here, place.blk), (there, 1 - place.blk)):
        for at, core in ((held, place.core), (held + half, 1 - place.core)):
            lanes = pl.ds(pl.multiple_of((2 * blk + core) * RUN, RUN), RUN)
            solved[:, :, lanes] = ref[at : at + half].reshape(half // 8, 8, RUN)
    zero = jones[pl.ds(pl.multiple_of(place.core * half, half), half), 0:RUN].reshape(half // 8, 8, RUN)
    lane = lax.broadcasted_iota(jnp.int32, zero.shape, 2)
    solved[:, :, 0:RUN] = jnp.where(lane < BLOCK, zero, solved[:, :, 0:RUN])

    gather_gains(jones[...], hots, gather)
    w = mask[:, pl.ds(place.last_lane, RUN)].astype(jnp.float32)
    shards = (s0, s1, s2, s3)
    channels = coherent.shape[0]
    per_shard = s0.shape[1]
    gains = [[gains_of(gather, side, 0, h) for h in range(rows // 64)] for side in (0, 1)]
    for channel in range(channels):
        part = None
        for h in range(rows // 64):
            coh = coherent_of(coherent, channel, h, slice(0, RUN), rows // 8, 8)
            z = product(gains[0][h], coh)
            part = product(z, gains[1][h], dagger_b=True, total=part)
        seen = shards[channel // per_shard][:, channel % per_shard, 0, pl.ds(place.last_lane, RUN)]
        residual[:, place.slot(channel, per_shard), 0] = w * (seen - sum_rows(part))


def call(kernel, out_shape, scratch, operands, space=pltpu.VMEM):
    return pl.pallas_call(
        kernel,
        out_shape=out_shape,
        in_specs=[pl.BlockSpec(memory_space=space)] * len(operands),
        out_specs=jax.tree.map(lambda _: pl.BlockSpec(memory_space=pltpu.VMEM), out_shape),
        scratch_shapes=scratch,
        compiler_params=pltpu.CompilerParams(vmem_limit_bytes=40 << 20),
    )(*[pltpu.with_memory_space_constraint(x, space) for x in operands])


def f32(*shape):
    return jax.ShapeDtypeStruct(shape, jnp.float32)


def bf16(*shape):
    return jax.ShapeDtypeStruct(shape, jnp.bfloat16)


def swap(x, axis, bit=1):
    return lax.ppermute(x, axis, [(i, i ^ bit) for i in range(lax.axis_size(axis))])


def per_device_owned(
    visibilities,
    antenna_pairs,
    valid_mask,
    station_positions,
    source_offsets,
    brightness,
    source_cluster,
    jones_gains,
):
    relay_count = lax.axis_size("chan")
    per_shard = visibilities.shape[1]
    channels = per_shard * relay_count
    half_directions = jones_gains.shape[0]
    directions = 2 * half_directions
    rows = 8 * directions
    sources = source_offsets.shape[1]

    other = swap(jones_gains, "dir")
    shards = [swap(visibilities, "chan", bit) for bit in range(1, relay_count)]
    kept = (valid_mask, visibilities, jones_gains)
    inputs = (antenna_pairs, station_positions, source_offsets, brightness, source_cluster[None, :])
    coherent, last_coherent, gram, hots, last_hots, mask, seen, own = call(
        functools.partial(coherency_kernel, channels, per_shard),
        (
            f32(channels, 12 * directions, PAIR),
            f32(channels, 8 * directions, RUN),
            f32(8 * directions, PAIR),
            bf16(2, 2 * RUN, PAIR),
            bf16(2, 2 * RUN, RUN),
            *[jax.ShapeDtypeStruct(x.shape, x.dtype) for x in kept],
        ),
        [pltpu.VMEM(x.shape, x.dtype) for x in inputs]
        + [
            pltpu.VMEM((2, sources, PAIR + RUN), jnp.float32),
            pltpu.VMEM((2, sources, PAIR + RUN), jnp.float32),
            pltpu.VMEM((2, 2, 2, sources, PAIR), jnp.bfloat16),
            pltpu.VMEM((2, 2, sources, 2 * RUN), jnp.bfloat16),
            pltpu.SemaphoreType.DMA((len(inputs + kept),)),
        ],
        inputs + kept,
        pltpu.HBM,
    )
    shards = [seen] + shards
    scratch = [
        pltpu.VMEM((channels, 12, 8, RUN), jnp.float32),
        pltpu.VMEM((channels, 2, 8, RUN), jnp.float32),
        pltpu.VMEM((2, 2, rows, RUN), jnp.float32),
        pltpu.VMEM((2, 2, rows + directions, RUN), jnp.float32),
    ]
    table = f32(rows, 2 * RUN)
    held = (rows + directions) // 2
    packed, mine, jones = call(
        first_kernel,
        (f32(held, RUN), f32(rows + directions, RUN), table),
        scratch,
        (mask, coherent, gram, hots, own, other, *shards),
    )
    packed = packed + swap(packed, "dir")
    there = swap(packed, "blk")
    mine, jones = call(
        second_kernel,
        (f32(held + rows, RUN), table),
        scratch,
        (mask, coherent, gram, hots, jones, mine, packed, there, *shards),
    )
    other = swap(mine, "dir")
    joined = call(join_kernel, f32(held + rows, RUN), [], (mine, other))
    return call(
        last_kernel,
        (f32(8, channels, 1, RUN), f32(half_directions, 8, station_positions.shape[1])),
        [pltpu.VMEM((rows, 2 * RUN), jnp.float32), pltpu.VMEM((2, 1, rows, RUN), jnp.float32)],
        (mask, last_coherent, last_hots, jones, mine, other, joined, swap(joined, "blk"), *shards),
    )


def owned_layout(mesh, shapes):
    sizes = mesh.shape
    owners = sizes["chan"] * sizes["blk"]
    visibilities, pairs, jones = shapes
    return (
        owners == BLOCKS
        and sizes["blk"] == 2
        and sizes["dir"] == 2
        and sizes["chan"] == 4
        and pairs[1] * pairs[2] == owners * RUN
        and jones[0] == 16
        and jones[2] == BLOCKS * BLOCK
        and visibilities[1] % sizes["chan"] == 0
    )


def solution(mesh):
    in_specs = (
        P("groups", "chan", "blk", None),
        P(None, "blk", None),
        P("blk", "groups"),
        P(),
        P(),
        P(),
        P(),
        P("dir", "groups", None),
    )
    out_specs = (P("groups", None, "blk", "chan"), P("dir", "groups", None))

    def run(*arrays):
        owned = owned_layout(mesh, (arrays[0].shape, arrays[1].shape, arrays[7].shape))
        body = per_device_owned if owned else per_device
        return jax.shard_map(
            body, mesh=mesh, in_specs=in_specs, out_specs=out_specs, check_vma=False
        )(*arrays)

    return run
```

```python
import functools
import math

import jax
import jax.numpy as jnp
from jax import lax
from jax.experimental import pallas as pl
from jax.experimental.pallas import tpu as pltpu
from jax.sharding import PartitionSpec as P

ITERS = 2


TWO_PI = 2.0 * math.pi
STEP_SIZE = 0.3
EPSILON = 1e-06
HIGHEST = lax.Precision.HIGHEST


def jones_product(former, latter):
    real_list = []
    imag_list = []
    for row_number in (0, 1):
        for column in (0, 1):
            real_list.append(
                former[2 * row_number] * latter[column]
                - former[4 + 2 * row_number] * latter[4 + column]
                + former[2 * row_number + 1] * latter[2 + column]
                - former[5 + 2 * row_number] * latter[6 + column]
            )
            imag_list.append(
                former[2 * row_number] * latter[4 + column]
                + former[4 + 2 * row_number] * latter[column]
                + former[2 * row_number + 1] * latter[6 + column]
                + former[5 + 2 * row_number] * latter[2 + column]
            )
    return jnp.stack(real_list + imag_list)


def adjoint(matrix):
    return jnp.stack(
        [matrix[0], matrix[2], matrix[1], matrix[3], -matrix[4], -matrix[6], -matrix[5], -matrix[7]]
    )


def source_table(brightness, source_cluster, direction_ids):
    member = (source_cluster[None, :] == direction_ids[:, None]).astype(jnp.float32)
    return (brightness[:, None, :] * member[None, :, :]).reshape(
        4 * direction_ids.shape[0], brightness.shape[1]
    )


def coherency(bright_table, geometry, scales):
    phase_grid = (TWO_PI * scales)[None, :, None] * geometry[:, None, :]
    phases_flat = phase_grid.reshape(geometry.shape[0], -1)
    real_block = jnp.dot(bright_table, jnp.cos(phases_flat), precision=HIGHEST)
    imag_block = -jnp.dot(bright_table, jnp.sin(phases_flat), precision=HIGHEST)
    dir_count = bright_table.shape[0] // 4
    return jnp.concatenate([real_block, imag_block], axis=0).reshape(
        8, dir_count, scales.shape[0], geometry.shape[1]
    )


def per_device(
    visibilities,
    antenna_pairs,
    valid_mask,
    station_positions,
    source_offsets,
    brightness,
    source_cluster,
    jones_gains,
):
    relay_count = lax.axis_size("chan")
    base_count = antenna_pairs.shape[2] // relay_count
    station_count = station_positions.shape[1]
    offset = lax.axis_index("chan") * base_count
    own_pairs = lax.dynamic_slice_in_dim(antenna_pairs[:, 0], offset, base_count, 1)
    first_station = own_pairs[0]
    second_station = own_pairs[1]
    weight_row = lax.dynamic_slice_in_dim(valid_mask[0], offset, base_count, 0).astype(jnp.float32)
    regrouped = lax.all_to_all(visibilities, "chan", split_axis=3, concat_axis=1, tiled=True)[
        :, :, 0, :
    ]
    total_channels = regrouped.shape[1]
    own_directions = jones_gains.shape[0]
    channel_ids = jnp.arange(total_channels)
    gains_now = jones_gains
    direction_ids = lax.axis_index("dir") * own_directions + jnp.arange(own_directions)
    local_channels = regrouped.shape[1]
    scales = 1.0 + 0.5 * channel_ids.astype(jnp.float32) / total_channels
    u_coord = station_positions[0][first_station] - station_positions[0][second_station]
    v_coord = station_positions[1][first_station] - station_positions[1][second_station]
    geometry = (
        source_offsets[0][:, None] * u_coord[None, :]
        + source_offsets[1][:, None] * v_coord[None, :]
    )
    bright_table = source_table(brightness, source_cluster, direction_ids)
    group_size = math.gcd(local_channels, max(1, 2048 // base_count))
    group_count = local_channels // group_size
    scale_groups = scales.reshape(group_count, group_size)
    onehot_first = (first_station[:, None] == jnp.arange(station_count)[None, :]).astype(
        jnp.float32
    )
    onehot_second = (second_station[:, None] == jnp.arange(station_count)[None, :]).astype(
        jnp.float32
    )

    def station_gains(gains_current):
        gain_first = jnp.take(gains_current, first_station, axis=2).transpose(1, 0, 2)[
            :, :, None, :
        ]
        gain_second = jnp.take(gains_current, second_station, axis=2).transpose(1, 0, 2)[
            :, :, None, :
        ]
        return (gain_first, gain_second)

    def residual_of(gains_current):
        gain_first, gain_second = station_gains(gains_current)

        def residual_one_group(scale_group):
            coherent = coherency(bright_table, geometry, scale_group)
            return jnp.sum(
                jones_product(jones_product(gain_first, coherent), adjoint(gain_second)), axis=1
            )

        partial_model = jnp.moveaxis(lax.map(residual_one_group, scale_groups), 0, 1).reshape(
            8, local_channels, base_count
        )
        model_vis = lax.psum(partial_model, "dir")
        return weight_row * (regrouped - model_vis)

    for iteration in range(ITERS):
        residual_now = residual_of(gains_now)
        updated_gain_first, updated_gain_second = station_gains(gains_now)
        resid_groups = jnp.moveaxis(
            residual_now.reshape(8, group_count, group_size, base_count), 1, 0
        )
        dir_count = gains_now.shape[0]

        def updated_one_group(running, inputs):
            scale_group, resid_group = inputs
            coherent = coherency(bright_table, geometry, scale_group)
            toward_second = jones_product(updated_gain_second, adjoint(coherent))
            toward_first = jones_product(updated_gain_first, coherent)
            grad_first = jnp.sum(jones_product(resid_group[:, None], toward_second), axis=2)
            grad_second = jnp.sum(
                jones_product(adjoint(resid_group)[:, None], toward_first), axis=2
            )
            curv_first = jnp.sum(toward_second * toward_second, axis=(0, 2))
            curv_second = jnp.sum(toward_first * toward_first, axis=(0, 2))
            return (
                (
                    running[0] + grad_first,
                    running[1] + grad_second,
                    running[2] + curv_first,
                    running[3] + curv_second,
                ),
                None,
            )

        zero_sums = (
            jnp.zeros((8, dir_count, base_count), jnp.float32),
            jnp.zeros((8, dir_count, base_count), jnp.float32),
            jnp.zeros((dir_count, base_count), jnp.float32),
            jnp.zeros((dir_count, base_count), jnp.float32),
        )
        totals, ignored = lax.scan(updated_one_group, zero_sums, (scale_groups, resid_groups))
        grad_station = jnp.einsum(
            "cdb,bs->dcs", totals[0], onehot_first, precision=HIGHEST
        ) + jnp.einsum("cdb,bs->dcs", totals[1], onehot_second, precision=HIGHEST)
        curv_station = jnp.dot(weight_row * totals[2], onehot_first, precision=HIGHEST) + jnp.dot(
            weight_row * totals[3], onehot_second, precision=HIGHEST
        )
        grad_station, curv_station = lax.psum((grad_station, curv_station), ("chan", "blk"))
        gains_now = gains_now + STEP_SIZE * grad_station / (curv_station[:, None, :] + EPSILON)
    residual_now = residual_of(gains_now)
    return (residual_now[:, :, None, :], gains_now)


COS_TERMS = (
    0.9999999890590228,
    -19.739204499454,
    64.93911745989914,
    -85.45013953093448,
    60.16763095128989,
    -25.96759924954187,
    6.528658162606979,
)
SIN_TERMS = (
    6.283185302511502,
    -41.34170040531754,
    81.6051313857969,
    -76.70301535383193,
    42.02592698564183,
    -14.899846667160109,
    3.2381375090822355,
)
RUN = 128
BLOCK = 64
BLOCKS = 8
PAIR = 2 * RUN


def pieces(value, count):
    result = []
    for index in range(count):
        piece = value.astype(jnp.bfloat16)
        result.append(piece)
        if index < count - 1:
            value = value - piece.astype(jnp.float32)
    return result


def dot_f32(left, right, contract_right=0):
    return lax.dot_general(
        left,
        right,
        (((1,), (contract_right,)), ((), ())),
        preferred_element_type=jnp.float32,
    )


def horner(terms, x):
    total = jnp.full_like(x, terms[-1])
    for term in terms[-2::-1]:
        total = total * x + term
    return total


def turn_pair(turns):
    rest = turns - jnp.round(turns)
    square = rest * rest
    return horner(COS_TERMS, square), horner([-term for term in SIN_TERMS], square) * rest


def product(a, b, dagger_a=False, dagger_b=False, total=None):
    result = [None] * 8 if total is None else list(total)

    def add(n, x, y, positive):
        term = x * y
        if result[n] is None:
            result[n] = term if positive else -term
        else:
            result[n] = result[n] + term if positive else result[n] - term

    for row in (0, 1):
        for col in (0, 1):
            n = 2 * row + col
            for inner in (0, 1):
                i = 2 * inner + row if dagger_a else 2 * row + inner
                j = 2 * col + inner if dagger_b else 2 * inner + col
                add(n, a[i], b[j], True)
                add(n, a[4 + i], b[4 + j], dagger_a != dagger_b)
                if dagger_a:
                    add(4 + n, a[i], b[4 + j], not dagger_b)
                    add(4 + n, a[4 + i], b[j], False)
                else:
                    add(4 + n, a[4 + i], b[j], True)
                    add(4 + n, a[i], b[4 + j], not dagger_b)
    return result


def sum_rows(parts):
    row = lax.broadcasted_iota(jnp.int32, parts[0].shape, 0)
    low = row < 4
    parts = [
        jnp.where(low, a, b) + pltpu.roll(jnp.where(low, b, a), 4, 0)
        for a, b in zip(parts[:4], parts[4:])
    ]
    for step in (2, 1):
        low = jnp.bitwise_and(row, step) == 0
        parts = [
            jnp.where(low, a + pltpu.roll(a, 8 - step, 0), b + pltpu.roll(b, step, 0))
            for a, b in zip(parts[:step], parts[step:])
        ]
    return parts[0]


class Place:
    def __init__(self):
        self.chan = lax.axis_index("chan")
        self.core = lax.axis_index("dir")
        self.blk = lax.axis_index("blk")
        self.first_lane = pl.multiple_of(self.core * PAIR, PAIR)
        self.last_core = self.chan // 2
        self.last_lane = pl.multiple_of(self.chan * RUN, RUN)

    def first_station(self, core):
        return pl.multiple_of((2 * self.blk + core) * RUN, RUN)

    def slot(self, channel, per_shard):
        return jnp.bitwise_xor(channel // per_shard, self.chan) * per_shard + channel % per_shard


def onehot(station, first_station):
    local = jnp.where(station < BLOCK, station, station - first_station + RUN)
    rows = lax.broadcasted_iota(jnp.int32, (2 * RUN, station.shape[1]), 0)
    return jnp.where(rows == local, 1.0, 0.0).astype(jnp.bfloat16)


def split_rows(value, count):
    split = [p.astype(jnp.float32) for p in pieces(value, count)]
    missing = -count * value.shape[0] % 16
    if missing:
        split.append(jnp.zeros((missing, value.shape[1]), jnp.float32))
    return jnp.concatenate(split).astype(jnp.bfloat16)


def grams(coh):
    re, im = coh[:4], coh[4:]
    size = [a * a + b * b for a, b in zip(re, im)]

    def cross(i, j, k, l):
        real = re[i] * re[j] + im[i] * im[j] + re[k] * re[l] + im[k] * im[l]
        imag = re[i] * im[j] - im[i] * re[j] + re[k] * im[l] - im[k] * re[l]
        return [real + real, imag + imag]

    inner = [size[0] + size[2], size[1] + size[3]] + cross(0, 1, 2, 3)
    outer = [size[0] + size[1], size[2] + size[3]] + cross(2, 0, 3, 1)
    return inner + outer


def curvature_of(gain, gram):
    re, im = gain[:4], gain[4:]
    size = [a * a + b * b for a, b in zip(re, im)]
    real = re[0] * re[1] + im[0] * im[1] + re[2] * re[3] + im[2] * im[3]
    imag = im[0] * re[1] - re[0] * im[1] + im[2] * re[3] - re[2] * im[3]
    total = (size[0] + size[2]) * gram[0] + (size[1] + size[3]) * gram[1] + real * gram[2] - imag * gram[3]
    return jnp.maximum(total, 0.0)


def coherency_kernel(
    channels, pairs_at, positions_at, offsets_at, brightness_at, cluster_at, mask_at, seen_at, own_at, other,
    out, share, gram, hots, last_hots, mask, seen, jones, gather, predicted,
    pairs, positions, offsets, brightness, cluster, own, base, spin, parts, model, sems,
):
    copies = [
        pltpu.make_async_copy(source, target, sems.at[index])
        for index, (source, target) in enumerate(
            (
                (pairs_at, pairs),
                (positions_at, positions),
                (offsets_at, offsets),
                (brightness_at, brightness),
                (cluster_at, cluster),
                (mask_at, mask),
                (seen_at, seen),
                (own_at, own),
            )
        )
    ]
    for copy in copies:
        copy.start()
    for copy in copies[:5]:
        copy.wait()
    place = Place()
    window = place.first_station(place.core)
    table = jnp.concatenate([positions[:, 0:RUN], positions[:, pl.ds(window, RUN)]], axis=1)
    table = split_rows(table, 3)
    there = []
    for side in (0, 1):
        hots[side] = onehot(pairs[side, :, pl.ds(place.first_lane, PAIR)], window)
        last = pairs[side, :, pl.ds(place.last_lane, RUN)]
        last_hots[side] = onehot(last, place.first_station(place.last_core))
        found = dot_f32(table, hots[side])
        there.append(found[0:2] + found[2:4] + found[4:6])
    span = there[0] - there[1]
    sources = offsets.shape[1]
    columns = jnp.transpose(jnp.concatenate([offsets[...], jnp.zeros((6, sources))]))
    step = 16
    for start in range(0, sources, step):
        rows = slice(start, start + step)
        geometry = columns[rows, 0:1] * span[0:1] + columns[rows, 1:2] * span[1:2]
        base[0, rows], base[1, rows] = turn_pair(geometry)
        spin[0, rows], spin[1, rows] = turn_pair(geometry * (0.5 / channels))

    directions = out.shape[1] // 12
    second_run = lax.rem(place.chan, 2) == 1
    member = lax.broadcasted_iota(jnp.int32, (directions, sources), 0) == cluster[...]
    bright = jnp.concatenate([jnp.where(member, brightness[n : n + 1], 0.0) for n in range(4)])
    high, low = pieces(bright, 2)
    both = jnp.concatenate([high, low])
    half = 4 * directions

    def table_times(refs):
        wide = dot_f32(both, refs[0])
        return wide[:half] + wide[half:] + dot_f32(high, refs[1])

    for channel in range(channels):
        odd = channel % 2
        for start in range(0, sources, step):
            rows = slice(start, start + step)
            c, s = base[0, rows], base[1, rows]
            for index, value in enumerate((c, s)):
                for size, piece in enumerate(pieces(value, 2)):
                    parts[odd, index, size, rows] = piece
            if channel < channels - 1:
                dc, ds = spin[0, rows], spin[1, rows]
                base[0, rows] = c * dc - s * ds
                base[1, rows] = s * dc + c * ds
        found = [table_times((parts[odd, index, 0], parts[odd, index, 1])) for index in (0, 1)]
        out[channel, :half] = found[0]
        out[channel, half : 2 * half] = found[1]
        out[channel, 2 * half :] = found[0] - found[1]
        for index in (0, 1):
            mine = jnp.where(second_run, found[index][:, RUN:], found[index][:, :RUN])
            share[channel, half * index : half * (index + 1)] = mine
        entries = [found[n // 4][n % 4 * directions : (n % 4 + 1) * directions] for n in range(8)]
        for n, value in enumerate(grams(entries)):
            rows = slice(n * directions, (n + 1) * directions)
            gram[rows] = value if channel == 0 else gram[rows] + value
    for copy in copies[5:]:
        copy.wait()
    fill_table(place, jones, own, other)
    gather_gains(jones[...], hots, gather)
    for run in range(2):
        predict(out, gather, run, model, predicted)


def gather_gains(table, hots, gather):
    rows = table.shape[0]
    split = jnp.concatenate(pieces(table, 2))
    for side in (0, 1):
        found = dot_f32(split, hots[side])
        found = found[:rows] + found[rows:]
        for run in range(found.shape[1] // RUN):
            gather[side, run] = found[:, run * RUN : (run + 1) * RUN]


def gains_of(gather, side, run, h):
    return [gather[side, run, pl.ds(64 * h + n, 8, stride=8), :] for n in range(8)]


def coherent_of(coherent, channel, h, lanes, directions, count):
    return [
        coherent[channel, n * directions + 8 * h : n * directions + 8 * h + 8, lanes] for n in range(count)
    ]


def small_product(a, b, turned=False):
    order = ((0, 1), (2, 3)) if turned else ((0, 2), (1, 3))
    return [
        a[2 * row] * b[order[col][0]] + a[2 * row + 1] * b[order[col][1]] for row in (0, 1) for col in (0, 1)
    ]


def less(a, b):
    return [x - y for x, y in zip(a, b)]


def plus(a, b):
    return [x + y for x, y in zip(a, b)]


def model_parts(first, second, coh):
    re, im, mixed = coh[:4], coh[4:8], coh[8:]
    p1 = small_product(first[:4], re)
    p2 = small_product(first[4:8], im)
    p3 = small_product(first[8:], mixed)
    zr = less(p1, p2)
    zi = less(plus(p1, p2), p3)
    return (
        small_product(zr, second[:4], True)
        + small_product(zi, second[4:8], True)
        + small_product(plus(zr, zi), second[8:], True)
    )


def model_of(parts):
    a, b, d = parts[:4], parts[4:8], parts[8:]
    return plus(a, b) + plus(less(d, a), b)


def with_difference(matrix):
    return matrix + less(matrix[:4], matrix[4:])


def multiply_into(total, a, b, conj_b=False):
    real = a[0] * b[0]
    imag = a[1] * b[0]
    if total is not None:
        real, imag = total[0] + real, total[1] + imag
    if conj_b:
        return real + a[1] * b[1], imag - a[0] * b[1]
    return real - a[1] * b[1], imag + a[0] * b[1]


def fill_table(place, jones, own, other):
    count = own.shape[0] * own.shape[1]
    for ref, core in ((own, place.core), (other, 1 - place.core)):
        at = pl.ds(pl.multiple_of(core * count, count), count)
        jones[at, 0:RUN] = ref[:, :, 0:RUN].reshape(count, RUN)
        window = ref[:, :, pl.ds(place.first_station(place.core), RUN)]
        jones[at, RUN:] = window.reshape(count, RUN)


def predict(coherent, gather, run, model, predicted):
    channels = coherent.shape[0]
    directions = coherent.shape[1] // 12
    halves = directions // 8
    lanes = slice(run * RUN, (run + 1) * RUN)
    for h in range(halves):
        first_gain = with_difference(gains_of(gather, 0, run, h))
        second_gain = with_difference(gains_of(gather, 1, run, h))
        for channel in range(channels):
            coh = coherent_of(coherent, channel, h, lanes, directions, 12)
            part = model_parts(first_gain, second_gain, coh)
            if h > 0:
                part = [a + model[channel, n] for n, a in enumerate(part)]
            if h < halves - 1:
                for n in range(12):
                    model[channel, n] = part[n]
            else:
                predicted[run, channel] = sum_rows(model_of(part))


def iterate(place, coherent, gram, hots, shards, mask, gather, predicted, error, sums):
    directions = coherent.shape[1] // 12
    rows = 8 * directions
    halves = rows // 64
    weight = mask[:, pl.ds(place.first_lane, PAIR)].astype(jnp.float32)
    channels = coherent.shape[0]
    per_shard = shards[0].shape[1]
    for run in range(2):
        lanes = slice(run * RUN, (run + 1) * RUN)
        w = weight[:, lanes]
        at = pl.multiple_of(place.first_lane + run * RUN, RUN)
        for slot in range(channels):
            channel = place.slot(slot, per_shard)
            seen = shards[slot // per_shard][:, slot % per_shard, 0, pl.ds(at, RUN)]
            err = w * (seen - predicted[run, channel])
            error[channel, 0] = err
            error[channel, 1] = err + pltpu.roll(err, 4, 0)

        for h in range(halves):
            first_gain, second_gain = gains_of(gather, 0, run, h), gains_of(gather, 1, run, h)
            second = [None] * 4
            for i in (0, 1):
                zero = jnp.zeros((8, RUN), jnp.float32)
                p1, p2, p3 = [zero] * 8, [zero] * 8, [zero] * 8
                for channel in range(channels):
                    coh = coherent_of(coherent, channel, h, lanes, directions, 12)

                    def err(tile, n):
                        return jnp.broadcast_to(error[channel, tile, n : n + 1], (8, RUN))

                    for j in (0, 1):
                        er, ei, es = err(0, 2 * i + j), err(0, 4 + 2 * i + j), err(1, 2 * i + j)
                        for kl in range(4):
                            n = 4 * j + kl
                            p1[n] = p1[n] + er * coh[kl]
                            p2[n] = p2[n] + ei * coh[4 + kl]
                            p3[n] = p3[n] + es * coh[8 + kl]
                outer = list(zip(plus(p1, p2), plus(less(p3, p1), p2)))
                for l in (0, 1):
                    total = None
                    for j in (0, 1):
                        for k in (0, 1):
                            g = (second_gain[2 * j + k], second_gain[4 + 2 * j + k])
                            total = multiply_into(total, outer[4 * j + 2 * l + k], g)
                    for imag in (0, 1):
                        n = 4 * imag + 2 * i + l
                        sums[0, run, pl.ds(64 * h + n, 8, stride=8), :] = total[imag]
                for a in (0, 1):
                    for l in (0, 1):
                        for k in (0, 1):
                            g = (first_gain[2 * i + k], first_gain[4 + 2 * i + k])
                            second[2 * a + l] = multiply_into(
                                second[2 * a + l], g, outer[4 * a + 2 * k + l], conj_b=True
                            )
            for n in range(8):
                sums[1, run, pl.ds(64 * h + n, 8, stride=8), :] = second[n % 4][n // 4]
            form = [gram[n * directions + 8 * h : n * directions + 8 * h + 8, lanes] for n in range(8)]
            sums[0, run, rows + 8 * h : rows + 8 * h + 8] = w * curvature_of(second_gain, form[:4])
            sums[1, run, rows + 8 * h : rows + 8 * h + 8] = w * curvature_of(first_gain, form[4:])

    total = None
    height = sums.shape[2]
    for side in (0, 1):
        whole = jnp.concatenate([sums[side, run] for run in range(2)], axis=1)
        found = dot_f32(jnp.concatenate(pieces(whole, 2)), hots[side], 1)
        found = found[:height] + found[height:]
        total = found if total is None else total + found
    return total


def pack(total, rows):
    half = rows // 2
    low = jnp.concatenate([total[:half], total[rows : rows + half // 8]])
    high = jnp.concatenate([total[half:rows], total[rows + half // 8 :]])
    lane = lax.broadcasted_iota(jnp.int32, low.shape, 1)
    return jnp.where(lane < BLOCK, low, pltpu.roll(high, BLOCK, 1))


def unpack(packed):
    half = packed.shape[0] * 8 // 9
    turned = pltpu.roll(packed, BLOCK, 1)
    return jnp.concatenate([packed[:half], turned[:half], packed[half:], turned[half:]])


def update(jones, lanes, sums, keep=None):
    rows = jones.shape[0]
    for d in range(rows // 8):
        now = jones[8 * d : 8 * d + 8, lanes]
        ratio = STEP_SIZE / (sums[rows + d : rows + d + 1] + EPSILON)
        new = now + ratio * sums[8 * d : 8 * d + 8]
        if keep is not None:
            new = jnp.where(keep, new, now)
        jones[8 * d : 8 * d + 8, lanes] = new


def block_zero():
    return lax.broadcasted_iota(jnp.int32, (8, RUN), 1) < BLOCK


def first_kernel(
    mask, coherent, gram, hots, gather, predicted, s0, s1, s2, s3, packed, mine, error, sums
):
    place = Place()
    total = iterate(place, coherent, gram, hots, (s0, s1, s2, s3), mask, gather, predicted, error, sums)
    packed[...] = pack(total[:, :RUN], 8 * (coherent.shape[1] // 12))
    mine[...] = total[:, RUN:]


def block_sums(refs, held):
    here, over_core, over_blk, over_both = [ref[:held] for ref in refs]
    return unpack((here + over_core) + (over_blk + over_both))


def second_kernel(
    mask, coherent, gram, hots, before, mine, p0, p1, p2, p3, s0, s1, s2, s3,
    to_core, to_blk, to_both, jones, model, error, gather, predicted, sums,
):
    place = Place()
    held = p0.shape[0]
    jones[...] = before[...]
    update(jones, slice(0, RUN), block_sums((p0, p1, p2, p3), held), block_zero())
    update(jones, slice(RUN, None), mine[...])
    gather_gains(jones[...], hots, gather)
    for run in range(2):
        predict(coherent, gather, run, model, predicted)
    total = iterate(place, coherent, gram, hots, (s0, s1, s2, s3), mask, gather, predicted, error, sums)
    rows = jones.shape[0]
    half = rows // 2
    packed = pack(total[:, :RUN], rows)
    update(jones, slice(RUN, None), total[:, RUN:])
    to_core[:held] = packed
    to_blk[:held] = packed
    to_both[:held] = packed
    to_core[held:] = jones[:, RUN:]
    to_blk[held:] = jones[pl.ds(pl.multiple_of(place.core * half, half), half), RUN:]
    to_both[held:] = jones[pl.ds(pl.multiple_of((1 - place.core) * half, half), half), RUN:]


def last_kernel(
    mask, share, other_share, hots, before, p0, p1, p2, p3, s0, s1, s2, s3,
    residual, solved_at, jones, gather, solved, sem,
):
    place = Place()
    rows = before.shape[0]
    half = rows // 2
    held = p0.shape[0] - rows
    owned = place.last_core == place.core
    jones[:, 0:RUN] = before[:, 0:RUN]
    jones[:, RUN:] = jnp.where(owned, p0[held:], p1[held:])
    update(jones, slice(0, RUN), block_sums((p0, p1, p2, p3), held), block_zero())

    own_rows = pl.multiple_of(place.core * half, half)
    for ref, start, blk, core in (
        (p0, held + own_rows, place.blk, place.core),
        (p1, held + own_rows, place.blk, 1 - place.core),
        (p2, held, 1 - place.blk, place.core),
        (p3, held, 1 - place.blk, 1 - place.core),
    ):
        lanes = pl.ds(pl.multiple_of((2 * blk + core) * RUN, RUN), RUN)
        solved[:, :, lanes] = ref[pl.ds(pl.multiple_of(start, 8), half)].reshape(half // 8, 8, RUN)
    zero = jones[pl.ds(own_rows, half), 0:RUN].reshape(half // 8, 8, RUN)
    lane = lax.broadcasted_iota(jnp.int32, zero.shape, 2)
    solved[:, :, 0:RUN] = jnp.where(lane < BLOCK, zero, solved[:, :, 0:RUN])
    copy = pltpu.make_async_copy(solved, solved_at, sem)
    copy.start()

    gather_gains(jones[...], hots, gather)
    w = mask[:, pl.ds(place.last_lane, RUN)].astype(jnp.float32)
    shards = (s0, s1, s2, s3)
    channels = share.shape[0]
    per_shard = s0.shape[1]
    gains = [[gains_of(gather, side, 0, h) for h in range(rows // 64)] for side in (0, 1)]
    for slot in range(channels):
        channel = place.slot(slot, per_shard)
        part = None
        for h in range(rows // 64):
            coh = [
                jnp.where(owned, a, b)
                for a, b in zip(
                    coherent_of(share, channel, h, slice(0, RUN), rows // 8, 8),
                    coherent_of(other_share, channel, h, slice(0, RUN), rows // 8, 8),
                )
            ]
            part = product(product(gains[0][h], coh), gains[1][h], dagger_b=True, total=part)
        seen = shards[slot // per_shard][:, slot % per_shard, 0, pl.ds(place.last_lane, RUN)]
        residual[:, channel, 0] = w * (seen - sum_rows(part))
    copy.wait()


def call(kernel, out_shape, scratch, operands, flops, in_hbm=0, out_spaces=None):
    spaces = [pltpu.HBM] * in_hbm + [pltpu.VMEM] * (len(operands) - in_hbm)
    return pl.pallas_call(
        kernel,
        out_shape=out_shape,
        in_specs=[pl.BlockSpec(memory_space=space) for space in spaces],
        out_specs=tuple(
            pl.BlockSpec(memory_space=space) for space in out_spaces or [pltpu.VMEM] * len(out_shape)
        ),
        scratch_shapes=scratch,
        compiler_params=pltpu.CompilerParams(vmem_limit_bytes=40 << 20),
        cost_estimate=pl.CostEstimate(
            flops=flops,
            transcendentals=0,
            bytes_accessed=sum(x.size * x.dtype.itemsize for x in [*operands, *out_shape]),
        ),
    )(*[pltpu.with_memory_space_constraint(x, space) for x, space in zip(operands, spaces)])


def f32(*shape):
    return jax.ShapeDtypeStruct(shape, jnp.float32)


def bf16(*shape):
    return jax.ShapeDtypeStruct(shape, jnp.bfloat16)


def swap(x, axis, bit=1):
    return lax.ppermute(x, axis, [(i, i ^ bit) for i in range(lax.axis_size(axis))])


def from_three(core, blk, both):
    return swap(core, "dir"), swap(blk, "blk"), swap(both, ("blk", "dir"), 3)


def per_device_owned(
    visibilities,
    antenna_pairs,
    valid_mask,
    station_positions,
    source_offsets,
    brightness,
    source_cluster,
    jones_gains,
):
    relay_count = lax.axis_size("chan")
    channels = visibilities.shape[1] * relay_count
    half_directions = jones_gains.shape[0]
    directions = 2 * half_directions
    rows = 8 * directions
    sources = source_offsets.shape[1]

    other = swap(jones_gains, "dir")
    shards = [swap(visibilities, "chan", bit) for bit in range(1, relay_count)]
    inputs = (antenna_pairs, station_positions, source_offsets, brightness, source_cluster[None, :])
    kept = (valid_mask, visibilities)
    held = (rows + directions) // 2
    table = f32(rows, 2 * RUN)
    gathered = f32(2, 2, rows, RUN)
    predictions = f32(2, channels, 8, RUN)
    model = pltpu.VMEM((channels, 12, 8, RUN), jnp.float32)
    scratch = [
        pltpu.VMEM((channels, 2, 8, RUN), jnp.float32),
        pltpu.VMEM((2, 2, rows + directions, RUN), jnp.float32),
    ]
    coherent, share, gram, hots, last_hots, mask, seen, jones, gather, predicted = call(
        functools.partial(coherency_kernel, channels),
        (
            f32(channels, 12 * directions, PAIR),
            f32(channels, 8 * directions, RUN),
            f32(8 * directions, PAIR),
            bf16(2, 2 * RUN, PAIR),
            bf16(2, 2 * RUN, RUN),
            *[jax.ShapeDtypeStruct(x.shape, x.dtype) for x in kept],
            table,
            gathered,
            predictions,
        ),
        [pltpu.VMEM(x.shape, x.dtype) for x in inputs + (jones_gains,)]
        + [
            pltpu.VMEM((2, sources, PAIR), jnp.float32),
            pltpu.VMEM((2, sources, PAIR), jnp.float32),
            pltpu.VMEM((2, 2, 2, sources, PAIR), jnp.bfloat16),
            model,
            pltpu.SemaphoreType.DMA((len(inputs + kept) + 1,)),
        ],
        inputs + kept + (jones_gains, other),
        4 * 10**9,
        len(inputs + kept) + 1,
    )
    shards = [seen] + shards
    packed, mine = call(
        first_kernel,
        (f32(held, RUN), f32(rows + directions, RUN)),
        scratch,
        (mask, coherent, gram, hots, gather, predicted, *shards),
        10**9,
    )
    sums = from_three(packed, packed, packed)
    *sums, share = lax.optimization_barrier((*sums, share))
    other_share = swap(share, "dir")
    to_core, to_blk, to_both, jones = call(
        second_kernel,
        (f32(held + rows, RUN), f32(held + rows // 2, RUN), f32(held + rows // 2, RUN), table),
        [
            model,
            scratch[0],
            pltpu.VMEM(gathered.shape, jnp.float32),
            pltpu.VMEM(predictions.shape, jnp.float32),
            scratch[1],
        ],
        (mask, coherent, gram, hots, jones, mine, packed, *sums, *shards),
        2 * 10**9,
    )
    solved = f32(half_directions, 8, station_positions.shape[1])
    return call(
        last_kernel,
        (f32(8, channels, 1, RUN), solved),
        [
            pltpu.VMEM((rows, 2 * RUN), jnp.float32),
            pltpu.VMEM((2, 1, rows, RUN), jnp.float32),
            pltpu.VMEM(solved.shape, jnp.float32),
            pltpu.SemaphoreType.DMA,
        ],
        (
            mask, share, other_share, last_hots, jones,
            to_core, *from_three(to_core, to_blk, to_both), *shards,
        ),
        10**9,
        0,
        (pltpu.VMEM, pltpu.HBM),
    )


def owned_layout(mesh, shapes):
    sizes = mesh.shape
    owners = sizes["chan"] * sizes["blk"]
    visibilities, pairs, jones = shapes
    return (
        owners == BLOCKS
        and sizes["blk"] == 2
        and sizes["dir"] == 2
        and sizes["chan"] == 4
        and pairs[1] * pairs[2] == owners * RUN
        and jones[0] == 16
        and jones[2] == BLOCKS * BLOCK
        and visibilities[1] % sizes["chan"] == 0
    )


def solution(mesh):
    in_specs = (
        P("groups", "chan", "blk", None),
        P(None, "blk", None),
        P("blk", "groups"),
        P(),
        P(),
        P(),
        P(),
        P("dir", "groups", None),
    )
    out_specs = (P("groups", None, "blk", "chan"), P("dir", "groups", None))

    def run(*arrays):
        owned = owned_layout(mesh, (arrays[0].shape, arrays[1].shape, arrays[7].shape))
        body = per_device_owned if owned else per_device
        return jax.shard_map(
            body, mesh=mesh, in_specs=in_specs, out_specs=out_specs, check_vma=False
        )(*arrays)

    return run
```

```python
import functools
import math

import jax
import jax.numpy as jnp
from jax import lax
from jax.experimental import pallas as pl
from jax.experimental.pallas import tpu as pltpu
from jax.sharding import PartitionSpec as P

ITERS = 2


TWO_PI = 2.0 * math.pi
STEP_SIZE = 0.3
EPSILON = 1e-06
HIGHEST = lax.Precision.HIGHEST


def jones_product(former, latter):
    real_list = []
    imag_list = []
    for row_number in (0, 1):
        for column in (0, 1):
            real_list.append(
                former[2 * row_number] * latter[column]
                - former[4 + 2 * row_number] * latter[4 + column]
                + former[2 * row_number + 1] * latter[2 + column]
                - former[5 + 2 * row_number] * latter[6 + column]
            )
            imag_list.append(
                former[2 * row_number] * latter[4 + column]
                + former[4 + 2 * row_number] * latter[column]
                + former[2 * row_number + 1] * latter[6 + column]
                + former[5 + 2 * row_number] * latter[2 + column]
            )
    return jnp.stack(real_list + imag_list)


def adjoint(matrix):
    return jnp.stack(
        [matrix[0], matrix[2], matrix[1], matrix[3], -matrix[4], -matrix[6], -matrix[5], -matrix[7]]
    )


def source_table(brightness, source_cluster, direction_ids):
    member = (source_cluster[None, :] == direction_ids[:, None]).astype(jnp.float32)
    return (brightness[:, None, :] * member[None, :, :]).reshape(
        4 * direction_ids.shape[0], brightness.shape[1]
    )


def coherency(bright_table, geometry, scales):
    phase_grid = (TWO_PI * scales)[None, :, None] * geometry[:, None, :]
    phases_flat = phase_grid.reshape(geometry.shape[0], -1)
    real_block = jnp.dot(bright_table, jnp.cos(phases_flat), precision=HIGHEST)
    imag_block = -jnp.dot(bright_table, jnp.sin(phases_flat), precision=HIGHEST)
    dir_count = bright_table.shape[0] // 4
    return jnp.concatenate([real_block, imag_block], axis=0).reshape(
        8, dir_count, scales.shape[0], geometry.shape[1]
    )


def per_device(
    visibilities,
    antenna_pairs,
    valid_mask,
    station_positions,
    source_offsets,
    brightness,
    source_cluster,
    jones_gains,
):
    relay_count = lax.axis_size("chan")
    base_count = antenna_pairs.shape[2] // relay_count
    station_count = station_positions.shape[1]
    offset = lax.axis_index("chan") * base_count
    own_pairs = lax.dynamic_slice_in_dim(antenna_pairs[:, 0], offset, base_count, 1)
    first_station = own_pairs[0]
    second_station = own_pairs[1]
    weight_row = lax.dynamic_slice_in_dim(valid_mask[0], offset, base_count, 0).astype(jnp.float32)
    regrouped = lax.all_to_all(visibilities, "chan", split_axis=3, concat_axis=1, tiled=True)[
        :, :, 0, :
    ]
    total_channels = regrouped.shape[1]
    own_directions = jones_gains.shape[0]
    channel_ids = jnp.arange(total_channels)
    gains_now = jones_gains
    direction_ids = lax.axis_index("dir") * own_directions + jnp.arange(own_directions)
    local_channels = regrouped.shape[1]
    scales = 1.0 + 0.5 * channel_ids.astype(jnp.float32) / total_channels
    u_coord = station_positions[0][first_station] - station_positions[0][second_station]
    v_coord = station_positions[1][first_station] - station_positions[1][second_station]
    geometry = (
        source_offsets[0][:, None] * u_coord[None, :]
        + source_offsets[1][:, None] * v_coord[None, :]
    )
    bright_table = source_table(brightness, source_cluster, direction_ids)
    group_size = math.gcd(local_channels, max(1, 2048 // base_count))
    group_count = local_channels // group_size
    scale_groups = scales.reshape(group_count, group_size)
    onehot_first = (first_station[:, None] == jnp.arange(station_count)[None, :]).astype(
        jnp.float32
    )
    onehot_second = (second_station[:, None] == jnp.arange(station_count)[None, :]).astype(
        jnp.float32
    )

    def station_gains(gains_current):
        gain_first = jnp.take(gains_current, first_station, axis=2).transpose(1, 0, 2)[
            :, :, None, :
        ]
        gain_second = jnp.take(gains_current, second_station, axis=2).transpose(1, 0, 2)[
            :, :, None, :
        ]
        return (gain_first, gain_second)

    def residual_of(gains_current):
        gain_first, gain_second = station_gains(gains_current)

        def residual_one_group(scale_group):
            coherent = coherency(bright_table, geometry, scale_group)
            return jnp.sum(
                jones_product(jones_product(gain_first, coherent), adjoint(gain_second)), axis=1
            )

        partial_model = jnp.moveaxis(lax.map(residual_one_group, scale_groups), 0, 1).reshape(
            8, local_channels, base_count
        )
        model_vis = lax.psum(partial_model, "dir")
        return weight_row * (regrouped - model_vis)

    for iteration in range(ITERS):
        residual_now = residual_of(gains_now)
        updated_gain_first, updated_gain_second = station_gains(gains_now)
        resid_groups = jnp.moveaxis(
            residual_now.reshape(8, group_count, group_size, base_count), 1, 0
        )
        dir_count = gains_now.shape[0]

        def updated_one_group(running, inputs):
            scale_group, resid_group = inputs
            coherent = coherency(bright_table, geometry, scale_group)
            toward_second = jones_product(updated_gain_second, adjoint(coherent))
            toward_first = jones_product(updated_gain_first, coherent)
            grad_first = jnp.sum(jones_product(resid_group[:, None], toward_second), axis=2)
            grad_second = jnp.sum(
                jones_product(adjoint(resid_group)[:, None], toward_first), axis=2
            )
            curv_first = jnp.sum(toward_second * toward_second, axis=(0, 2))
            curv_second = jnp.sum(toward_first * toward_first, axis=(0, 2))
            return (
                (
                    running[0] + grad_first,
                    running[1] + grad_second,
                    running[2] + curv_first,
                    running[3] + curv_second,
                ),
                None,
            )

        zero_sums = (
            jnp.zeros((8, dir_count, base_count), jnp.float32),
            jnp.zeros((8, dir_count, base_count), jnp.float32),
            jnp.zeros((dir_count, base_count), jnp.float32),
            jnp.zeros((dir_count, base_count), jnp.float32),
        )
        totals, ignored = lax.scan(updated_one_group, zero_sums, (scale_groups, resid_groups))
        grad_station = jnp.einsum(
            "cdb,bs->dcs", totals[0], onehot_first, precision=HIGHEST
        ) + jnp.einsum("cdb,bs->dcs", totals[1], onehot_second, precision=HIGHEST)
        curv_station = jnp.dot(weight_row * totals[2], onehot_first, precision=HIGHEST) + jnp.dot(
            weight_row * totals[3], onehot_second, precision=HIGHEST
        )
        grad_station, curv_station = lax.psum((grad_station, curv_station), ("chan", "blk"))
        gains_now = gains_now + STEP_SIZE * grad_station / (curv_station[:, None, :] + EPSILON)
    residual_now = residual_of(gains_now)
    return (residual_now[:, :, None, :], gains_now)


COS_TERMS = (
    0.9999999890590228,
    -19.739204499454,
    64.93911745989914,
    -85.45013953093448,
    60.16763095128989,
    -25.96759924954187,
    6.528658162606979,
)
SIN_TERMS = (
    6.283185302511502,
    -41.34170040531754,
    81.6051313857969,
    -76.70301535383193,
    42.02592698564183,
    -14.899846667160109,
    3.2381375090822355,
)
RUN = 128
BLOCK = 64
BLOCKS = 8
PAIR = 2 * RUN


def pieces(value, count):
    result = []
    for index in range(count):
        piece = value.astype(jnp.bfloat16)
        result.append(piece)
        if index < count - 1:
            value = value - piece.astype(jnp.float32)
    return result


def dot_f32(left, right, contract_right=0):
    return lax.dot_general(
        left,
        right,
        (((1,), (contract_right,)), ((), ())),
        preferred_element_type=jnp.float32,
    )


def horner(terms, x):
    total = jnp.full_like(x, terms[-1])
    for term in terms[-2::-1]:
        total = total * x + term
    return total


def turn_pair(turns):
    rest = turns - jnp.round(turns)
    square = rest * rest
    return horner(COS_TERMS, square), horner([-term for term in SIN_TERMS], square) * rest


def product(a, b, dagger_a=False, dagger_b=False, total=None):
    result = [None] * 8 if total is None else list(total)

    def add(n, x, y, positive):
        term = x * y
        if result[n] is None:
            result[n] = term if positive else -term
        else:
            result[n] = result[n] + term if positive else result[n] - term

    for row in (0, 1):
        for col in (0, 1):
            n = 2 * row + col
            for inner in (0, 1):
                i = 2 * inner + row if dagger_a else 2 * row + inner
                j = 2 * col + inner if dagger_b else 2 * inner + col
                add(n, a[i], b[j], True)
                add(n, a[4 + i], b[4 + j], dagger_a != dagger_b)
                if dagger_a:
                    add(4 + n, a[i], b[4 + j], not dagger_b)
                    add(4 + n, a[4 + i], b[j], False)
                else:
                    add(4 + n, a[4 + i], b[j], True)
                    add(4 + n, a[i], b[4 + j], not dagger_b)
    return result


def sum_rows(parts):
    row = lax.broadcasted_iota(jnp.int32, parts[0].shape, 0)
    low = row < 4
    parts = [
        jnp.where(low, a, b) + pltpu.roll(jnp.where(low, b, a), 4, 0)
        for a, b in zip(parts[:4], parts[4:])
    ]
    for step in (2, 1):
        low = jnp.bitwise_and(row, step) == 0
        parts = [
            jnp.where(low, a + pltpu.roll(a, 8 - step, 0), b + pltpu.roll(b, step, 0))
            for a, b in zip(parts[:step], parts[step:])
        ]
    return parts[0]


class Place:
    def __init__(self):
        self.chan = lax.axis_index("chan")
        self.core = lax.axis_index("dir")
        self.blk = lax.axis_index("blk")
        self.first_lane = pl.multiple_of(self.core * PAIR, PAIR)
        self.last_core = self.chan // 2
        self.last_lane = pl.multiple_of(self.chan * RUN, RUN)

    def first_station(self, core):
        return pl.multiple_of((2 * self.blk + core) * RUN, RUN)

    def channel_of(self, slot, per_shard):
        bits = (0, 1 + 2 * self.core, 2, 3 - 2 * self.core)[slot // per_shard]
        return jnp.bitwise_xor(bits, self.chan) * per_shard + slot % per_shard


def onehot(station, first_station):
    local = jnp.where(station < BLOCK, station, station - first_station + RUN)
    rows = lax.broadcasted_iota(jnp.int32, (2 * RUN, station.shape[1]), 0)
    return jnp.where(rows == local, 1.0, 0.0).astype(jnp.bfloat16)


def split_rows(value, count):
    split = [p.astype(jnp.float32) for p in pieces(value, count)]
    missing = -count * value.shape[0] % 16
    if missing:
        split.append(jnp.zeros((missing, value.shape[1]), jnp.float32))
    return jnp.concatenate(split).astype(jnp.bfloat16)


def grams(coh):
    re, im = coh[:4], coh[4:]
    size = [a * a + b * b for a, b in zip(re, im)]

    def cross(i, j, k, l):
        real = re[i] * re[j] + im[i] * im[j] + re[k] * re[l] + im[k] * im[l]
        imag = re[i] * im[j] - im[i] * re[j] + re[k] * im[l] - im[k] * re[l]
        return [real + real, imag + imag]

    inner = [size[0] + size[2], size[1] + size[3]] + cross(0, 1, 2, 3)
    outer = [size[0] + size[1], size[2] + size[3]] + cross(2, 0, 3, 1)
    return inner + outer


def curvature_of(gain, gram):
    re, im = gain[:4], gain[4:]
    size = [a * a + b * b for a, b in zip(re, im)]
    real = re[0] * re[1] + im[0] * im[1] + re[2] * re[3] + im[2] * im[3]
    imag = im[0] * re[1] - re[0] * im[1] + im[2] * re[3] - re[2] * im[3]
    total = (size[0] + size[2]) * gram[0] + (size[1] + size[3]) * gram[1] + real * gram[2] - imag * gram[3]
    return jnp.maximum(total, 0.0)


def coherency_kernel(
    channels, pairs_at, positions_at, offsets_at, brightness_at, cluster_at, mask_at, seen_at, own_at,
    out, gram, hots, last_hots, mask, seen, own,
    pairs, positions, offsets, brightness, cluster, base, spin, parts, sems,
):
    copies = [
        pltpu.make_async_copy(source, target, sems.at[index])
        for index, (source, target) in enumerate(
            (
                (pairs_at, pairs),
                (positions_at, positions),
                (offsets_at, offsets),
                (brightness_at, brightness),
                (cluster_at, cluster),
                (mask_at, mask),
                (seen_at, seen),
                (own_at, own),
            )
        )
    ]
    for copy in copies:
        copy.start()
    for copy in copies[:5]:
        copy.wait()
    place = Place()
    window = place.first_station(place.core)
    table = jnp.concatenate([positions[:, 0:RUN], positions[:, pl.ds(window, RUN)]], axis=1)
    table = split_rows(table, 3)
    there = []
    for side in (0, 1):
        hots[side] = onehot(pairs[side, :, pl.ds(place.first_lane, PAIR)], window)
        last = pairs[side, :, pl.ds(place.last_lane, RUN)]
        last_hots[side] = onehot(last, place.first_station(place.last_core))
        found = dot_f32(table, hots[side])
        there.append(found[0:2] + found[2:4] + found[4:6])
    span = there[0] - there[1]
    sources = offsets.shape[1]
    columns = jnp.transpose(jnp.concatenate([offsets[...], jnp.zeros((6, sources))]))
    step = 16
    for start in range(0, sources, step):
        rows = slice(start, start + step)
        geometry = columns[rows, 0:1] * span[0:1] + columns[rows, 1:2] * span[1:2]
        c, s = turn_pair(geometry * (0.5 / channels))
        spin[0, rows], spin[1, rows] = c, s
        for _ in range((2 * channels).bit_length() - 1):
            twice = s + s
            c, s = 1.0 - twice * s, twice * c
        base[0, rows], base[1, rows] = c, s

    directions = out.shape[1] // 12
    member = lax.broadcasted_iota(jnp.int32, (directions, sources), 0) == cluster[...]
    bright = jnp.concatenate([jnp.where(member, brightness[n : n + 1], 0.0) for n in range(4)])
    high, low = pieces(bright, 2)
    both = jnp.concatenate([high, low])
    half = 4 * directions

    def table_times(refs):
        wide = dot_f32(both, refs[0])
        return wide[:half] + wide[half:] + dot_f32(high, refs[1])

    for channel in range(channels):
        odd = channel % 2
        for start in range(0, sources, step):
            rows = slice(start, start + step)
            c, s = base[0, rows], base[1, rows]
            for index, value in enumerate((c, s)):
                for size, piece in enumerate(pieces(value, 2)):
                    parts[odd, index, size, rows] = piece
            if channel < channels - 1:
                dc, ds = spin[0, rows], spin[1, rows]
                base[0, rows] = c * dc - s * ds
                base[1, rows] = s * dc + c * ds
        found = [table_times((parts[odd, index, 0], parts[odd, index, 1])) for index in (0, 1)]
        out[channel, :half] = found[0]
        out[channel, half : 2 * half] = found[1]
        out[channel, 2 * half :] = found[0] - found[1]
        entries = [found[n // 4][n % 4 * directions : (n % 4 + 1) * directions] for n in range(8)]
        for n, value in enumerate(grams(entries)):
            rows = slice(n * directions, (n + 1) * directions)
            gram[rows] = value if channel == 0 else gram[rows] + value
    for copy in copies[5:]:
        copy.wait()


def model_kernel(coherent, hots, own, other, jones, gather, predicted, model):
    place = Place()
    fill_table(place, jones, own, other)
    gather_gains(jones[...], hots, gather)
    for run in range(2):
        predict(coherent, gather, run, model, predicted)


def gather_gains(table, hots, gather):
    rows = table.shape[0]
    split = jnp.concatenate(pieces(table, 2))
    for side in (0, 1):
        found = dot_f32(split, hots[side])
        found = found[:rows] + found[rows:]
        for run in range(found.shape[1] // RUN):
            gather[side, run] = found[:, run * RUN : (run + 1) * RUN]


def gains_of(gather, side, run, h):
    return [gather[side, run, pl.ds(64 * h + n, 8, stride=8), :] for n in range(8)]


def coherent_of(coherent, channel, h, lanes, directions, count):
    return [
        coherent[channel, n * directions + 8 * h : n * directions + 8 * h + 8, lanes] for n in range(count)
    ]


def small_product(a, b, turned=False):
    order = ((0, 1), (2, 3)) if turned else ((0, 2), (1, 3))
    return [
        a[2 * row] * b[order[col][0]] + a[2 * row + 1] * b[order[col][1]] for row in (0, 1) for col in (0, 1)
    ]


def less(a, b):
    return [x - y for x, y in zip(a, b)]


def plus(a, b):
    return [x + y for x, y in zip(a, b)]


def model_parts(first, second, coh):
    re, im, mixed = coh[:4], coh[4:8], coh[8:]
    p1 = small_product(first[:4], re)
    p2 = small_product(first[4:8], im)
    p3 = small_product(first[8:], mixed)
    zr = less(p1, p2)
    zi = less(plus(p1, p2), p3)
    return (
        small_product(zr, second[:4], True)
        + small_product(zi, second[4:8], True)
        + small_product(plus(zr, zi), second[8:], True)
    )


def model_of(parts):
    a, b, d = parts[:4], parts[4:8], parts[8:]
    return plus(a, b) + plus(less(d, a), b)


def with_difference(matrix):
    return matrix + less(matrix[:4], matrix[4:])


def multiply_into(total, a, b, conj_b=False):
    real = a[0] * b[0]
    imag = a[1] * b[0]
    if total is not None:
        real, imag = total[0] + real, total[1] + imag
    if conj_b:
        return real + a[1] * b[1], imag - a[0] * b[1]
    return real - a[1] * b[1], imag + a[0] * b[1]


def fill_table(place, jones, own, other):
    count = own.shape[0] * own.shape[1]
    for ref, core in ((own, place.core), (other, 1 - place.core)):
        at = pl.ds(pl.multiple_of(core * count, count), count)
        jones[at, 0:RUN] = ref[:, :, 0:RUN].reshape(count, RUN)
        window = ref[:, :, pl.ds(place.first_station(place.core), RUN)]
        jones[at, RUN:] = window.reshape(count, RUN)


def predict(coherent, gather, run, model, predicted):
    channels = coherent.shape[0]
    directions = coherent.shape[1] // 12
    halves = directions // 8
    lanes = slice(run * RUN, (run + 1) * RUN)
    for h in range(halves):
        first_gain = with_difference(gains_of(gather, 0, run, h))
        second_gain = with_difference(gains_of(gather, 1, run, h))
        for channel in range(channels):
            coh = coherent_of(coherent, channel, h, lanes, directions, 12)
            part = model_parts(first_gain, second_gain, coh)
            if h > 0:
                part = [a + model[channel, n] for n, a in enumerate(part)]
            if h < halves - 1:
                for n in range(12):
                    model[channel, n] = part[n]
            else:
                predicted[run, channel] = sum_rows(model_of(part))


def iterate(place, coherent, gram, hots, shards, mask, gather, predicted, error, sums):
    directions = coherent.shape[1] // 12
    rows = 8 * directions
    halves = rows // 64
    weight = mask[:, pl.ds(place.first_lane, PAIR)].astype(jnp.float32)
    channels = coherent.shape[0]
    per_shard = shards[0].shape[1]
    for run in range(2):
        lanes = slice(run * RUN, (run + 1) * RUN)
        w = weight[:, lanes]
        at = pl.multiple_of(place.first_lane + run * RUN, RUN)
        for slot in range(channels):
            channel = place.channel_of(slot, per_shard)
            seen = shards[slot // per_shard][:, slot % per_shard, 0, pl.ds(at, RUN)]
            err = w * (seen - predicted[run, channel])
            error[channel, 0] = err
            error[channel, 1] = err + pltpu.roll(err, 4, 0)

        for h in range(halves):
            first_gain, second_gain = gains_of(gather, 0, run, h), gains_of(gather, 1, run, h)
            second = [None] * 4
            for i in (0, 1):
                zero = jnp.zeros((8, RUN), jnp.float32)
                p1, p2, p3 = [zero] * 8, [zero] * 8, [zero] * 8
                for channel in range(channels):
                    coh = coherent_of(coherent, channel, h, lanes, directions, 12)

                    def err(tile, n):
                        return jnp.broadcast_to(error[channel, tile, n : n + 1], (8, RUN))

                    for j in (0, 1):
                        er, ei, es = err(0, 2 * i + j), err(0, 4 + 2 * i + j), err(1, 2 * i + j)
                        for kl in range(4):
                            n = 4 * j + kl
                            p1[n] = p1[n] + er * coh[kl]
                            p2[n] = p2[n] + ei * coh[4 + kl]
                            p3[n] = p3[n] + es * coh[8 + kl]
                outer = list(zip(plus(p1, p2), plus(less(p3, p1), p2)))
                for l in (0, 1):
                    total = None
                    for j in (0, 1):
                        for k in (0, 1):
                            g = (second_gain[2 * j + k], second_gain[4 + 2 * j + k])
                            total = multiply_into(total, outer[4 * j + 2 * l + k], g)
                    for imag in (0, 1):
                        n = 4 * imag + 2 * i + l
                        sums[0, run, pl.ds(64 * h + n, 8, stride=8), :] = total[imag]
                for a in (0, 1):
                    for l in (0, 1):
                        for k in (0, 1):
                            g = (first_gain[2 * i + k], first_gain[4 + 2 * i + k])
                            second[2 * a + l] = multiply_into(
                                second[2 * a + l], g, outer[4 * a + 2 * k + l], conj_b=True
                            )
            for n in range(8):
                sums[1, run, pl.ds(64 * h + n, 8, stride=8), :] = second[n % 4][n // 4]
            form = [gram[n * directions + 8 * h : n * directions + 8 * h + 8, lanes] for n in range(8)]
            sums[0, run, rows + 8 * h : rows + 8 * h + 8] = w * curvature_of(second_gain, form[:4])
            sums[1, run, rows + 8 * h : rows + 8 * h + 8] = w * curvature_of(first_gain, form[4:])

    total = None
    height = sums.shape[2]
    for side in (0, 1):
        whole = jnp.concatenate([sums[side, run] for run in range(2)], axis=1)
        found = dot_f32(jnp.concatenate(pieces(whole, 2)), hots[side], 1)
        found = found[:height] + found[height:]
        total = found if total is None else total + found
    return total


def pack(total, rows):
    half = rows // 2
    low = jnp.concatenate([total[:half], total[rows : rows + half // 8]])
    high = jnp.concatenate([total[half:rows], total[rows + half // 8 :]])
    lane = lax.broadcasted_iota(jnp.int32, low.shape, 1)
    return jnp.where(lane < BLOCK, low, pltpu.roll(high, BLOCK, 1))


def unpack(packed):
    half = packed.shape[0] * 8 // 9
    turned = pltpu.roll(packed, BLOCK, 1)
    return jnp.concatenate([packed[:half], turned[:half], packed[half:], turned[half:]])


def update(jones, lanes, sums, keep=None):
    rows = jones.shape[0]
    for d in range(rows // 8):
        now = jones[8 * d : 8 * d + 8, lanes]
        ratio = STEP_SIZE / (sums[rows + d : rows + d + 1] + EPSILON)
        new = now + ratio * sums[8 * d : 8 * d + 8]
        if keep is not None:
            new = jnp.where(keep, new, now)
        jones[8 * d : 8 * d + 8, lanes] = new


def block_zero():
    return lax.broadcasted_iota(jnp.int32, (8, RUN), 1) < BLOCK


def first_kernel(
    mask, coherent, gram, hots, gather, predicted, s0, s1, s2, s3, packed, to_core, mine, error, sums
):
    place = Place()
    held = packed.shape[0]
    count = 8 * (coherent.shape[1] // 12)
    run = pl.ds(pl.multiple_of(lax.rem(place.chan, 2) * RUN, RUN), RUN)
    for channel in range(coherent.shape[0]):
        to_core[held + count * channel : held + count * (channel + 1)] = coherent[channel, :count, run]
    total = iterate(place, coherent, gram, hots, (s0, s1, s2, s3), mask, gather, predicted, error, sums)
    packed[...] = pack(total[:, :RUN], count)
    to_core[:held] = packed[...]
    mine[...] = total[:, RUN:]


def block_sums(refs, held):
    here, over_core, over_blk, over_both = [ref[:held] for ref in refs]
    return unpack((here + over_core) + (over_blk + over_both))


def second_kernel(
    mask, coherent, gram, hots, before, mine, p0, p1, p2, p3, s0, s1, s2, s3,
    to_core, to_blk, to_both, jones, model, error, gather, predicted, sums,
):
    place = Place()
    held = p0.shape[0]
    jones[...] = before[...]
    update(jones, slice(0, RUN), block_sums((p0, p1, p2, p3), held), block_zero())
    update(jones, slice(RUN, None), mine[...])
    gather_gains(jones[...], hots, gather)
    for run in range(2):
        predict(coherent, gather, run, model, predicted)
    total = iterate(place, coherent, gram, hots, (s0, s1, s2, s3), mask, gather, predicted, error, sums)
    rows = jones.shape[0]
    half = rows // 2
    packed = pack(total[:, :RUN], rows)
    update(jones, slice(RUN, None), total[:, RUN:])
    to_core[:held] = packed
    to_blk[:held] = packed
    to_both[:held] = packed
    to_core[held:] = jones[:, RUN:]
    to_blk[held:] = jones[pl.ds(pl.multiple_of(place.core * half, half), half), RUN:]
    to_both[held:] = jones[pl.ds(pl.multiple_of((1 - place.core) * half, half), half), RUN:]


def shared_of(share, channel, h, rows):
    start = (rows + rows // 8) // 2 + channel * rows + 8 * h
    return [share[pl.ds(pl.multiple_of(start + n * (rows // 8), 8), 8)] for n in range(8)]


def last_kernel(
    mask, share, other_share, hots, before, p0, p1, p2, p3, s0, s1, s2, s3,
    residual, solved_at, jones, gather, solved, sem,
):
    place = Place()
    rows = before.shape[0]
    half = rows // 2
    held = p0.shape[0] - rows
    owned = place.last_core == place.core
    jones[:, 0:RUN] = before[:, 0:RUN]
    jones[:, RUN:] = jnp.where(owned, p0[held:], p1[held:])
    update(jones, slice(0, RUN), block_sums((p0, p1, p2, p3), held), block_zero())

    own_rows = pl.multiple_of(place.core * half, half)
    for ref, start, blk, core in (
        (p0, held + own_rows, place.blk, place.core),
        (p1, held + own_rows, place.blk, 1 - place.core),
        (p2, held, 1 - place.blk, place.core),
        (p3, held, 1 - place.blk, 1 - place.core),
    ):
        lanes = pl.ds(pl.multiple_of((2 * blk + core) * RUN, RUN), RUN)
        solved[:, :, lanes] = ref[pl.ds(pl.multiple_of(start, 8), half)].reshape(half // 8, 8, RUN)
    zero = jones[pl.ds(own_rows, half), 0:RUN].reshape(half // 8, 8, RUN)
    lane = lax.broadcasted_iota(jnp.int32, zero.shape, 2)
    solved[:, :, 0:RUN] = jnp.where(lane < BLOCK, zero, solved[:, :, 0:RUN])
    copy = pltpu.make_async_copy(solved, solved_at, sem)
    copy.start()

    gather_gains(jones[...], hots, gather)
    w = mask[:, pl.ds(place.last_lane, RUN)].astype(jnp.float32)
    shards = (s0, s1, s2, s3)
    per_shard = s0.shape[1]
    channels = 4 * per_shard
    gains = [[gains_of(gather, side, 0, h) for h in range(rows // 64)] for side in (0, 1)]
    for slot in range(channels):
        channel = place.channel_of(slot, per_shard)
        part = None
        for h in range(rows // 64):
            coh = [
                jnp.where(owned, a, b)
                for a, b in zip(shared_of(share, channel, h, rows), shared_of(other_share, channel, h, rows))
            ]
            part = product(product(gains[0][h], coh), gains[1][h], dagger_b=True, total=part)
        seen = shards[slot // per_shard][:, slot % per_shard, 0, pl.ds(place.last_lane, RUN)]
        residual[:, channel, 0] = w * (seen - sum_rows(part))
    copy.wait()


def call(kernel, out_shape, scratch, operands, flops, in_hbm=0, out_spaces=None):
    spaces = [pltpu.HBM] * in_hbm + [pltpu.VMEM] * (len(operands) - in_hbm)
    return pl.pallas_call(
        kernel,
        out_shape=out_shape,
        in_specs=[pl.BlockSpec(memory_space=space) for space in spaces],
        out_specs=tuple(
            pl.BlockSpec(memory_space=space) for space in out_spaces or [pltpu.VMEM] * len(out_shape)
        ),
        scratch_shapes=scratch,
        compiler_params=pltpu.CompilerParams(vmem_limit_bytes=40 << 20),
        cost_estimate=pl.CostEstimate(
            flops=flops,
            transcendentals=0,
            bytes_accessed=sum(x.size * x.dtype.itemsize for x in [*operands, *out_shape]),
        ),
    )(*[pltpu.with_memory_space_constraint(x, space) for x, space in zip(operands, spaces)])


def f32(*shape):
    return jax.ShapeDtypeStruct(shape, jnp.float32)


def bf16(*shape):
    return jax.ShapeDtypeStruct(shape, jnp.bfloat16)


def swap(x, axis, bit=1):
    return lax.ppermute(x, axis, [(i, i ^ bit) for i in range(lax.axis_size(axis))])


def from_three(core, blk, both):
    return swap(core, "dir"), swap(blk, "blk"), swap(both, ("blk", "dir"), 3)


def per_device_owned(
    visibilities,
    antenna_pairs,
    valid_mask,
    station_positions,
    source_offsets,
    brightness,
    source_cluster,
    jones_gains,
):
    relay_count = lax.axis_size("chan")
    channels = visibilities.shape[1] * relay_count
    half_directions = jones_gains.shape[0]
    directions = 2 * half_directions
    rows = 8 * directions
    sources = source_offsets.shape[1]

    other = swap(jones_gains, "dir")
    places = [(chan, core) for chan in range(relay_count) for core in range(2)]
    odd = lax.ppermute(
        visibilities,
        ("chan", "dir"),
        [(2 * chan + core, 2 * (chan ^ (1 + 2 * core)) + core) for chan, core in places],
    )
    even = swap(visibilities, "chan", 2)
    inputs = (antenna_pairs, station_positions, source_offsets, brightness, source_cluster[None, :])
    kept = (valid_mask, visibilities, jones_gains)
    held = (rows + directions) // 2
    table = f32(rows, 2 * RUN)
    gathered = f32(2, 2, rows, RUN)
    predictions = f32(2, channels, 8, RUN)
    model = pltpu.VMEM((channels, 12, 8, RUN), jnp.float32)
    scratch = [
        pltpu.VMEM((channels, 2, 8, RUN), jnp.float32),
        pltpu.VMEM((2, 2, rows + directions, RUN), jnp.float32),
    ]
    coherent, gram, hots, last_hots, mask, seen, own = call(
        functools.partial(coherency_kernel, channels),
        (
            f32(channels, 12 * directions, PAIR),
            f32(8 * directions, PAIR),
            bf16(2, 2 * RUN, PAIR),
            bf16(2, 2 * RUN, RUN),
            *[jax.ShapeDtypeStruct(x.shape, x.dtype) for x in kept],
        ),
        [pltpu.VMEM(x.shape, x.dtype) for x in inputs]
        + [
            pltpu.VMEM((2, sources, PAIR), jnp.float32),
            pltpu.VMEM((2, sources, PAIR), jnp.float32),
            pltpu.VMEM((2, 2, 2, sources, PAIR), jnp.bfloat16),
            pltpu.SemaphoreType.DMA((len(inputs + kept),)),
        ],
        inputs + kept,
        4 * 10**9,
        len(inputs + kept),
    )
    odd, coherent, hots = lax.optimization_barrier((odd, coherent, hots))
    shards = [seen, odd, even, swap(odd, "dir")]
    jones, gather, predicted = call(
        model_kernel,
        (table, gathered, predictions),
        [model],
        (coherent, hots, own, other),
        2 * 10**9,
    )
    packed, share, mine = call(
        first_kernel,
        (f32(held, RUN), f32(held + channels * rows, RUN), f32(rows + directions, RUN)),
        scratch,
        (mask, coherent, gram, hots, gather, predicted, *shards),
        10**9,
    )
    sums = from_three(share, packed, packed)
    to_core, to_blk, to_both, jones = call(
        second_kernel,
        (f32(held + rows, RUN), f32(held + rows // 2, RUN), f32(held + rows // 2, RUN), table),
        [
            model,
            scratch[0],
            pltpu.VMEM(gathered.shape, jnp.float32),
            pltpu.VMEM(predictions.shape, jnp.float32),
            scratch[1],
        ],
        (mask, coherent, gram, hots, jones, mine, packed, *sums, *shards),
        2 * 10**9,
    )
    solved = f32(half_directions, 8, station_positions.shape[1])
    return call(
        last_kernel,
        (f32(8, channels, 1, RUN), solved),
        [
            pltpu.VMEM((rows, 2 * RUN), jnp.float32),
            pltpu.VMEM((2, 1, rows, RUN), jnp.float32),
            pltpu.VMEM(solved.shape, jnp.float32),
            pltpu.SemaphoreType.DMA,
        ],
        (
            mask, share, sums[0], last_hots, jones,
            to_core, *from_three(to_core, to_blk, to_both), *shards,
        ),
        10**9,
        0,
        (pltpu.VMEM, pltpu.HBM),
    )


def owned_layout(mesh, shapes):
    sizes = mesh.shape
    owners = sizes["chan"] * sizes["blk"]
    visibilities, pairs, jones = shapes
    return (
        owners == BLOCKS
        and sizes["blk"] == 2
        and sizes["dir"] == 2
        and sizes["chan"] == 4
        and pairs[1] * pairs[2] == owners * RUN
        and jones[0] == 16
        and jones[2] == BLOCKS * BLOCK
        and visibilities[1] % sizes["chan"] == 0
        and visibilities[1] & (visibilities[1] - 1) == 0
    )


def solution(mesh):
    in_specs = (
        P("groups", "chan", "blk", None),
        P(None, "blk", None),
        P("blk", "groups"),
        P(),
        P(),
        P(),
        P(),
        P("dir", "groups", None),
    )
    out_specs = (P("groups", None, "blk", "chan"), P("dir", "groups", None))

    def run(*arrays):
        owned = owned_layout(mesh, (arrays[0].shape, arrays[1].shape, arrays[7].shape))
        body = per_device_owned if owned else per_device
        return jax.shard_map(
            body, mesh=mesh, in_specs=in_specs, out_specs=out_specs, check_vma=False
        )(*arrays)

    return run
```

```python
import functools
import math

import jax
import jax.numpy as jnp
from jax import lax
from jax.experimental import pallas as pl
from jax.experimental.pallas import tpu as pltpu
from jax.sharding import PartitionSpec as P

ITERS = 2


TWO_PI = 2.0 * math.pi
STEP_SIZE = 0.3
EPSILON = 1e-06
HIGHEST = lax.Precision.HIGHEST


def jones_product(former, latter):
    real_list = []
    imag_list = []
    for row_number in (0, 1):
        for column in (0, 1):
            real_list.append(
                former[2 * row_number] * latter[column]
                - former[4 + 2 * row_number] * latter[4 + column]
                + former[2 * row_number + 1] * latter[2 + column]
                - former[5 + 2 * row_number] * latter[6 + column]
            )
            imag_list.append(
                former[2 * row_number] * latter[4 + column]
                + former[4 + 2 * row_number] * latter[column]
                + former[2 * row_number + 1] * latter[6 + column]
                + former[5 + 2 * row_number] * latter[2 + column]
            )
    return jnp.stack(real_list + imag_list)


def adjoint(matrix):
    return jnp.stack(
        [matrix[0], matrix[2], matrix[1], matrix[3], -matrix[4], -matrix[6], -matrix[5], -matrix[7]]
    )


def source_table(brightness, source_cluster, direction_ids):
    member = (source_cluster[None, :] == direction_ids[:, None]).astype(jnp.float32)
    return (brightness[:, None, :] * member[None, :, :]).reshape(
        4 * direction_ids.shape[0], brightness.shape[1]
    )


def coherency(bright_table, geometry, scales):
    phase_grid = (TWO_PI * scales)[None, :, None] * geometry[:, None, :]
    phases_flat = phase_grid.reshape(geometry.shape[0], -1)
    real_block = jnp.dot(bright_table, jnp.cos(phases_flat), precision=HIGHEST)
    imag_block = -jnp.dot(bright_table, jnp.sin(phases_flat), precision=HIGHEST)
    dir_count = bright_table.shape[0] // 4
    return jnp.concatenate([real_block, imag_block], axis=0).reshape(
        8, dir_count, scales.shape[0], geometry.shape[1]
    )


def per_device(
    visibilities,
    antenna_pairs,
    valid_mask,
    station_positions,
    source_offsets,
    brightness,
    source_cluster,
    jones_gains,
):
    relay_count = lax.axis_size("chan")
    base_count = antenna_pairs.shape[2] // relay_count
    station_count = station_positions.shape[1]
    offset = lax.axis_index("chan") * base_count
    own_pairs = lax.dynamic_slice_in_dim(antenna_pairs[:, 0], offset, base_count, 1)
    first_station = own_pairs[0]
    second_station = own_pairs[1]
    weight_row = lax.dynamic_slice_in_dim(valid_mask[0], offset, base_count, 0).astype(jnp.float32)
    regrouped = lax.all_to_all(visibilities, "chan", split_axis=3, concat_axis=1, tiled=True)[
        :, :, 0, :
    ]
    total_channels = regrouped.shape[1]
    own_directions = jones_gains.shape[0]
    channel_ids = jnp.arange(total_channels)
    gains_now = jones_gains
    direction_ids = lax.axis_index("dir") * own_directions + jnp.arange(own_directions)
    local_channels = regrouped.shape[1]
    scales = 1.0 + 0.5 * channel_ids.astype(jnp.float32) / total_channels
    u_coord = station_positions[0][first_station] - station_positions[0][second_station]
    v_coord = station_positions[1][first_station] - station_positions[1][second_station]
    geometry = (
        source_offsets[0][:, None] * u_coord[None, :]
        + source_offsets[1][:, None] * v_coord[None, :]
    )
    bright_table = source_table(brightness, source_cluster, direction_ids)
    group_size = math.gcd(local_channels, max(1, 2048 // base_count))
    group_count = local_channels // group_size
    scale_groups = scales.reshape(group_count, group_size)
    onehot_first = (first_station[:, None] == jnp.arange(station_count)[None, :]).astype(
        jnp.float32
    )
    onehot_second = (second_station[:, None] == jnp.arange(station_count)[None, :]).astype(
        jnp.float32
    )

    def station_gains(gains_current):
        gain_first = jnp.take(gains_current, first_station, axis=2).transpose(1, 0, 2)[
            :, :, None, :
        ]
        gain_second = jnp.take(gains_current, second_station, axis=2).transpose(1, 0, 2)[
            :, :, None, :
        ]
        return (gain_first, gain_second)

    def residual_of(gains_current):
        gain_first, gain_second = station_gains(gains_current)

        def residual_one_group(scale_group):
            coherent = coherency(bright_table, geometry, scale_group)
            return jnp.sum(
                jones_product(jones_product(gain_first, coherent), adjoint(gain_second)), axis=1
            )

        partial_model = jnp.moveaxis(lax.map(residual_one_group, scale_groups), 0, 1).reshape(
            8, local_channels, base_count
        )
        model_vis = lax.psum(partial_model, "dir")
        return weight_row * (regrouped - model_vis)

    for iteration in range(ITERS):
        residual_now = residual_of(gains_now)
        updated_gain_first, updated_gain_second = station_gains(gains_now)
        resid_groups = jnp.moveaxis(
            residual_now.reshape(8, group_count, group_size, base_count), 1, 0
        )
        dir_count = gains_now.shape[0]

        def updated_one_group(running, inputs):
            scale_group, resid_group = inputs
            coherent = coherency(bright_table, geometry, scale_group)
            toward_second = jones_product(updated_gain_second, adjoint(coherent))
            toward_first = jones_product(updated_gain_first, coherent)
            grad_first = jnp.sum(jones_product(resid_group[:, None], toward_second), axis=2)
            grad_second = jnp.sum(
                jones_product(adjoint(resid_group)[:, None], toward_first), axis=2
            )
            curv_first = jnp.sum(toward_second * toward_second, axis=(0, 2))
            curv_second = jnp.sum(toward_first * toward_first, axis=(0, 2))
            return (
                (
                    running[0] + grad_first,
                    running[1] + grad_second,
                    running[2] + curv_first,
                    running[3] + curv_second,
                ),
                None,
            )

        zero_sums = (
            jnp.zeros((8, dir_count, base_count), jnp.float32),
            jnp.zeros((8, dir_count, base_count), jnp.float32),
            jnp.zeros((dir_count, base_count), jnp.float32),
            jnp.zeros((dir_count, base_count), jnp.float32),
        )
        totals, ignored = lax.scan(updated_one_group, zero_sums, (scale_groups, resid_groups))
        grad_station = jnp.einsum(
            "cdb,bs->dcs", totals[0], onehot_first, precision=HIGHEST
        ) + jnp.einsum("cdb,bs->dcs", totals[1], onehot_second, precision=HIGHEST)
        curv_station = jnp.dot(weight_row * totals[2], onehot_first, precision=HIGHEST) + jnp.dot(
            weight_row * totals[3], onehot_second, precision=HIGHEST
        )
        grad_station, curv_station = lax.psum((grad_station, curv_station), ("chan", "blk"))
        gains_now = gains_now + STEP_SIZE * grad_station / (curv_station[:, None, :] + EPSILON)
    residual_now = residual_of(gains_now)
    return (residual_now[:, :, None, :], gains_now)


COS_TERMS = (
    0.9999999890590228,
    -19.739204499454,
    64.93911745989914,
    -85.45013953093448,
    60.16763095128989,
    -25.96759924954187,
    6.528658162606979,
)
SIN_TERMS = (
    6.283185302511502,
    -41.34170040531754,
    81.6051313857969,
    -76.70301535383193,
    42.02592698564183,
    -14.899846667160109,
    3.2381375090822355,
)
RUN = 128
BLOCK = 64
BLOCKS = 8
PAIR = 2 * RUN


def pieces(value, count):
    result = []
    for index in range(count):
        piece = value.astype(jnp.bfloat16)
        result.append(piece)
        if index < count - 1:
            value = value - piece.astype(jnp.float32)
    return result


def dot_f32(left, right, contract_right=0):
    return lax.dot_general(
        left,
        right,
        (((1,), (contract_right,)), ((), ())),
        preferred_element_type=jnp.float32,
    )


def horner(terms, x):
    total = jnp.full_like(x, terms[-1])
    for term in terms[-2::-1]:
        total = total * x + term
    return total


def turn_pair(turns):
    rest = turns - jnp.round(turns)
    square = rest * rest
    return horner(COS_TERMS, square), horner([-term for term in SIN_TERMS], square) * rest


def product(a, b, dagger_a=False, dagger_b=False, total=None):
    result = [None] * 8 if total is None else list(total)

    def add(n, x, y, positive):
        term = x * y
        if result[n] is None:
            result[n] = term if positive else -term
        else:
            result[n] = result[n] + term if positive else result[n] - term

    for row in (0, 1):
        for col in (0, 1):
            n = 2 * row + col
            for inner in (0, 1):
                i = 2 * inner + row if dagger_a else 2 * row + inner
                j = 2 * col + inner if dagger_b else 2 * inner + col
                add(n, a[i], b[j], True)
                add(n, a[4 + i], b[4 + j], dagger_a != dagger_b)
                if dagger_a:
                    add(4 + n, a[i], b[4 + j], not dagger_b)
                    add(4 + n, a[4 + i], b[j], False)
                else:
                    add(4 + n, a[4 + i], b[j], True)
                    add(4 + n, a[i], b[4 + j], not dagger_b)
    return result


def sum_rows(parts):
    row = lax.broadcasted_iota(jnp.int32, parts[0].shape, 0)
    low = row < 4
    parts = [
        jnp.where(low, a, b) + pltpu.roll(jnp.where(low, b, a), 4, 0)
        for a, b in zip(parts[:4], parts[4:])
    ]
    for step in (2, 1):
        low = jnp.bitwise_and(row, step) == 0
        parts = [
            jnp.where(low, a + pltpu.roll(a, 8 - step, 0), b + pltpu.roll(b, step, 0))
            for a, b in zip(parts[:step], parts[step:])
        ]
    return parts[0]


class Place:
    def __init__(self):
        self.chan = lax.axis_index("chan")
        self.core = lax.axis_index("dir")
        self.blk = lax.axis_index("blk")
        self.first_lane = pl.multiple_of(self.core * PAIR, PAIR)
        self.last_core = self.chan // 2
        self.last_lane = pl.multiple_of(self.chan * RUN, RUN)

    def first_station(self, core):
        return pl.multiple_of((2 * self.blk + core) * RUN, RUN)

    def channel_of(self, slot, per_shard):
        bits = (0, 1 + 2 * self.core, 2, 3 - 2 * self.core)[slot // per_shard]
        return jnp.bitwise_xor(bits, self.chan) * per_shard + slot % per_shard


def onehot(station, first_station):
    local = jnp.where(station < BLOCK, station, station - first_station + RUN)
    rows = lax.broadcasted_iota(jnp.int32, (2 * RUN, station.shape[1]), 0)
    return jnp.where(rows == local, 1.0, 0.0).astype(jnp.bfloat16)


def split_rows(value, count):
    split = [p.astype(jnp.float32) for p in pieces(value, count)]
    missing = -count * value.shape[0] % 16
    if missing:
        split.append(jnp.zeros((missing, value.shape[1]), jnp.float32))
    return jnp.concatenate(split).astype(jnp.bfloat16)


def grams(coh):
    re, im = coh[:4], coh[4:]
    size = [a * a + b * b for a, b in zip(re, im)]

    def cross(i, j, k, l):
        real = re[i] * re[j] + im[i] * im[j] + re[k] * re[l] + im[k] * im[l]
        imag = re[i] * im[j] - im[i] * re[j] + re[k] * im[l] - im[k] * re[l]
        return [real + real, imag + imag]

    inner = [size[0] + size[2], size[1] + size[3]] + cross(0, 1, 2, 3)
    outer = [size[0] + size[1], size[2] + size[3]] + cross(2, 0, 3, 1)
    return inner + outer


def curvature_of(gain, gram):
    re, im = gain[:4], gain[4:]
    size = [a * a + b * b for a, b in zip(re, im)]
    real = re[0] * re[1] + im[0] * im[1] + re[2] * re[3] + im[2] * im[3]
    imag = im[0] * re[1] - re[0] * im[1] + im[2] * re[3] - re[2] * im[3]
    total = (size[0] + size[2]) * gram[0] + (size[1] + size[3]) * gram[1] + real * gram[2] - imag * gram[3]
    return jnp.maximum(total, 0.0)


def coherency_kernel(
    channels, pairs_at, positions_at, offsets_at, brightness_at, cluster_at, mask_at, seen_at, own_at,
    out, share, gram, hots, last_hots, mask, seen, own,
    pairs, positions, offsets, brightness, cluster, base, spin, parts, sems,
):
    copies = [
        pltpu.make_async_copy(source, target, sems.at[index])
        for index, (source, target) in enumerate(
            (
                (pairs_at, pairs),
                (positions_at, positions),
                (offsets_at, offsets),
                (brightness_at, brightness),
                (cluster_at, cluster),
                (mask_at, mask),
                (seen_at, seen),
                (own_at, own),
            )
        )
    ]
    for copy in copies:
        copy.start()
    for copy in copies[:5]:
        copy.wait()
    place = Place()
    window = place.first_station(place.core)
    table = jnp.concatenate([positions[:, 0:RUN], positions[:, pl.ds(window, RUN)]], axis=1)
    table = split_rows(table, 3)
    there = []
    for side in (0, 1):
        hots[side] = onehot(pairs[side, :, pl.ds(place.first_lane, PAIR)], window)
        last = pairs[side, :, pl.ds(place.last_lane, RUN)]
        last_hots[side] = onehot(last, place.first_station(place.last_core))
        found = dot_f32(table, hots[side])
        there.append(found[0:2] + found[2:4] + found[4:6])
    span = there[0] - there[1]
    sources = offsets.shape[1]
    columns = jnp.transpose(jnp.concatenate([offsets[...], jnp.zeros((6, sources))]))
    step = 16
    for start in range(0, sources, step):
        rows = slice(start, start + step)
        geometry = columns[rows, 0:1] * span[0:1] + columns[rows, 1:2] * span[1:2]
        c, s = turn_pair(geometry * (0.5 / channels))
        spin[0, rows], spin[1, rows] = c, s
        for _ in range((2 * channels).bit_length() - 1):
            twice = s + s
            c, s = 1.0 - twice * s, twice * c
        base[0, rows], base[1, rows] = c, s

    directions = out.shape[1] // 12
    second_run = lax.rem(place.chan, 2) == 1
    member = lax.broadcasted_iota(jnp.int32, (directions, sources), 0) == cluster[...]
    bright = jnp.concatenate([jnp.where(member, brightness[n : n + 1], 0.0) for n in range(4)])
    high, low = pieces(bright, 2)
    both = jnp.concatenate([high, low])
    half = 4 * directions

    def table_times(refs):
        wide = dot_f32(both, refs[0])
        return wide[:half] + wide[half:] + dot_f32(high, refs[1])

    for channel in range(channels):
        odd = channel % 2
        for start in range(0, sources, step):
            rows = slice(start, start + step)
            c, s = base[0, rows], base[1, rows]
            for index, value in enumerate((c, s)):
                for size, piece in enumerate(pieces(value, 2)):
                    parts[odd, index, size, rows] = piece
            if channel < channels - 1:
                dc, ds = spin[0, rows], spin[1, rows]
                base[0, rows] = c * dc - s * ds
                base[1, rows] = s * dc + c * ds
        found = [table_times((parts[odd, index, 0], parts[odd, index, 1])) for index in (0, 1)]
        out[channel, :half] = found[0]
        out[channel, half : 2 * half] = found[1]
        out[channel, 2 * half :] = found[0] - found[1]
        for index in (0, 1):
            mine = jnp.where(second_run, found[index][:, RUN:], found[index][:, :RUN])
            share[channel, half * index : half * (index + 1)] = mine
        entries = [found[n // 4][n % 4 * directions : (n % 4 + 1) * directions] for n in range(8)]
        for n, value in enumerate(grams(entries)):
            rows = slice(n * directions, (n + 1) * directions)
            gram[rows] = value if channel == 0 else gram[rows] + value
    for copy in copies[5:]:
        copy.wait()


def model_kernel(coherent, hots, own, other, jones, gather, predicted, model):
    place = Place()
    fill_table(place, jones, own, other)
    gather_gains(jones[...], hots, gather)
    for run in range(2):
        predict(coherent, gather, run, model, predicted)


def gather_gains(table, hots, gather):
    rows = table.shape[0]
    split = jnp.concatenate(pieces(table, 2))
    for side in (0, 1):
        found = dot_f32(split, hots[side])
        found = found[:rows] + found[rows:]
        for run in range(found.shape[1] // RUN):
            gather[side, run] = found[:, run * RUN : (run + 1) * RUN]


def gains_of(gather, side, run, h):
    return [gather[side, run, pl.ds(64 * h + n, 8, stride=8), :] for n in range(8)]


def coherent_of(coherent, channel, h, lanes, directions, count):
    return [
        coherent[channel, n * directions + 8 * h : n * directions + 8 * h + 8, lanes] for n in range(count)
    ]


def small_product(a, b, turned=False):
    order = ((0, 1), (2, 3)) if turned else ((0, 2), (1, 3))
    return [
        a[2 * row] * b[order[col][0]] + a[2 * row + 1] * b[order[col][1]] for row in (0, 1) for col in (0, 1)
    ]


def less(a, b):
    return [x - y for x, y in zip(a, b)]


def plus(a, b):
    return [x + y for x, y in zip(a, b)]


def model_parts(first, second, coh):
    re, im, mixed = coh[:4], coh[4:8], coh[8:]
    p1 = small_product(first[:4], re)
    p2 = small_product(first[4:8], im)
    p3 = small_product(first[8:], mixed)
    zr = less(p1, p2)
    zi = less(plus(p1, p2), p3)
    return (
        small_product(zr, second[:4], True)
        + small_product(zi, second[4:8], True)
        + small_product(plus(zr, zi), second[8:], True)
    )


def model_of(parts):
    a, b, d = parts[:4], parts[4:8], parts[8:]
    return plus(a, b) + plus(less(d, a), b)


def with_difference(matrix):
    return matrix + less(matrix[:4], matrix[4:])


def multiply_into(total, a, b, conj_b=False):
    real = a[0] * b[0]
    imag = a[1] * b[0]
    if total is not None:
        real, imag = total[0] + real, total[1] + imag
    if conj_b:
        return real + a[1] * b[1], imag - a[0] * b[1]
    return real - a[1] * b[1], imag + a[0] * b[1]


def fill_table(place, jones, own, other):
    count = own.shape[0] * own.shape[1]
    for ref, core in ((own, place.core), (other, 1 - place.core)):
        at = pl.ds(pl.multiple_of(core * count, count), count)
        jones[at, 0:RUN] = ref[:, :, 0:RUN].reshape(count, RUN)
        window = ref[:, :, pl.ds(place.first_station(place.core), RUN)]
        jones[at, RUN:] = window.reshape(count, RUN)


def predict(coherent, gather, run, model, predicted):
    channels = coherent.shape[0]
    directions = coherent.shape[1] // 12
    halves = directions // 8
    lanes = slice(run * RUN, (run + 1) * RUN)
    for h in range(halves):
        first_gain = with_difference(gains_of(gather, 0, run, h))
        second_gain = with_difference(gains_of(gather, 1, run, h))
        for channel in range(channels):
            coh = coherent_of(coherent, channel, h, lanes, directions, 12)
            part = model_parts(first_gain, second_gain, coh)
            if h > 0:
                part = [a + model[channel, n] for n, a in enumerate(part)]
            if h < halves - 1:
                for n in range(12):
                    model[channel, n] = part[n]
            else:
                predicted[run, channel] = sum_rows(model_of(part))


def iterate(place, coherent, gram, hots, shards, mask, gather, predicted, error, sums):
    directions = coherent.shape[1] // 12
    rows = 8 * directions
    halves = rows // 64
    weight = mask[:, pl.ds(place.first_lane, PAIR)].astype(jnp.float32)
    channels = coherent.shape[0]
    per_shard = shards[0].shape[1]
    for run in range(2):
        lanes = slice(run * RUN, (run + 1) * RUN)
        w = weight[:, lanes]
        at = pl.multiple_of(place.first_lane + run * RUN, RUN)
        for slot in range(channels):
            channel = place.channel_of(slot, per_shard)
            seen = shards[slot // per_shard][:, slot % per_shard, 0, pl.ds(at, RUN)]
            err = w * (seen - predicted[run, channel])
            error[channel, 0] = err
            error[channel, 1] = err + pltpu.roll(err, 4, 0)

        for h in range(halves):
            first_gain, second_gain = gains_of(gather, 0, run, h), gains_of(gather, 1, run, h)
            second = [None] * 4
            for i in (0, 1):
                zero = jnp.zeros((8, RUN), jnp.float32)
                p1, p2, p3 = [zero] * 8, [zero] * 8, [zero] * 8
                for channel in range(channels):
                    coh = coherent_of(coherent, channel, h, lanes, directions, 12)

                    def err(tile, n):
                        return jnp.broadcast_to(error[channel, tile, n : n + 1], (8, RUN))

                    for j in (0, 1):
                        er, ei, es = err(0, 2 * i + j), err(0, 4 + 2 * i + j), err(1, 2 * i + j)
                        for kl in range(4):
                            n = 4 * j + kl
                            p1[n] = p1[n] + er * coh[kl]
                            p2[n] = p2[n] + ei * coh[4 + kl]
                            p3[n] = p3[n] + es * coh[8 + kl]
                outer = list(zip(plus(p1, p2), plus(less(p3, p1), p2)))
                for l in (0, 1):
                    total = None
                    for j in (0, 1):
                        for k in (0, 1):
                            g = (second_gain[2 * j + k], second_gain[4 + 2 * j + k])
                            total = multiply_into(total, outer[4 * j + 2 * l + k], g)
                    for imag in (0, 1):
                        n = 4 * imag + 2 * i + l
                        sums[0, run, pl.ds(64 * h + n, 8, stride=8), :] = total[imag]
                for a in (0, 1):
                    for l in (0, 1):
                        for k in (0, 1):
                            g = (first_gain[2 * i + k], first_gain[4 + 2 * i + k])
                            second[2 * a + l] = multiply_into(
                                second[2 * a + l], g, outer[4 * a + 2 * k + l], conj_b=True
                            )
            for n in range(8):
                sums[1, run, pl.ds(64 * h + n, 8, stride=8), :] = second[n % 4][n // 4]
            form = [gram[n * directions + 8 * h : n * directions + 8 * h + 8, lanes] for n in range(8)]
            sums[0, run, rows + 8 * h : rows + 8 * h + 8] = w * curvature_of(second_gain, form[:4])
            sums[1, run, rows + 8 * h : rows + 8 * h + 8] = w * curvature_of(first_gain, form[4:])

    total = None
    height = sums.shape[2]
    for side in (0, 1):
        whole = jnp.concatenate([sums[side, run] for run in range(2)], axis=1)
        found = dot_f32(jnp.concatenate(pieces(whole, 2)), hots[side], 1)
        found = found[:height] + found[height:]
        total = found if total is None else total + found
    return total


def pack(total, rows):
    half = rows // 2
    low = jnp.concatenate([total[:half], total[rows : rows + half // 8]])
    high = jnp.concatenate([total[half:rows], total[rows + half // 8 :]])
    lane = lax.broadcasted_iota(jnp.int32, low.shape, 1)
    return jnp.where(lane < BLOCK, low, pltpu.roll(high, BLOCK, 1))


def unpack(packed):
    half = packed.shape[0] * 8 // 9
    turned = pltpu.roll(packed, BLOCK, 1)
    return jnp.concatenate([packed[:half], turned[:half], packed[half:], turned[half:]])


def update(jones, lanes, sums, keep=None):
    rows = jones.shape[0]
    for d in range(rows // 8):
        now = jones[8 * d : 8 * d + 8, lanes]
        ratio = STEP_SIZE / (sums[rows + d : rows + d + 1] + EPSILON)
        new = now + ratio * sums[8 * d : 8 * d + 8]
        if keep is not None:
            new = jnp.where(keep, new, now)
        jones[8 * d : 8 * d + 8, lanes] = new


def block_zero():
    return lax.broadcasted_iota(jnp.int32, (8, RUN), 1) < BLOCK


def first_kernel(
    mask, coherent, gram, hots, gather, predicted, s0, s1, s2, s3, packed, mine, error, sums
):
    place = Place()
    total = iterate(place, coherent, gram, hots, (s0, s1, s2, s3), mask, gather, predicted, error, sums)
    packed[...] = pack(total[:, :RUN], 8 * (coherent.shape[1] // 12))
    mine[...] = total[:, RUN:]


def block_sums(refs, held):
    here, over_core, over_blk, over_both = [ref[:held] for ref in refs]
    return unpack((here + over_core) + (over_blk + over_both))


def second_kernel(
    mask, coherent, gram, hots, before, mine, p0, p1, p2, p3, s0, s1, s2, s3,
    to_core, to_blk, to_both, jones, model, error, gather, predicted, sums,
):
    place = Place()
    held = p0.shape[0]
    jones[...] = before[...]
    update(jones, slice(0, RUN), block_sums((p0, p1, p2, p3), held), block_zero())
    update(jones, slice(RUN, None), mine[...])
    gather_gains(jones[...], hots, gather)
    for run in range(2):
        predict(coherent, gather, run, model, predicted)
    total = iterate(place, coherent, gram, hots, (s0, s1, s2, s3), mask, gather, predicted, error, sums)
    rows = jones.shape[0]
    half = rows // 2
    packed = pack(total[:, :RUN], rows)
    update(jones, slice(RUN, None), total[:, RUN:])
    to_core[:held] = packed
    to_blk[:held] = packed
    to_both[:held] = packed
    to_core[held:] = jones[:, RUN:]
    to_blk[held:] = jones[pl.ds(pl.multiple_of(place.core * half, half), half), RUN:]
    to_both[held:] = jones[pl.ds(pl.multiple_of((1 - place.core) * half, half), half), RUN:]


def last_kernel(
    mask, share, other_share, hots, before, p0, p1, p2, p3, s0, s1, s2, s3,
    residual, solved_at, jones, gather, solved, sem,
):
    place = Place()
    rows = before.shape[0]
    half = rows // 2
    held = p0.shape[0] - rows
    owned = place.last_core == place.core
    jones[:, 0:RUN] = before[:, 0:RUN]
    jones[:, RUN:] = jnp.where(owned, p0[held:], p1[held:])
    update(jones, slice(0, RUN), block_sums((p0, p1, p2, p3), held), block_zero())

    own_rows = pl.multiple_of(place.core * half, half)
    for ref, start, blk, core in (
        (p0, held + own_rows, place.blk, place.core),
        (p1, held + own_rows, place.blk, 1 - place.core),
        (p2, held, 1 - place.blk, place.core),
        (p3, held, 1 - place.blk, 1 - place.core),
    ):
        lanes = pl.ds(pl.multiple_of((2 * blk + core) * RUN, RUN), RUN)
        solved[:, :, lanes] = ref[pl.ds(pl.multiple_of(start, 8), half)].reshape(half // 8, 8, RUN)
    zero = jones[pl.ds(own_rows, half), 0:RUN].reshape(half // 8, 8, RUN)
    lane = lax.broadcasted_iota(jnp.int32, zero.shape, 2)
    solved[:, :, 0:RUN] = jnp.where(lane < BLOCK, zero, solved[:, :, 0:RUN])
    copy = pltpu.make_async_copy(solved, solved_at, sem)
    copy.start()

    gather_gains(jones[...], hots, gather)
    w = mask[:, pl.ds(place.last_lane, RUN)].astype(jnp.float32)
    shards = (s0, s1, s2, s3)
    channels = share.shape[0]
    per_shard = s0.shape[1]
    gains = [[gains_of(gather, side, 0, h) for h in range(rows // 64)] for side in (0, 1)]
    for slot in range(channels):
        channel = place.channel_of(slot, per_shard)
        part = None
        for h in range(rows // 64):
            coh = [
                jnp.where(owned, a, b)
                for a, b in zip(
                    coherent_of(share, channel, h, slice(0, RUN), rows // 8, 8),
                    coherent_of(other_share, channel, h, slice(0, RUN), rows // 8, 8),
                )
            ]
            part = product(product(gains[0][h], coh), gains[1][h], dagger_b=True, total=part)
        seen = shards[slot // per_shard][:, slot % per_shard, 0, pl.ds(place.last_lane, RUN)]
        residual[:, channel, 0] = w * (seen - sum_rows(part))
    copy.wait()


def call(kernel, out_shape, scratch, operands, flops, in_hbm=0, out_spaces=None):
    spaces = [pltpu.HBM] * in_hbm + [pltpu.VMEM] * (len(operands) - in_hbm)
    return pl.pallas_call(
        kernel,
        out_shape=out_shape,
        in_specs=[pl.BlockSpec(memory_space=space) for space in spaces],
        out_specs=tuple(
            pl.BlockSpec(memory_space=space) for space in out_spaces or [pltpu.VMEM] * len(out_shape)
        ),
        scratch_shapes=scratch,
        compiler_params=pltpu.CompilerParams(vmem_limit_bytes=40 << 20),
        cost_estimate=pl.CostEstimate(
            flops=flops,
            transcendentals=0,
            bytes_accessed=sum(x.size * x.dtype.itemsize for x in [*operands, *out_shape]),
        ),
    )(*[pltpu.with_memory_space_constraint(x, space) for x, space in zip(operands, spaces)])


def f32(*shape):
    return jax.ShapeDtypeStruct(shape, jnp.float32)


def bf16(*shape):
    return jax.ShapeDtypeStruct(shape, jnp.bfloat16)


def swap(x, axis, bit=1):
    return lax.ppermute(x, axis, [(i, i ^ bit) for i in range(lax.axis_size(axis))])


def from_three(core, blk, both):
    return swap(core, "dir"), swap(blk, "blk"), swap(both, ("blk", "dir"), 3)


def per_device_owned(
    visibilities,
    antenna_pairs,
    valid_mask,
    station_positions,
    source_offsets,
    brightness,
    source_cluster,
    jones_gains,
):
    relay_count = lax.axis_size("chan")
    channels = visibilities.shape[1] * relay_count
    half_directions = jones_gains.shape[0]
    directions = 2 * half_directions
    rows = 8 * directions
    sources = source_offsets.shape[1]

    other = swap(jones_gains, "dir")
    places = [(chan, core) for chan in range(relay_count) for core in range(2)]
    odd = lax.ppermute(
        visibilities,
        ("chan", "dir"),
        [(2 * chan + core, 2 * (chan ^ (1 + 2 * core)) + core) for chan, core in places],
    )
    even = swap(visibilities, "chan", 2)
    inputs = (antenna_pairs, station_positions, source_offsets, brightness, source_cluster[None, :])
    kept = (valid_mask, visibilities, jones_gains)
    held = (rows + directions) // 2
    table = f32(rows, 2 * RUN)
    gathered = f32(2, 2, rows, RUN)
    predictions = f32(2, channels, 8, RUN)
    model = pltpu.VMEM((channels, 12, 8, RUN), jnp.float32)
    scratch = [
        pltpu.VMEM((channels, 2, 8, RUN), jnp.float32),
        pltpu.VMEM((2, 2, rows + directions, RUN), jnp.float32),
    ]
    coherent, share, gram, hots, last_hots, mask, seen, own = call(
        functools.partial(coherency_kernel, channels),
        (
            f32(channels, 12 * directions, PAIR),
            f32(channels, 8 * directions, RUN),
            f32(8 * directions, PAIR),
            bf16(2, 2 * RUN, PAIR),
            bf16(2, 2 * RUN, RUN),
            *[jax.ShapeDtypeStruct(x.shape, x.dtype) for x in kept],
        ),
        [pltpu.VMEM(x.shape, x.dtype) for x in inputs]
        + [
            pltpu.VMEM((2, sources, PAIR), jnp.float32),
            pltpu.VMEM((2, sources, PAIR), jnp.float32),
            pltpu.VMEM((2, 2, 2, sources, PAIR), jnp.bfloat16),
            pltpu.SemaphoreType.DMA((len(inputs + kept),)),
        ],
        inputs + kept,
        4 * 10**9,
        len(inputs + kept),
    )
    odd, coherent, hots, share = lax.optimization_barrier((odd, coherent, hots, share))
    shards = [seen, odd, even, swap(odd, "dir")]
    other_share = swap(share, "dir")
    jones, gather, predicted = call(
        model_kernel,
        (table, gathered, predictions),
        [model],
        (coherent, hots, own, other),
        2 * 10**9,
    )
    packed, mine = call(
        first_kernel,
        (f32(held, RUN), f32(rows + directions, RUN)),
        scratch,
        (mask, coherent, gram, hots, gather, predicted, *shards),
        10**9,
    )
    sums = from_three(packed, packed, packed)
    to_core, to_blk, to_both, jones = call(
        second_kernel,
        (f32(held + rows, RUN), f32(held + rows // 2, RUN), f32(held + rows // 2, RUN), table),
        [
            model,
            scratch[0],
            pltpu.VMEM(gathered.shape, jnp.float32),
            pltpu.VMEM(predictions.shape, jnp.float32),
            scratch[1],
        ],
        (mask, coherent, gram, hots, jones, mine, packed, *sums, *shards),
        2 * 10**9,
    )
    solved = f32(half_directions, 8, station_positions.shape[1])
    return call(
        last_kernel,
        (f32(8, channels, 1, RUN), solved),
        [
            pltpu.VMEM((rows, 2 * RUN), jnp.float32),
            pltpu.VMEM((2, 1, rows, RUN), jnp.float32),
            pltpu.VMEM(solved.shape, jnp.float32),
            pltpu.SemaphoreType.DMA,
        ],
        (
            mask, share, other_share, last_hots, jones,
            to_core, *from_three(to_core, to_blk, to_both), *shards,
        ),
        10**9,
        0,
        (pltpu.VMEM, pltpu.HBM),
    )


def owned_layout(mesh, shapes):
    sizes = mesh.shape
    owners = sizes["chan"] * sizes["blk"]
    visibilities, pairs, jones = shapes
    return (
        owners == BLOCKS
        and sizes["blk"] == 2
        and sizes["dir"] == 2
        and sizes["chan"] == 4
        and pairs[1] * pairs[2] == owners * RUN
        and jones[0] == 16
        and jones[2] == BLOCKS * BLOCK
        and visibilities[1] % sizes["chan"] == 0
        and visibilities[1] & (visibilities[1] - 1) == 0
    )


def solution(mesh):
    in_specs = (
        P("groups", "chan", "blk", None),
        P(None, "blk", None),
        P("blk", "groups"),
        P(),
        P(),
        P(),
        P(),
        P("dir", "groups", None),
    )
    out_specs = (P("groups", None, "blk", "chan"), P("dir", "groups", None))

    def run(*arrays):
        owned = owned_layout(mesh, (arrays[0].shape, arrays[1].shape, arrays[7].shape))
        body = per_device_owned if owned else per_device
        return jax.shard_map(
            body, mesh=mesh, in_specs=in_specs, out_specs=out_specs, check_vma=False
        )(*arrays)

    return run
```

```python
import functools
import math

import jax
import jax.numpy as jnp
from jax import lax
from jax.experimental import pallas as pl
from jax.experimental.pallas import tpu as pltpu
from jax.sharding import PartitionSpec as P

ITERS = 2


TWO_PI = 2.0 * math.pi
STEP_SIZE = 0.3
EPSILON = 1e-06
HIGHEST = lax.Precision.HIGHEST


def jones_product(former, latter):
    real_list = []
    imag_list = []
    for row_number in (0, 1):
        for column in (0, 1):
            real_list.append(
                former[2 * row_number] * latter[column]
                - former[4 + 2 * row_number] * latter[4 + column]
                + former[2 * row_number + 1] * latter[2 + column]
                - former[5 + 2 * row_number] * latter[6 + column]
            )
            imag_list.append(
                former[2 * row_number] * latter[4 + column]
                + former[4 + 2 * row_number] * latter[column]
                + former[2 * row_number + 1] * latter[6 + column]
                + former[5 + 2 * row_number] * latter[2 + column]
            )
    return jnp.stack(real_list + imag_list)


def adjoint(matrix):
    return jnp.stack(
        [matrix[0], matrix[2], matrix[1], matrix[3], -matrix[4], -matrix[6], -matrix[5], -matrix[7]]
    )


def source_table(brightness, source_cluster, direction_ids):
    member = (source_cluster[None, :] == direction_ids[:, None]).astype(jnp.float32)
    return (brightness[:, None, :] * member[None, :, :]).reshape(
        4 * direction_ids.shape[0], brightness.shape[1]
    )


def coherency(bright_table, geometry, scales):
    phase_grid = (TWO_PI * scales)[None, :, None] * geometry[:, None, :]
    phases_flat = phase_grid.reshape(geometry.shape[0], -1)
    real_block = jnp.dot(bright_table, jnp.cos(phases_flat), precision=HIGHEST)
    imag_block = -jnp.dot(bright_table, jnp.sin(phases_flat), precision=HIGHEST)
    dir_count = bright_table.shape[0] // 4
    return jnp.concatenate([real_block, imag_block], axis=0).reshape(
        8, dir_count, scales.shape[0], geometry.shape[1]
    )


def per_device(
    visibilities,
    antenna_pairs,
    valid_mask,
    station_positions,
    source_offsets,
    brightness,
    source_cluster,
    jones_gains,
):
    relay_count = lax.axis_size("chan")
    base_count = antenna_pairs.shape[2] // relay_count
    station_count = station_positions.shape[1]
    offset = lax.axis_index("chan") * base_count
    own_pairs = lax.dynamic_slice_in_dim(antenna_pairs[:, 0], offset, base_count, 1)
    first_station = own_pairs[0]
    second_station = own_pairs[1]
    weight_row = lax.dynamic_slice_in_dim(valid_mask[0], offset, base_count, 0).astype(jnp.float32)
    regrouped = lax.all_to_all(visibilities, "chan", split_axis=3, concat_axis=1, tiled=True)[
        :, :, 0, :
    ]
    total_channels = regrouped.shape[1]
    own_directions = jones_gains.shape[0]
    channel_ids = jnp.arange(total_channels)
    gains_now = jones_gains
    direction_ids = lax.axis_index("dir") * own_directions + jnp.arange(own_directions)
    local_channels = regrouped.shape[1]
    scales = 1.0 + 0.5 * channel_ids.astype(jnp.float32) / total_channels
    u_coord = station_positions[0][first_station] - station_positions[0][second_station]
    v_coord = station_positions[1][first_station] - station_positions[1][second_station]
    geometry = (
        source_offsets[0][:, None] * u_coord[None, :]
        + source_offsets[1][:, None] * v_coord[None, :]
    )
    bright_table = source_table(brightness, source_cluster, direction_ids)
    group_size = math.gcd(local_channels, max(1, 2048 // base_count))
    group_count = local_channels // group_size
    scale_groups = scales.reshape(group_count, group_size)
    onehot_first = (first_station[:, None] == jnp.arange(station_count)[None, :]).astype(
        jnp.float32
    )
    onehot_second = (second_station[:, None] == jnp.arange(station_count)[None, :]).astype(
        jnp.float32
    )

    def station_gains(gains_current):
        gain_first = jnp.take(gains_current, first_station, axis=2).transpose(1, 0, 2)[
            :, :, None, :
        ]
        gain_second = jnp.take(gains_current, second_station, axis=2).transpose(1, 0, 2)[
            :, :, None, :
        ]
        return (gain_first, gain_second)

    def residual_of(gains_current):
        gain_first, gain_second = station_gains(gains_current)

        def residual_one_group(scale_group):
            coherent = coherency(bright_table, geometry, scale_group)
            return jnp.sum(
                jones_product(jones_product(gain_first, coherent), adjoint(gain_second)), axis=1
            )

        partial_model = jnp.moveaxis(lax.map(residual_one_group, scale_groups), 0, 1).reshape(
            8, local_channels, base_count
        )
        model_vis = lax.psum(partial_model, "dir")
        return weight_row * (regrouped - model_vis)

    for iteration in range(ITERS):
        residual_now = residual_of(gains_now)
        updated_gain_first, updated_gain_second = station_gains(gains_now)
        resid_groups = jnp.moveaxis(
            residual_now.reshape(8, group_count, group_size, base_count), 1, 0
        )
        dir_count = gains_now.shape[0]

        def updated_one_group(running, inputs):
            scale_group, resid_group = inputs
            coherent = coherency(bright_table, geometry, scale_group)
            toward_second = jones_product(updated_gain_second, adjoint(coherent))
            toward_first = jones_product(updated_gain_first, coherent)
            grad_first = jnp.sum(jones_product(resid_group[:, None], toward_second), axis=2)
            grad_second = jnp.sum(
                jones_product(adjoint(resid_group)[:, None], toward_first), axis=2
            )
            curv_first = jnp.sum(toward_second * toward_second, axis=(0, 2))
            curv_second = jnp.sum(toward_first * toward_first, axis=(0, 2))
            return (
                (
                    running[0] + grad_first,
                    running[1] + grad_second,
                    running[2] + curv_first,
                    running[3] + curv_second,
                ),
                None,
            )

        zero_sums = (
            jnp.zeros((8, dir_count, base_count), jnp.float32),
            jnp.zeros((8, dir_count, base_count), jnp.float32),
            jnp.zeros((dir_count, base_count), jnp.float32),
            jnp.zeros((dir_count, base_count), jnp.float32),
        )
        totals, ignored = lax.scan(updated_one_group, zero_sums, (scale_groups, resid_groups))
        grad_station = jnp.einsum(
            "cdb,bs->dcs", totals[0], onehot_first, precision=HIGHEST
        ) + jnp.einsum("cdb,bs->dcs", totals[1], onehot_second, precision=HIGHEST)
        curv_station = jnp.dot(weight_row * totals[2], onehot_first, precision=HIGHEST) + jnp.dot(
            weight_row * totals[3], onehot_second, precision=HIGHEST
        )
        grad_station, curv_station = lax.psum((grad_station, curv_station), ("chan", "blk"))
        gains_now = gains_now + STEP_SIZE * grad_station / (curv_station[:, None, :] + EPSILON)
    residual_now = residual_of(gains_now)
    return (residual_now[:, :, None, :], gains_now)


COS_TERMS = (
    0.9999999890590228,
    -19.739204499454,
    64.93911745989914,
    -85.45013953093448,
    60.16763095128989,
    -25.96759924954187,
    6.528658162606979,
)
SIN_TERMS = (
    6.283185302511502,
    -41.34170040531754,
    81.6051313857969,
    -76.70301535383193,
    42.02592698564183,
    -14.899846667160109,
    3.2381375090822355,
)
RUN = 128
BLOCK = 64
BLOCKS = 8
PAIR = 2 * RUN


def pieces(value, count):
    result = []
    for index in range(count):
        piece = value.astype(jnp.bfloat16)
        result.append(piece)
        if index < count - 1:
            value = value - piece.astype(jnp.float32)
    return result


def dot_f32(left, right, contract_right=0):
    return lax.dot_general(
        left,
        right,
        (((1,), (contract_right,)), ((), ())),
        preferred_element_type=jnp.float32,
    )


def horner(terms, x):
    total = jnp.full_like(x, terms[-1])
    for term in terms[-2::-1]:
        total = total * x + term
    return total


def turn_pair(turns):
    rest = turns - jnp.round(turns)
    square = rest * rest
    return horner(COS_TERMS, square), horner([-term for term in SIN_TERMS], square) * rest


def product(a, b, dagger_a=False, dagger_b=False, total=None):
    result = [None] * 8 if total is None else list(total)

    def add(n, x, y, positive):
        term = x * y
        if result[n] is None:
            result[n] = term if positive else -term
        else:
            result[n] = result[n] + term if positive else result[n] - term

    for row in (0, 1):
        for col in (0, 1):
            n = 2 * row + col
            for inner in (0, 1):
                i = 2 * inner + row if dagger_a else 2 * row + inner
                j = 2 * col + inner if dagger_b else 2 * inner + col
                add(n, a[i], b[j], True)
                add(n, a[4 + i], b[4 + j], dagger_a != dagger_b)
                if dagger_a:
                    add(4 + n, a[i], b[4 + j], not dagger_b)
                    add(4 + n, a[4 + i], b[j], False)
                else:
                    add(4 + n, a[4 + i], b[j], True)
                    add(4 + n, a[i], b[4 + j], not dagger_b)
    return result


def sum_rows(parts):
    row = lax.broadcasted_iota(jnp.int32, parts[0].shape, 0)
    low = row < 4
    parts = [
        jnp.where(low, a, b) + pltpu.roll(jnp.where(low, b, a), 4, 0)
        for a, b in zip(parts[:4], parts[4:])
    ]
    for step in (2, 1):
        low = jnp.bitwise_and(row, step) == 0
        parts = [
            jnp.where(low, a + pltpu.roll(a, 8 - step, 0), b + pltpu.roll(b, step, 0))
            for a, b in zip(parts[:step], parts[step:])
        ]
    return parts[0]


class Place:
    def __init__(self):
        self.chan = lax.axis_index("chan")
        self.core = lax.axis_index("dir")
        self.blk = lax.axis_index("blk")
        self.first_lane = pl.multiple_of(self.core * PAIR, PAIR)
        self.last_core = self.chan // 2
        self.last_lane = pl.multiple_of(self.chan * RUN, RUN)

    def first_station(self, core):
        return pl.multiple_of((2 * self.blk + core) * RUN, RUN)

    def channel_of(self, slot, per_shard):
        bits = (0, 1 + 2 * self.core, 2, 3 - 2 * self.core)[slot // per_shard]
        return jnp.bitwise_xor(bits, self.chan) * per_shard + slot % per_shard


def onehot(station, first_station):
    local = jnp.where(station < BLOCK, station, station - first_station + RUN)
    rows = lax.broadcasted_iota(jnp.int32, (2 * RUN, station.shape[1]), 0)
    return jnp.where(rows == local, 1.0, 0.0).astype(jnp.bfloat16)


def split_rows(value, count):
    split = [p.astype(jnp.float32) for p in pieces(value, count)]
    missing = -count * value.shape[0] % 16
    if missing:
        split.append(jnp.zeros((missing, value.shape[1]), jnp.float32))
    return jnp.concatenate(split).astype(jnp.bfloat16)


def grams(coh):
    re, im = coh[:4], coh[4:]
    size = [a * a + b * b for a, b in zip(re, im)]

    def cross(i, j, k, l):
        real = re[i] * re[j] + im[i] * im[j] + re[k] * re[l] + im[k] * im[l]
        imag = re[i] * im[j] - im[i] * re[j] + re[k] * im[l] - im[k] * re[l]
        return [real + real, imag + imag]

    inner = [size[0] + size[2], size[1] + size[3]] + cross(0, 1, 2, 3)
    outer = [size[0] + size[1], size[2] + size[3]] + cross(2, 0, 3, 1)
    return inner + outer


def curvature_of(gain, gram):
    re, im = gain[:4], gain[4:]
    size = [a * a + b * b for a, b in zip(re, im)]
    real = re[0] * re[1] + im[0] * im[1] + re[2] * re[3] + im[2] * im[3]
    imag = im[0] * re[1] - re[0] * im[1] + im[2] * re[3] - re[2] * im[3]
    total = (size[0] + size[2]) * gram[0] + (size[1] + size[3]) * gram[1] + real * gram[2] - imag * gram[3]
    return jnp.maximum(total, 0.0)


def coherency_kernel(
    channels, pairs_at, positions_at, offsets_at, brightness_at, cluster_at, mask_at, seen_at, own_at,
    out, share, gram, hots, last_hots, mask, seen, own,
    pairs, positions, offsets, brightness, cluster, base, spin, parts, sems,
):
    copies = [
        pltpu.make_async_copy(source, target, sems.at[index])
        for index, (source, target) in enumerate(
            (
                (pairs_at, pairs),
                (positions_at, positions),
                (offsets_at, offsets),
                (brightness_at, brightness),
                (cluster_at, cluster),
                (mask_at, mask),
                (seen_at, seen),
                (own_at, own),
            )
        )
    ]
    for copy in copies:
        copy.start()
    for copy in copies[:5]:
        copy.wait()
    place = Place()
    window = place.first_station(place.core)
    table = jnp.concatenate([positions[:, 0:RUN], positions[:, pl.ds(window, RUN)]], axis=1)
    table = split_rows(table, 3)
    there = []
    for side in (0, 1):
        hots[side] = onehot(pairs[side, :, pl.ds(place.first_lane, PAIR)], window)
        last = pairs[side, :, pl.ds(place.last_lane, RUN)]
        last_hots[side] = onehot(last, place.first_station(place.last_core))
        found = dot_f32(table, hots[side])
        there.append(found[0:2] + found[2:4] + found[4:6])
    span = there[0] - there[1]
    sources = offsets.shape[1]
    columns = jnp.transpose(jnp.concatenate([offsets[...], jnp.zeros((6, sources))]))
    step = 16
    for start in range(0, sources, step):
        rows = slice(start, start + step)
        geometry = columns[rows, 0:1] * span[0:1] + columns[rows, 1:2] * span[1:2]
        c, s = turn_pair(geometry * (0.5 / channels))
        spin[0, rows], spin[1, rows] = c, s
        for _ in range((2 * channels).bit_length() - 1):
            twice = s + s
            c, s = 1.0 - twice * s, twice * c
        base[0, rows], base[1, rows] = c, s

    directions = out.shape[1] // 12
    second_run = lax.rem(place.chan, 2) == 1
    member = lax.broadcasted_iota(jnp.int32, (directions, sources), 0) == cluster[...]
    bright = jnp.concatenate([jnp.where(member, brightness[n : n + 1], 0.0) for n in range(4)])
    high, low = pieces(bright, 2)
    both = jnp.concatenate([high, low])
    half = 4 * directions

    def table_times(refs):
        wide = dot_f32(both, refs[0])
        return wide[:half] + wide[half:] + dot_f32(high, refs[1])

    for channel in range(channels):
        odd = channel % 2
        for start in range(0, sources, step):
            rows = slice(start, start + step)
            c, s = base[0, rows], base[1, rows]
            for index, value in enumerate((c, s)):
                for size, piece in enumerate(pieces(value, 2)):
                    parts[odd, index, size, rows] = piece
            if channel < channels - 1:
                dc, ds = spin[0, rows], spin[1, rows]
                base[0, rows] = c * dc - s * ds
                base[1, rows] = s * dc + c * ds
        found = [table_times((parts[odd, index, 0], parts[odd, index, 1])) for index in (0, 1)]
        out[channel, :half] = found[0]
        out[channel, half : 2 * half] = found[1]
        out[channel, 2 * half :] = found[0] - found[1]
        for index in (0, 1):
            mine = jnp.where(second_run, found[index][:, RUN:], found[index][:, :RUN])
            share[channel, half * index : half * (index + 1)] = mine
        entries = [found[n // 4][n % 4 * directions : (n % 4 + 1) * directions] for n in range(8)]
        for n, value in enumerate(grams(entries)):
            rows = slice(n * directions, (n + 1) * directions)
            gram[rows] = value if channel == 0 else gram[rows] + value
    for copy in copies[5:]:
        copy.wait()


def model_kernel(coherent, hots, own, other, jones, gather, predicted, model):
    place = Place()
    fill_table(place, jones, own, other)
    gather_gains(jones[...], hots, gather)
    for run in range(2):
        predict(coherent, gather, run, model, predicted)


def gather_gains(table, hots, gather):
    rows = table.shape[0]
    split = jnp.concatenate(pieces(table, 2))
    for side in (0, 1):
        found = dot_f32(split, hots[side])
        found = found[:rows] + found[rows:]
        for run in range(found.shape[1] // RUN):
            gather[side, run] = found[:, run * RUN : (run + 1) * RUN]


def gains_of(gather, side, run, h):
    return [gather[side, run, pl.ds(64 * h + n, 8, stride=8), :] for n in range(8)]


def coherent_of(coherent, channel, h, lanes, directions, count):
    return [
        coherent[channel, n * directions + 8 * h : n * directions + 8 * h + 8, lanes] for n in range(count)
    ]


def small_product(a, b, turned=False):
    order = ((0, 1), (2, 3)) if turned else ((0, 2), (1, 3))
    return [
        a[2 * row] * b[order[col][0]] + a[2 * row + 1] * b[order[col][1]] for row in (0, 1) for col in (0, 1)
    ]


def less(a, b):
    return [x - y for x, y in zip(a, b)]


def plus(a, b):
    return [x + y for x, y in zip(a, b)]


def model_parts(first, second, coh):
    re, im, mixed = coh[:4], coh[4:8], coh[8:]
    p1 = small_product(first[:4], re)
    p2 = small_product(first[4:8], im)
    p3 = small_product(first[8:], mixed)
    zr = less(p1, p2)
    zi = less(plus(p1, p2), p3)
    return (
        small_product(zr, second[:4], True)
        + small_product(zi, second[4:8], True)
        + small_product(plus(zr, zi), second[8:], True)
    )


def model_of(parts):
    a, b, d = parts[:4], parts[4:8], parts[8:]
    return plus(a, b) + plus(less(d, a), b)


def with_difference(matrix):
    return matrix + less(matrix[:4], matrix[4:])


def multiply_into(total, a, b, conj_b=False):
    real = a[0] * b[0]
    imag = a[1] * b[0]
    if total is not None:
        real, imag = total[0] + real, total[1] + imag
    if conj_b:
        return real + a[1] * b[1], imag - a[0] * b[1]
    return real - a[1] * b[1], imag + a[0] * b[1]


def fill_table(place, jones, own, other):
    count = own.shape[0] * own.shape[1]
    for ref, core in ((own, place.core), (other, 1 - place.core)):
        at = pl.ds(pl.multiple_of(core * count, count), count)
        jones[at, 0:RUN] = ref[:, :, 0:RUN].reshape(count, RUN)
        window = ref[:, :, pl.ds(place.first_station(place.core), RUN)]
        jones[at, RUN:] = window.reshape(count, RUN)


def predict(coherent, gather, run, model, predicted):
    channels = coherent.shape[0]
    directions = coherent.shape[1] // 12
    halves = directions // 8
    lanes = slice(run * RUN, (run + 1) * RUN)
    for h in range(halves):
        first_gain = with_difference(gains_of(gather, 0, run, h))
        second_gain = with_difference(gains_of(gather, 1, run, h))
        for channel in range(channels):
            coh = coherent_of(coherent, channel, h, lanes, directions, 12)
            part = model_parts(first_gain, second_gain, coh)
            if h > 0:
                part = [a + model[channel, n] for n, a in enumerate(part)]
            if h < halves - 1:
                for n in range(12):
                    model[channel, n] = part[n]
            else:
                predicted[run, channel] = sum_rows(model_of(part))


def iterate(place, coherent, gram, hots, shards, mask, gather, predicted, error, sums):
    directions = coherent.shape[1] // 12
    rows = 8 * directions
    halves = rows // 64
    weight = mask[:, pl.ds(place.first_lane, PAIR)].astype(jnp.float32)
    channels = coherent.shape[0]
    per_shard = shards[0].shape[1]
    for run in range(2):
        lanes = slice(run * RUN, (run + 1) * RUN)
        w = weight[:, lanes]
        at = pl.multiple_of(place.first_lane + run * RUN, RUN)
        for slot in range(channels):
            channel = place.channel_of(slot, per_shard)
            seen = shards[slot // per_shard][:, slot % per_shard, 0, pl.ds(at, RUN)]
            err = w * (seen - predicted[run, channel])
            error[channel, 0] = err
            error[channel, 1] = err + pltpu.roll(err, 4, 0)

        for h in range(halves):
            first_gain, second_gain = gains_of(gather, 0, run, h), gains_of(gather, 1, run, h)
            second = [None] * 4
            for i in (0, 1):
                zero = jnp.zeros((8, RUN), jnp.float32)
                p1, p2, p3 = [zero] * 8, [zero] * 8, [zero] * 8
                for channel in range(channels):
                    coh = coherent_of(coherent, channel, h, lanes, directions, 12)

                    def err(tile, n):
                        return jnp.broadcast_to(error[channel, tile, n : n + 1], (8, RUN))

                    for j in (0, 1):
                        er, ei, es = err(0, 2 * i + j), err(0, 4 + 2 * i + j), err(1, 2 * i + j)
                        for kl in range(4):
                            n = 4 * j + kl
                            p1[n] = p1[n] + er * coh[kl]
                            p2[n] = p2[n] + ei * coh[4 + kl]
                            p3[n] = p3[n] + es * coh[8 + kl]
                outer = list(zip(plus(p1, p2), plus(less(p3, p1), p2)))
                for l in (0, 1):
                    total = None
                    for j in (0, 1):
                        for k in (0, 1):
                            g = (second_gain[2 * j + k], second_gain[4 + 2 * j + k])
                            total = multiply_into(total, outer[4 * j + 2 * l + k], g)
                    for imag in (0, 1):
                        n = 4 * imag + 2 * i + l
                        sums[0, run, pl.ds(64 * h + n, 8, stride=8), :] = total[imag]
                for a in (0, 1):
                    for l in (0, 1):
                        for k in (0, 1):
                            g = (first_gain[2 * i + k], first_gain[4 + 2 * i + k])
                            second[2 * a + l] = multiply_into(
                                second[2 * a + l], g, outer[4 * a + 2 * k + l], conj_b=True
                            )
            for n in range(8):
                sums[1, run, pl.ds(64 * h + n, 8, stride=8), :] = second[n % 4][n // 4]
            form = [gram[n * directions + 8 * h : n * directions + 8 * h + 8, lanes] for n in range(8)]
            sums[0, run, rows + 8 * h : rows + 8 * h + 8] = w * curvature_of(second_gain, form[:4])
            sums[1, run, rows + 8 * h : rows + 8 * h + 8] = w * curvature_of(first_gain, form[4:])

    total = None
    height = sums.shape[2]
    for side in (0, 1):
        whole = jnp.concatenate([sums[side, run] for run in range(2)], axis=1)
        found = dot_f32(jnp.concatenate(pieces(whole, 2)), hots[side], 1)
        found = found[:height] + found[height:]
        total = found if total is None else total + found
    return total


def pack(total, rows):
    half = rows // 2
    low = jnp.concatenate([total[:half], total[rows : rows + half // 8]])
    high = jnp.concatenate([total[half:rows], total[rows + half // 8 :]])
    lane = lax.broadcasted_iota(jnp.int32, low.shape, 1)
    return jnp.where(lane < BLOCK, low, pltpu.roll(high, BLOCK, 1))


def unpack(packed):
    half = packed.shape[0] * 8 // 9
    turned = pltpu.roll(packed, BLOCK, 1)
    return jnp.concatenate([packed[:half], turned[:half], packed[half:], turned[half:]])


def update(jones, lanes, sums, keep=None):
    rows = jones.shape[0]
    for d in range(rows // 8):
        now = jones[8 * d : 8 * d + 8, lanes]
        ratio = STEP_SIZE / (sums[rows + d : rows + d + 1] + EPSILON)
        new = now + ratio * sums[8 * d : 8 * d + 8]
        if keep is not None:
            new = jnp.where(keep, new, now)
        jones[8 * d : 8 * d + 8, lanes] = new


def block_zero():
    return lax.broadcasted_iota(jnp.int32, (8, RUN), 1) < BLOCK


def first_kernel(
    mask, coherent, gram, hots, gather, predicted, s0, s1, s2, s3, packed, mine, error, sums
):
    place = Place()
    total = iterate(place, coherent, gram, hots, (s0, s1, s2, s3), mask, gather, predicted, error, sums)
    packed[...] = pack(total[:, :RUN], 8 * (coherent.shape[1] // 12))
    mine[...] = total[:, RUN:]


def block_sums(refs, held):
    here, over_core, over_blk, over_both = [ref[:held] for ref in refs]
    return unpack((here + over_core) + (over_blk + over_both))


def second_kernel(
    mask, coherent, gram, hots, before, mine, p0, p1, p2, p3, s0, s1, s2, s3,
    to_core, to_blk, to_both, jones, model, error, gather, predicted, sums,
):
    place = Place()
    held = p0.shape[0]
    jones[...] = before[...]
    update(jones, slice(0, RUN), block_sums((p0, p1, p2, p3), held), block_zero())
    update(jones, slice(RUN, None), mine[...])
    gather_gains(jones[...], hots, gather)
    for run in range(2):
        predict(coherent, gather, run, model, predicted)
    total = iterate(place, coherent, gram, hots, (s0, s1, s2, s3), mask, gather, predicted, error, sums)
    rows = jones.shape[0]
    half = rows // 2
    packed = pack(total[:, :RUN], rows)
    update(jones, slice(RUN, None), total[:, RUN:])
    to_core[:held] = packed
    to_blk[:held] = packed
    to_both[:held] = packed
    to_core[held:] = jones[:, RUN:]
    to_blk[held:] = jones[pl.ds(pl.multiple_of(place.core * half, half), half), RUN:]
    to_both[held:] = jones[pl.ds(pl.multiple_of((1 - place.core) * half, half), half), RUN:]


def last_kernel(
    mask, share, other_share, hots, before, p0, p1, p2, p3, s0, s1, s2, s3,
    residual, solved_at, jones, gather, solved, sem,
):
    place = Place()
    rows = before.shape[0]
    half = rows // 2
    held = p0.shape[0] - rows
    owned = place.last_core == place.core
    jones[:, 0:RUN] = before[:, 0:RUN]
    jones[:, RUN:] = jnp.where(owned, p0[held:], p1[held:])
    update(jones, slice(0, RUN), block_sums((p0, p1, p2, p3), held), block_zero())

    own_rows = pl.multiple_of(place.core * half, half)
    for ref, start, blk, core in (
        (p0, held + own_rows, place.blk, place.core),
        (p1, held + own_rows, place.blk, 1 - place.core),
        (p2, held, 1 - place.blk, place.core),
        (p3, held, 1 - place.blk, 1 - place.core),
    ):
        lanes = pl.ds(pl.multiple_of((2 * blk + core) * RUN, RUN), RUN)
        solved[:, :, lanes] = ref[pl.ds(pl.multiple_of(start, 8), half)].reshape(half // 8, 8, RUN)
    zero = jones[pl.ds(own_rows, half), 0:RUN].reshape(half // 8, 8, RUN)
    lane = lax.broadcasted_iota(jnp.int32, zero.shape, 2)
    solved[:, :, 0:RUN] = jnp.where(lane < BLOCK, zero, solved[:, :, 0:RUN])
    copy = pltpu.make_async_copy(solved, solved_at, sem)
    copy.start()

    gather_gains(jones[...], hots, gather)
    w = mask[:, pl.ds(place.last_lane, RUN)].astype(jnp.float32)
    shards = (s0, s1, s2, s3)
    channels = share.shape[0]
    per_shard = s0.shape[1]
    gains = [[gains_of(gather, side, 0, h) for h in range(rows // 64)] for side in (0, 1)]
    for slot in range(channels):
        channel = place.channel_of(slot, per_shard)
        part = None
        for h in range(rows // 64):
            coh = [
                jnp.where(owned, a, b)
                for a, b in zip(
                    coherent_of(share, channel, h, slice(0, RUN), rows // 8, 8),
                    coherent_of(other_share, channel, h, slice(0, RUN), rows // 8, 8),
                )
            ]
            part = product(product(gains[0][h], coh), gains[1][h], dagger_b=True, total=part)
        seen = shards[slot // per_shard][:, slot % per_shard, 0, pl.ds(place.last_lane, RUN)]
        residual[:, channel, 0] = w * (seen - sum_rows(part))
    copy.wait()


def call(kernel, out_shape, scratch, operands, flops, in_hbm=0, out_spaces=None):
    spaces = [pltpu.HBM] * in_hbm + [pltpu.VMEM] * (len(operands) - in_hbm)
    return pl.pallas_call(
        kernel,
        out_shape=out_shape,
        in_specs=[pl.BlockSpec(memory_space=space) for space in spaces],
        out_specs=tuple(
            pl.BlockSpec(memory_space=space) for space in out_spaces or [pltpu.VMEM] * len(out_shape)
        ),
        scratch_shapes=scratch,
        compiler_params=pltpu.CompilerParams(vmem_limit_bytes=40 << 20),
        cost_estimate=pl.CostEstimate(
            flops=flops,
            transcendentals=0,
            bytes_accessed=sum(x.size * x.dtype.itemsize for x in [*operands, *out_shape]),
        ),
    )(*[pltpu.with_memory_space_constraint(x, space) for x, space in zip(operands, spaces)])


def f32(*shape):
    return jax.ShapeDtypeStruct(shape, jnp.float32)


def bf16(*shape):
    return jax.ShapeDtypeStruct(shape, jnp.bfloat16)


def swap(x, axis, bit=1):
    return lax.ppermute(x, axis, [(i, i ^ bit) for i in range(lax.axis_size(axis))])


def from_three(core, blk, both):
    return swap(core, "dir"), swap(blk, "blk"), swap(both, ("blk", "dir"), 3)


def per_device_owned(
    visibilities,
    antenna_pairs,
    valid_mask,
    station_positions,
    source_offsets,
    brightness,
    source_cluster,
    jones_gains,
):
    relay_count = lax.axis_size("chan")
    channels = visibilities.shape[1] * relay_count
    half_directions = jones_gains.shape[0]
    directions = 2 * half_directions
    rows = 8 * directions
    sources = source_offsets.shape[1]

    other = swap(jones_gains, "dir")
    places = [(chan, core) for chan in range(relay_count) for core in range(2)]
    odd = lax.ppermute(
        visibilities,
        ("chan", "dir"),
        [(2 * chan + core, 2 * (chan ^ (1 + 2 * core)) + core) for chan, core in places],
    )
    even = swap(visibilities, "chan", 2)
    inputs = (antenna_pairs, station_positions, source_offsets, brightness, source_cluster[None, :])
    kept = (valid_mask, visibilities, jones_gains)
    held = (rows + directions) // 2
    table = f32(rows, 2 * RUN)
    gathered = f32(2, 2, rows, RUN)
    predictions = f32(2, channels, 8, RUN)
    model = pltpu.VMEM((channels, 12, 8, RUN), jnp.float32)
    scratch = [
        pltpu.VMEM((channels, 2, 8, RUN), jnp.float32),
        pltpu.VMEM((2, 2, rows + directions, RUN), jnp.float32),
    ]
    coherent, share, gram, hots, last_hots, mask, seen, own = call(
        functools.partial(coherency_kernel, channels),
        (
            f32(channels, 12 * directions, PAIR),
            f32(channels, 8 * directions, RUN),
            f32(8 * directions, PAIR),
            bf16(2, 2 * RUN, PAIR),
            bf16(2, 2 * RUN, RUN),
            *[jax.ShapeDtypeStruct(x.shape, x.dtype) for x in kept],
        ),
        [pltpu.VMEM(x.shape, x.dtype) for x in inputs]
        + [
            pltpu.VMEM((2, sources, PAIR), jnp.float32),
            pltpu.VMEM((2, sources, PAIR), jnp.float32),
            pltpu.VMEM((2, 2, 2, sources, PAIR), jnp.bfloat16),
            pltpu.SemaphoreType.DMA((len(inputs + kept),)),
        ],
        inputs + kept,
        8 * 10**10,
        len(inputs + kept),
    )
    odd, coherent, hots, share = lax.optimization_barrier((odd, coherent, hots, share))
    shards = [seen, odd, even, swap(odd, "dir")]
    other_share = swap(share, "dir")
    jones, gather, predicted = call(
        model_kernel,
        (table, gathered, predictions),
        [model],
        (coherent, hots, own, other),
        4 * 10**10,
    )
    packed, mine = call(
        first_kernel,
        (f32(held, RUN), f32(rows + directions, RUN)),
        scratch,
        (mask, coherent, gram, hots, gather, predicted, *shards),
        2 * 10**10,
    )
    sums = from_three(packed, packed, packed)
    to_core, to_blk, to_both, jones = call(
        second_kernel,
        (f32(held + rows, RUN), f32(held + rows // 2, RUN), f32(held + rows // 2, RUN), table),
        [
            model,
            scratch[0],
            pltpu.VMEM(gathered.shape, jnp.float32),
            pltpu.VMEM(predictions.shape, jnp.float32),
            scratch[1],
        ],
        (mask, coherent, gram, hots, jones, mine, packed, *sums, *shards),
        4 * 10**10,
    )
    solved = f32(half_directions, 8, station_positions.shape[1])
    return call(
        last_kernel,
        (f32(8, channels, 1, RUN), solved),
        [
            pltpu.VMEM((rows, 2 * RUN), jnp.float32),
            pltpu.VMEM((2, 1, rows, RUN), jnp.float32),
            pltpu.VMEM(solved.shape, jnp.float32),
            pltpu.SemaphoreType.DMA,
        ],
        (
            mask, share, other_share, last_hots, jones,
            to_core, *from_three(to_core, to_blk, to_both), *shards,
        ),
        2 * 10**10,
        0,
        (pltpu.VMEM, pltpu.HBM),
    )


def owned_layout(mesh, shapes):
    sizes = mesh.shape
    owners = sizes["chan"] * sizes["blk"]
    visibilities, pairs, jones = shapes
    return (
        owners == BLOCKS
        and sizes["blk"] == 2
        and sizes["dir"] == 2
        and sizes["chan"] == 4
        and pairs[1] * pairs[2] == owners * RUN
        and jones[0] == 16
        and jones[2] == BLOCKS * BLOCK
        and visibilities[1] % sizes["chan"] == 0
        and visibilities[1] & (visibilities[1] - 1) == 0
    )


def solution(mesh):
    in_specs = (
        P("groups", "chan", "blk", None),
        P(None, "blk", None),
        P("blk", "groups"),
        P(),
        P(),
        P(),
        P(),
        P("dir", "groups", None),
    )
    out_specs = (P("groups", None, "blk", "chan"), P("dir", "groups", None))

    def run(*arrays):
        owned = owned_layout(mesh, (arrays[0].shape, arrays[1].shape, arrays[7].shape))
        body = per_device_owned if owned else per_device
        return jax.shard_map(
            body, mesh=mesh, in_specs=in_specs, out_specs=out_specs, check_vma=False
        )(*arrays)

    return run
```

```python
import functools
import math

import jax
import jax.numpy as jnp
from jax import lax
from jax.experimental import pallas as pl
from jax.experimental.pallas import tpu as pltpu
from jax.sharding import PartitionSpec as P

ITERS = 2


TWO_PI = 2.0 * math.pi
STEP_SIZE = 0.3
EPSILON = 1e-06
HIGHEST = lax.Precision.HIGHEST


def jones_product(former, latter):
    real_list = []
    imag_list = []
    for row_number in (0, 1):
        for column in (0, 1):
            real_list.append(
                former[2 * row_number] * latter[column]
                - former[4 + 2 * row_number] * latter[4 + column]
                + former[2 * row_number + 1] * latter[2 + column]
                - former[5 + 2 * row_number] * latter[6 + column]
            )
            imag_list.append(
                former[2 * row_number] * latter[4 + column]
                + former[4 + 2 * row_number] * latter[column]
                + former[2 * row_number + 1] * latter[6 + column]
                + former[5 + 2 * row_number] * latter[2 + column]
            )
    return jnp.stack(real_list + imag_list)


def adjoint(matrix):
    return jnp.stack(
        [matrix[0], matrix[2], matrix[1], matrix[3], -matrix[4], -matrix[6], -matrix[5], -matrix[7]]
    )


def source_table(brightness, source_cluster, direction_ids):
    member = (source_cluster[None, :] == direction_ids[:, None]).astype(jnp.float32)
    return (brightness[:, None, :] * member[None, :, :]).reshape(
        4 * direction_ids.shape[0], brightness.shape[1]
    )


def coherency(bright_table, geometry, scales):
    phase_grid = (TWO_PI * scales)[None, :, None] * geometry[:, None, :]
    phases_flat = phase_grid.reshape(geometry.shape[0], -1)
    real_block = jnp.dot(bright_table, jnp.cos(phases_flat), precision=HIGHEST)
    imag_block = -jnp.dot(bright_table, jnp.sin(phases_flat), precision=HIGHEST)
    dir_count = bright_table.shape[0] // 4
    return jnp.concatenate([real_block, imag_block], axis=0).reshape(
        8, dir_count, scales.shape[0], geometry.shape[1]
    )


def per_device(
    visibilities,
    antenna_pairs,
    valid_mask,
    station_positions,
    source_offsets,
    brightness,
    source_cluster,
    jones_gains,
):
    relay_count = lax.axis_size("chan")
    base_count = antenna_pairs.shape[2] // relay_count
    station_count = station_positions.shape[1]
    offset = lax.axis_index("chan") * base_count
    own_pairs = lax.dynamic_slice_in_dim(antenna_pairs[:, 0], offset, base_count, 1)
    first_station = own_pairs[0]
    second_station = own_pairs[1]
    weight_row = lax.dynamic_slice_in_dim(valid_mask[0], offset, base_count, 0).astype(jnp.float32)
    regrouped = lax.all_to_all(visibilities, "chan", split_axis=3, concat_axis=1, tiled=True)[
        :, :, 0, :
    ]
    total_channels = regrouped.shape[1]
    own_directions = jones_gains.shape[0]
    channel_ids = jnp.arange(total_channels)
    gains_now = jones_gains
    direction_ids = lax.axis_index("dir") * own_directions + jnp.arange(own_directions)
    local_channels = regrouped.shape[1]
    scales = 1.0 + 0.5 * channel_ids.astype(jnp.float32) / total_channels
    u_coord = station_positions[0][first_station] - station_positions[0][second_station]
    v_coord = station_positions[1][first_station] - station_positions[1][second_station]
    geometry = (
        source_offsets[0][:, None] * u_coord[None, :]
        + source_offsets[1][:, None] * v_coord[None, :]
    )
    bright_table = source_table(brightness, source_cluster, direction_ids)
    group_size = math.gcd(local_channels, max(1, 2048 // base_count))
    group_count = local_channels // group_size
    scale_groups = scales.reshape(group_count, group_size)
    onehot_first = (first_station[:, None] == jnp.arange(station_count)[None, :]).astype(
        jnp.float32
    )
    onehot_second = (second_station[:, None] == jnp.arange(station_count)[None, :]).astype(
        jnp.float32
    )

    def station_gains(gains_current):
        gain_first = jnp.take(gains_current, first_station, axis=2).transpose(1, 0, 2)[
            :, :, None, :
        ]
        gain_second = jnp.take(gains_current, second_station, axis=2).transpose(1, 0, 2)[
            :, :, None, :
        ]
        return (gain_first, gain_second)

    def residual_of(gains_current):
        gain_first, gain_second = station_gains(gains_current)

        def residual_one_group(scale_group):
            coherent = coherency(bright_table, geometry, scale_group)
            return jnp.sum(
                jones_product(jones_product(gain_first, coherent), adjoint(gain_second)), axis=1
            )

        partial_model = jnp.moveaxis(lax.map(residual_one_group, scale_groups), 0, 1).reshape(
            8, local_channels, base_count
        )
        model_vis = lax.psum(partial_model, "dir")
        return weight_row * (regrouped - model_vis)

    for iteration in range(ITERS):
        residual_now = residual_of(gains_now)
        updated_gain_first, updated_gain_second = station_gains(gains_now)
        resid_groups = jnp.moveaxis(
            residual_now.reshape(8, group_count, group_size, base_count), 1, 0
        )
        dir_count = gains_now.shape[0]

        def updated_one_group(running, inputs):
            scale_group, resid_group = inputs
            coherent = coherency(bright_table, geometry, scale_group)
            toward_second = jones_product(updated_gain_second, adjoint(coherent))
            toward_first = jones_product(updated_gain_first, coherent)
            grad_first = jnp.sum(jones_product(resid_group[:, None], toward_second), axis=2)
            grad_second = jnp.sum(
                jones_product(adjoint(resid_group)[:, None], toward_first), axis=2
            )
            curv_first = jnp.sum(toward_second * toward_second, axis=(0, 2))
            curv_second = jnp.sum(toward_first * toward_first, axis=(0, 2))
            return (
                (
                    running[0] + grad_first,
                    running[1] + grad_second,
                    running[2] + curv_first,
                    running[3] + curv_second,
                ),
                None,
            )

        zero_sums = (
            jnp.zeros((8, dir_count, base_count), jnp.float32),
            jnp.zeros((8, dir_count, base_count), jnp.float32),
            jnp.zeros((dir_count, base_count), jnp.float32),
            jnp.zeros((dir_count, base_count), jnp.float32),
        )
        totals, ignored = lax.scan(updated_one_group, zero_sums, (scale_groups, resid_groups))
        grad_station = jnp.einsum(
            "cdb,bs->dcs", totals[0], onehot_first, precision=HIGHEST
        ) + jnp.einsum("cdb,bs->dcs", totals[1], onehot_second, precision=HIGHEST)
        curv_station = jnp.dot(weight_row * totals[2], onehot_first, precision=HIGHEST) + jnp.dot(
            weight_row * totals[3], onehot_second, precision=HIGHEST
        )
        grad_station, curv_station = lax.psum((grad_station, curv_station), ("chan", "blk"))
        gains_now = gains_now + STEP_SIZE * grad_station / (curv_station[:, None, :] + EPSILON)
    residual_now = residual_of(gains_now)
    return (residual_now[:, :, None, :], gains_now)


COS_TERMS = (
    0.9999999890590228,
    -19.739204499454,
    64.93911745989914,
    -85.45013953093448,
    60.16763095128989,
    -25.96759924954187,
    6.528658162606979,
)
SIN_TERMS = (
    6.283185302511502,
    -41.34170040531754,
    81.6051313857969,
    -76.70301535383193,
    42.02592698564183,
    -14.899846667160109,
    3.2381375090822355,
)
RUN = 128
BLOCK = 64
BLOCKS = 8
PAIR = 2 * RUN


def pieces(value, count):
    result = []
    for index in range(count):
        piece = value.astype(jnp.bfloat16)
        result.append(piece)
        if index < count - 1:
            value = value - piece.astype(jnp.float32)
    return result


def dot_f32(left, right, contract_right=0):
    return lax.dot_general(
        left,
        right,
        (((1,), (contract_right,)), ((), ())),
        preferred_element_type=jnp.float32,
    )


def horner(terms, x):
    total = jnp.full_like(x, terms[-1])
    for term in terms[-2::-1]:
        total = total * x + term
    return total


def turn_pair(turns):
    rest = turns - jnp.round(turns)
    square = rest * rest
    return horner(COS_TERMS, square), horner([-term for term in SIN_TERMS], square) * rest


def product(a, b, dagger_a=False, dagger_b=False, total=None):
    result = [None] * 8 if total is None else list(total)

    def add(n, x, y, positive):
        term = x * y
        if result[n] is None:
            result[n] = term if positive else -term
        else:
            result[n] = result[n] + term if positive else result[n] - term

    for row in (0, 1):
        for col in (0, 1):
            n = 2 * row + col
            for inner in (0, 1):
                i = 2 * inner + row if dagger_a else 2 * row + inner
                j = 2 * col + inner if dagger_b else 2 * inner + col
                add(n, a[i], b[j], True)
                add(n, a[4 + i], b[4 + j], dagger_a != dagger_b)
                if dagger_a:
                    add(4 + n, a[i], b[4 + j], not dagger_b)
                    add(4 + n, a[4 + i], b[j], False)
                else:
                    add(4 + n, a[4 + i], b[j], True)
                    add(4 + n, a[i], b[4 + j], not dagger_b)
    return result


def sum_rows(parts):
    row = lax.broadcasted_iota(jnp.int32, parts[0].shape, 0)
    low = row < 4
    parts = [
        jnp.where(low, a, b) + pltpu.roll(jnp.where(low, b, a), 4, 0)
        for a, b in zip(parts[:4], parts[4:])
    ]
    for step in (2, 1):
        low = jnp.bitwise_and(row, step) == 0
        parts = [
            jnp.where(low, a + pltpu.roll(a, 8 - step, 0), b + pltpu.roll(b, step, 0))
            for a, b in zip(parts[:step], parts[step:])
        ]
    return parts[0]


class Place:
    def __init__(self):
        self.chan = lax.axis_index("chan")
        self.core = lax.axis_index("dir")
        self.blk = lax.axis_index("blk")
        self.first_lane = pl.multiple_of(self.core * PAIR, PAIR)
        self.last_core = self.chan // 2
        self.last_lane = pl.multiple_of(self.chan * RUN, RUN)

    def first_station(self, core):
        return pl.multiple_of((2 * self.blk + core) * RUN, RUN)

    def channel_of(self, slot, per_shard):
        bits = (0, 1 + 2 * self.core, 2, 3 - 2 * self.core)[slot // per_shard]
        return jnp.bitwise_xor(bits, self.chan) * per_shard + slot % per_shard


def onehot(station, first_station):
    local = jnp.where(station < BLOCK, station, station - first_station + RUN)
    rows = lax.broadcasted_iota(jnp.int32, (2 * RUN, station.shape[1]), 0)
    return jnp.where(rows == local, 1.0, 0.0).astype(jnp.bfloat16)


def split_rows(value, count):
    split = [p.astype(jnp.float32) for p in pieces(value, count)]
    missing = -count * value.shape[0] % 16
    if missing:
        split.append(jnp.zeros((missing, value.shape[1]), jnp.float32))
    return jnp.concatenate(split).astype(jnp.bfloat16)


def grams(coh):
    re, im = coh[:4], coh[4:]
    size = [a * a + b * b for a, b in zip(re, im)]

    def cross(i, j, k, l):
        real = re[i] * re[j] + im[i] * im[j] + re[k] * re[l] + im[k] * im[l]
        imag = re[i] * im[j] - im[i] * re[j] + re[k] * im[l] - im[k] * re[l]
        return [real + real, imag + imag]

    inner = [size[0] + size[2], size[1] + size[3]] + cross(0, 1, 2, 3)
    outer = [size[0] + size[1], size[2] + size[3]] + cross(2, 0, 3, 1)
    return inner + outer


def curvature_of(gain, gram):
    re, im = gain[:4], gain[4:]
    size = [a * a + b * b for a, b in zip(re, im)]
    real = re[0] * re[1] + im[0] * im[1] + re[2] * re[3] + im[2] * im[3]
    imag = im[0] * re[1] - re[0] * im[1] + im[2] * re[3] - re[2] * im[3]
    total = (size[0] + size[2]) * gram[0] + (size[1] + size[3]) * gram[1] + real * gram[2] - imag * gram[3]
    return jnp.maximum(total, 0.0)


def coherency_kernel(
    channels, pairs_at, positions_at, offsets_at, brightness_at, cluster_at, mask_at, seen_at, own_at,
    out, share, gram, hots, last_hots, mask, seen, own,
    pairs, positions, offsets, brightness, cluster, base, spin, parts, sems,
):
    copies = [
        pltpu.make_async_copy(source, target, sems.at[index])
        for index, (source, target) in enumerate(
            (
                (pairs_at, pairs),
                (positions_at, positions),
                (offsets_at, offsets),
                (brightness_at, brightness),
                (cluster_at, cluster),
                (mask_at, mask),
                (seen_at, seen),
                (own_at, own),
            )
        )
    ]
    for copy in copies:
        copy.start()
    for copy in copies[:5]:
        copy.wait()
    place = Place()
    window = place.first_station(place.core)
    table = jnp.concatenate([positions[:, 0:RUN], positions[:, pl.ds(window, RUN)]], axis=1)
    table = split_rows(table, 3)
    there = []
    for side in (0, 1):
        hots[side] = onehot(pairs[side, :, pl.ds(place.first_lane, PAIR)], window)
        last = pairs[side, :, pl.ds(place.last_lane, RUN)]
        last_hots[side] = onehot(last, place.first_station(place.last_core))
        found = dot_f32(table, hots[side])
        there.append(found[0:2] + found[2:4] + found[4:6])
    span = there[0] - there[1]
    sources = offsets.shape[1]
    columns = jnp.transpose(jnp.concatenate([offsets[...], jnp.zeros((6, sources))]))
    step = 32
    for start in range(0, sources, step):
        rows = slice(start, start + step)
        geometry = columns[rows, 0:1] * span[0:1] + columns[rows, 1:2] * span[1:2]
        c, s = turn_pair(geometry * (0.5 / channels))
        spin[0, rows], spin[1, rows] = c, s
        for _ in range((2 * channels).bit_length() - 1):
            twice = s + s
            c, s = 1.0 - twice * s, twice * c
        base[0, rows], base[1, rows] = c, s

    directions = out.shape[1] // 12
    second_run = lax.rem(place.chan, 2) == 1
    member = lax.broadcasted_iota(jnp.int32, (directions, sources), 0) == cluster[...]
    bright = jnp.concatenate([jnp.where(member, brightness[n : n + 1], 0.0) for n in range(4)])
    high, low = pieces(bright, 2)
    both = jnp.concatenate([high, low])
    half = 4 * directions

    def table_times(refs):
        wide = dot_f32(both, refs[0])
        return wide[:half] + wide[half:] + dot_f32(high, refs[1])

    for channel in range(channels):
        odd = channel % 2
        for start in range(0, sources, step):
            rows = slice(start, start + step)
            c, s = base[0, rows], base[1, rows]
            for index, value in enumerate((c, s)):
                for size, piece in enumerate(pieces(value, 2)):
                    parts[odd, index, size, rows] = piece
            if channel < channels - 1:
                dc, ds = spin[0, rows], spin[1, rows]
                base[0, rows] = c * dc - s * ds
                base[1, rows] = s * dc + c * ds
        found = [table_times((parts[odd, index, 0], parts[odd, index, 1])) for index in (0, 1)]
        out[channel, :half] = found[0]
        out[channel, half : 2 * half] = found[1]
        out[channel, 2 * half :] = found[0] - found[1]
        for index in (0, 1):
            mine = jnp.where(second_run, found[index][:, RUN:], found[index][:, :RUN])
            share[channel, half * index : half * (index + 1)] = mine
        entries = [found[n // 4][n % 4 * directions : (n % 4 + 1) * directions] for n in range(8)]
        for n, value in enumerate(grams(entries)):
            rows = slice(n * directions, (n + 1) * directions)
            gram[rows] = value if channel == 0 else gram[rows] + value
    for copy in copies[5:]:
        copy.wait()


def model_kernel(coherent, hots, own, other, jones, gather, predicted, model):
    place = Place()
    fill_table(place, jones, own, other)
    gather_gains(jones[...], hots, gather)
    for run in range(2):
        predict(coherent, gather, run, model, predicted)


def gather_gains(table, hots, gather):
    rows = table.shape[0]
    split = jnp.concatenate(pieces(table, 2))
    for side in (0, 1):
        found = dot_f32(split, hots[side])
        found = found[:rows] + found[rows:]
        for run in range(found.shape[1] // RUN):
            gather[side, run] = found[:, run * RUN : (run + 1) * RUN]


def gains_of(gather, side, run, h):
    return [gather[side, run, pl.ds(64 * h + n, 8, stride=8), :] for n in range(8)]


def coherent_of(coherent, channel, h, lanes, directions, count):
    return [
        coherent[channel, n * directions + 8 * h : n * directions + 8 * h + 8, lanes] for n in range(count)
    ]


def small_product(a, b, turned=False):
    order = ((0, 1), (2, 3)) if turned else ((0, 2), (1, 3))
    return [
        a[2 * row] * b[order[col][0]] + a[2 * row + 1] * b[order[col][1]] for row in (0, 1) for col in (0, 1)
    ]


def less(a, b):
    return [x - y for x, y in zip(a, b)]


def plus(a, b):
    return [x + y for x, y in zip(a, b)]


def model_parts(first, second, coh):
    re, im, mixed = coh[:4], coh[4:8], coh[8:]
    p1 = small_product(first[:4], re)
    p2 = small_product(first[4:8], im)
    p3 = small_product(first[8:], mixed)
    zr = less(p1, p2)
    zi = less(plus(p1, p2), p3)
    return (
        small_product(zr, second[:4], True)
        + small_product(zi, second[4:8], True)
        + small_product(plus(zr, zi), second[8:], True)
    )


def model_of(parts):
    a, b, d = parts[:4], parts[4:8], parts[8:]
    return plus(a, b) + plus(less(d, a), b)


def with_difference(matrix):
    return matrix + less(matrix[:4], matrix[4:])


def multiply_into(total, a, b, conj_b=False):
    real = a[0] * b[0]
    imag = a[1] * b[0]
    if total is not None:
        real, imag = total[0] + real, total[1] + imag
    if conj_b:
        return real + a[1] * b[1], imag - a[0] * b[1]
    return real - a[1] * b[1], imag + a[0] * b[1]


def fill_table(place, jones, own, other):
    count = own.shape[0] * own.shape[1]
    for ref, core in ((own, place.core), (other, 1 - place.core)):
        at = pl.ds(pl.multiple_of(core * count, count), count)
        jones[at, 0:RUN] = ref[:, :, 0:RUN].reshape(count, RUN)
        window = ref[:, :, pl.ds(place.first_station(place.core), RUN)]
        jones[at, RUN:] = window.reshape(count, RUN)


def predict(coherent, gather, run, model, predicted):
    channels = coherent.shape[0]
    directions = coherent.shape[1] // 12
    halves = directions // 8
    lanes = slice(run * RUN, (run + 1) * RUN)
    for h in range(halves):
        first_gain = with_difference(gains_of(gather, 0, run, h))
        second_gain = with_difference(gains_of(gather, 1, run, h))
        for channel in range(channels):
            coh = coherent_of(coherent, channel, h, lanes, directions, 12)
            part = model_parts(first_gain, second_gain, coh)
            if h > 0:
                part = [a + model[channel, n] for n, a in enumerate(part)]
            if h < halves - 1:
                for n in range(12):
                    model[channel, n] = part[n]
            else:
                predicted[run, channel] = sum_rows(model_of(part))


def iterate(place, coherent, gram, hots, shards, mask, gather, predicted, error, sums):
    directions = coherent.shape[1] // 12
    rows = 8 * directions
    halves = rows // 64
    weight = mask[:, pl.ds(place.first_lane, PAIR)].astype(jnp.float32)
    channels = coherent.shape[0]
    per_shard = shards[0].shape[1]
    for run in range(2):
        lanes = slice(run * RUN, (run + 1) * RUN)
        w = weight[:, lanes]
        at = pl.multiple_of(place.first_lane + run * RUN, RUN)
        for slot in range(channels):
            channel = place.channel_of(slot, per_shard)
            seen = shards[slot // per_shard][:, slot % per_shard, 0, pl.ds(at, RUN)]
            err = w * (seen - predicted[run, channel])
            error[channel, 0] = err
            error[channel, 1] = err + pltpu.roll(err, 4, 0)

        for h in range(halves):
            first_gain, second_gain = gains_of(gather, 0, run, h), gains_of(gather, 1, run, h)
            second = [None] * 4
            for i in (0, 1):
                zero = jnp.zeros((8, RUN), jnp.float32)
                p1, p2, p3 = [zero] * 8, [zero] * 8, [zero] * 8
                for channel in range(channels):
                    coh = coherent_of(coherent, channel, h, lanes, directions, 12)

                    def err(tile, n):
                        return jnp.broadcast_to(error[channel, tile, n : n + 1], (8, RUN))

                    for j in (0, 1):
                        er, ei, es = err(0, 2 * i + j), err(0, 4 + 2 * i + j), err(1, 2 * i + j)
                        for kl in range(4):
                            n = 4 * j + kl
                            p1[n] = p1[n] + er * coh[kl]
                            p2[n] = p2[n] + ei * coh[4 + kl]
                            p3[n] = p3[n] + es * coh[8 + kl]
                outer = list(zip(plus(p1, p2), plus(less(p3, p1), p2)))
                for l in (0, 1):
                    total = None
                    for j in (0, 1):
                        for k in (0, 1):
                            g = (second_gain[2 * j + k], second_gain[4 + 2 * j + k])
                            total = multiply_into(total, outer[4 * j + 2 * l + k], g)
                    for imag in (0, 1):
                        n = 4 * imag + 2 * i + l
                        sums[0, run, pl.ds(64 * h + n, 8, stride=8), :] = total[imag]
                for a in (0, 1):
                    for l in (0, 1):
                        for k in (0, 1):
                            g = (first_gain[2 * i + k], first_gain[4 + 2 * i + k])
                            second[2 * a + l] = multiply_into(
                                second[2 * a + l], g, outer[4 * a + 2 * k + l], conj_b=True
                            )
            for n in range(8):
                sums[1, run, pl.ds(64 * h + n, 8, stride=8), :] = second[n % 4][n // 4]
            form = [gram[n * directions + 8 * h : n * directions + 8 * h + 8, lanes] for n in range(8)]
            sums[0, run, rows + 8 * h : rows + 8 * h + 8] = w * curvature_of(second_gain, form[:4])
            sums[1, run, rows + 8 * h : rows + 8 * h + 8] = w * curvature_of(first_gain, form[4:])

    total = None
    height = sums.shape[2]
    for side in (0, 1):
        whole = jnp.concatenate([sums[side, run] for run in range(2)], axis=1)
        found = dot_f32(jnp.concatenate(pieces(whole, 2)), hots[side], 1)
        found = found[:height] + found[height:]
        total = found if total is None else total + found
    return total


def pack(total, rows):
    half = rows // 2
    low = jnp.concatenate([total[:half], total[rows : rows + half // 8]])
    high = jnp.concatenate([total[half:rows], total[rows + half // 8 :]])
    lane = lax.broadcasted_iota(jnp.int32, low.shape, 1)
    return jnp.where(lane < BLOCK, low, pltpu.roll(high, BLOCK, 1))


def unpack(packed):
    half = packed.shape[0] * 8 // 9
    turned = pltpu.roll(packed, BLOCK, 1)
    return jnp.concatenate([packed[:half], turned[:half], packed[half:], turned[half:]])


def update(jones, lanes, sums, keep=None):
    rows = jones.shape[0]
    for d in range(rows // 8):
        now = jones[8 * d : 8 * d + 8, lanes]
        ratio = STEP_SIZE / (sums[rows + d : rows + d + 1] + EPSILON)
        new = now + ratio * sums[8 * d : 8 * d + 8]
        if keep is not None:
            new = jnp.where(keep, new, now)
        jones[8 * d : 8 * d + 8, lanes] = new


def block_zero():
    return lax.broadcasted_iota(jnp.int32, (8, RUN), 1) < BLOCK


def first_kernel(
    mask, coherent, gram, hots, gather, predicted, s0, s1, s2, s3, packed, mine, error, sums
):
    place = Place()
    total = iterate(place, coherent, gram, hots, (s0, s1, s2, s3), mask, gather, predicted, error, sums)
    packed[...] = pack(total[:, :RUN], 8 * (coherent.shape[1] // 12))
    mine[...] = total[:, RUN:]


def block_sums(refs, held):
    here, over_core, over_blk, over_both = [ref[:held] for ref in refs]
    return unpack((here + over_core) + (over_blk + over_both))


def second_kernel(
    mask, coherent, gram, hots, before, mine, p0, p1, p2, p3, s0, s1, s2, s3,
    to_core, to_blk, to_both, jones, model, error, gather, predicted, sums,
):
    place = Place()
    held = p0.shape[0]
    jones[...] = before[...]
    update(jones, slice(0, RUN), block_sums((p0, p1, p2, p3), held), block_zero())
    update(jones, slice(RUN, None), mine[...])
    gather_gains(jones[...], hots, gather)
    for run in range(2):
        predict(coherent, gather, run, model, predicted)
    total = iterate(place, coherent, gram, hots, (s0, s1, s2, s3), mask, gather, predicted, error, sums)
    rows = jones.shape[0]
    half = rows // 2
    packed = pack(total[:, :RUN], rows)
    update(jones, slice(RUN, None), total[:, RUN:])
    to_core[:held] = packed
    to_blk[:held] = packed
    to_both[:held] = packed
    to_core[held:] = jones[:, RUN:]
    to_blk[held:] = jones[pl.ds(pl.multiple_of(place.core * half, half), half), RUN:]
    to_both[held:] = jones[pl.ds(pl.multiple_of((1 - place.core) * half, half), half), RUN:]


def last_kernel(
    mask, share, other_share, hots, before, p0, p1, p2, p3, s0, s1, s2, s3,
    residual, solved_at, jones, gather, solved, sem,
):
    place = Place()
    rows = before.shape[0]
    half = rows // 2
    held = p0.shape[0] - rows
    owned = place.last_core == place.core
    jones[:, 0:RUN] = before[:, 0:RUN]
    jones[:, RUN:] = jnp.where(owned, p0[held:], p1[held:])
    update(jones, slice(0, RUN), block_sums((p0, p1, p2, p3), held), block_zero())

    own_rows = pl.multiple_of(place.core * half, half)
    for ref, start, blk, core in (
        (p0, held + own_rows, place.blk, place.core),
        (p1, held + own_rows, place.blk, 1 - place.core),
        (p2, held, 1 - place.blk, place.core),
        (p3, held, 1 - place.blk, 1 - place.core),
    ):
        lanes = pl.ds(pl.multiple_of((2 * blk + core) * RUN, RUN), RUN)
        solved[:, :, lanes] = ref[pl.ds(pl.multiple_of(start, 8), half)].reshape(half // 8, 8, RUN)
    zero = jones[pl.ds(own_rows, half), 0:RUN].reshape(half // 8, 8, RUN)
    lane = lax.broadcasted_iota(jnp.int32, zero.shape, 2)
    solved[:, :, 0:RUN] = jnp.where(lane < BLOCK, zero, solved[:, :, 0:RUN])
    copy = pltpu.make_async_copy(solved, solved_at, sem)
    copy.start()

    gather_gains(jones[...], hots, gather)
    w = mask[:, pl.ds(place.last_lane, RUN)].astype(jnp.float32)
    shards = (s0, s1, s2, s3)
    channels = share.shape[0]
    per_shard = s0.shape[1]
    gains = [[gains_of(gather, side, 0, h) for h in range(rows // 64)] for side in (0, 1)]
    for slot in range(channels):
        channel = place.channel_of(slot, per_shard)
        part = None
        for h in range(rows // 64):
            coh = [
                jnp.where(owned, a, b)
                for a, b in zip(
                    coherent_of(share, channel, h, slice(0, RUN), rows // 8, 8),
                    coherent_of(other_share, channel, h, slice(0, RUN), rows // 8, 8),
                )
            ]
            part = product(product(gains[0][h], coh), gains[1][h], dagger_b=True, total=part)
        seen = shards[slot // per_shard][:, slot % per_shard, 0, pl.ds(place.last_lane, RUN)]
        residual[:, channel, 0] = w * (seen - sum_rows(part))
    copy.wait()


def call(kernel, out_shape, scratch, operands, flops, in_hbm=0, out_spaces=None):
    spaces = [pltpu.HBM] * in_hbm + [pltpu.VMEM] * (len(operands) - in_hbm)
    return pl.pallas_call(
        kernel,
        out_shape=out_shape,
        in_specs=[pl.BlockSpec(memory_space=space) for space in spaces],
        out_specs=tuple(
            pl.BlockSpec(memory_space=space) for space in out_spaces or [pltpu.VMEM] * len(out_shape)
        ),
        scratch_shapes=scratch,
        compiler_params=pltpu.CompilerParams(vmem_limit_bytes=40 << 20),
        cost_estimate=pl.CostEstimate(
            flops=flops,
            transcendentals=0,
            bytes_accessed=sum(x.size * x.dtype.itemsize for x in [*operands, *out_shape]),
        ),
    )(*[pltpu.with_memory_space_constraint(x, space) for x, space in zip(operands, spaces)])


def f32(*shape):
    return jax.ShapeDtypeStruct(shape, jnp.float32)


def bf16(*shape):
    return jax.ShapeDtypeStruct(shape, jnp.bfloat16)


def swap(x, axis, bit=1):
    return lax.ppermute(x, axis, [(i, i ^ bit) for i in range(lax.axis_size(axis))])


def from_three(core, blk, both):
    return swap(core, "dir"), swap(blk, "blk"), swap(both, ("blk", "dir"), 3)


def per_device_owned(
    visibilities,
    antenna_pairs,
    valid_mask,
    station_positions,
    source_offsets,
    brightness,
    source_cluster,
    jones_gains,
):
    relay_count = lax.axis_size("chan")
    channels = visibilities.shape[1] * relay_count
    half_directions = jones_gains.shape[0]
    directions = 2 * half_directions
    rows = 8 * directions
    sources = source_offsets.shape[1]

    other = swap(jones_gains, "dir")
    places = [(chan, core) for chan in range(relay_count) for core in range(2)]
    odd = lax.ppermute(
        visibilities,
        ("chan", "dir"),
        [(2 * chan + core, 2 * (chan ^ (1 + 2 * core)) + core) for chan, core in places],
    )
    even = swap(visibilities, "chan", 2)
    inputs = (antenna_pairs, station_positions, source_offsets, brightness, source_cluster[None, :])
    kept = (valid_mask, visibilities, jones_gains)
    held = (rows + directions) // 2
    table = f32(rows, 2 * RUN)
    gathered = f32(2, 2, rows, RUN)
    predictions = f32(2, channels, 8, RUN)
    model = pltpu.VMEM((channels, 12, 8, RUN), jnp.float32)
    scratch = [
        pltpu.VMEM((channels, 2, 8, RUN), jnp.float32),
        pltpu.VMEM((2, 2, rows + directions, RUN), jnp.float32),
    ]
    coherent, share, gram, hots, last_hots, mask, seen, own = call(
        functools.partial(coherency_kernel, channels),
        (
            f32(channels, 12 * directions, PAIR),
            f32(channels, 8 * directions, RUN),
            f32(8 * directions, PAIR),
            bf16(2, 2 * RUN, PAIR),
            bf16(2, 2 * RUN, RUN),
            *[jax.ShapeDtypeStruct(x.shape, x.dtype) for x in kept],
        ),
        [pltpu.VMEM(x.shape, x.dtype) for x in inputs]
        + [
            pltpu.VMEM((2, sources, PAIR), jnp.float32),
            pltpu.VMEM((2, sources, PAIR), jnp.float32),
            pltpu.VMEM((2, 2, 2, sources, PAIR), jnp.bfloat16),
            pltpu.SemaphoreType.DMA((len(inputs + kept),)),
        ],
        inputs + kept,
        4 * 10**9,
        len(inputs + kept),
    )
    odd, coherent, hots, share = lax.optimization_barrier((odd, coherent, hots, share))
    shards = [seen, odd, even, swap(odd, "dir")]
    other_share = swap(share, "dir")
    jones, gather, predicted = call(
        model_kernel,
        (table, gathered, predictions),
        [model],
        (coherent, hots, own, other),
        2 * 10**9,
    )
    packed, mine = call(
        first_kernel,
        (f32(held, RUN), f32(rows + directions, RUN)),
        scratch,
        (mask, coherent, gram, hots, gather, predicted, *shards),
        10**9,
    )
    sums = from_three(packed, packed, packed)
    to_core, to_blk, to_both, jones = call(
        second_kernel,
        (f32(held + rows, RUN), f32(held + rows // 2, RUN), f32(held + rows // 2, RUN), table),
        [
            model,
            scratch[0],
            pltpu.VMEM(gathered.shape, jnp.float32),
            pltpu.VMEM(predictions.shape, jnp.float32),
            scratch[1],
        ],
        (mask, coherent, gram, hots, jones, mine, packed, *sums, *shards),
        2 * 10**9,
    )
    solved = f32(half_directions, 8, station_positions.shape[1])
    return call(
        last_kernel,
        (f32(8, channels, 1, RUN), solved),
        [
            pltpu.VMEM((rows, 2 * RUN), jnp.float32),
            pltpu.VMEM((2, 1, rows, RUN), jnp.float32),
            pltpu.VMEM(solved.shape, jnp.float32),
            pltpu.SemaphoreType.DMA,
        ],
        (
            mask, share, other_share, last_hots, jones,
            to_core, *from_three(to_core, to_blk, to_both), *shards,
        ),
        10**9,
        0,
        (pltpu.VMEM, pltpu.HBM),
    )


def owned_layout(mesh, shapes):
    sizes = mesh.shape
    owners = sizes["chan"] * sizes["blk"]
    visibilities, pairs, jones = shapes
    return (
        owners == BLOCKS
        and sizes["blk"] == 2
        and sizes["dir"] == 2
        and sizes["chan"] == 4
        and pairs[1] * pairs[2] == owners * RUN
        and jones[0] == 16
        and jones[2] == BLOCKS * BLOCK
        and visibilities[1] % sizes["chan"] == 0
        and visibilities[1] & (visibilities[1] - 1) == 0
    )


def solution(mesh):
    in_specs = (
        P("groups", "chan", "blk", None),
        P(None, "blk", None),
        P("blk", "groups"),
        P(),
        P(),
        P(),
        P(),
        P("dir", "groups", None),
    )
    out_specs = (P("groups", None, "blk", "chan"), P("dir", "groups", None))

    def run(*arrays):
        owned = owned_layout(mesh, (arrays[0].shape, arrays[1].shape, arrays[7].shape))
        body = per_device_owned if owned else per_device
        return jax.shard_map(
            body, mesh=mesh, in_specs=in_specs, out_specs=out_specs, check_vma=False
        )(*arrays)

    return run
```
